32 devices in a mesh: dp: 2 (over x), seq: 4 (over z), tensor: 4 (over y, core).
Axes of the slice: x: 2, y: 2, z: 4, core: 2. Of those that a mesh axis runs over, the one named last changes fastest.
Arguments:
- tokens: bfloat16 [4, 2048, 768], P('dp', 'seq'), may hold values from -6 to 6
- cotangent: bfloat16 [4, 2048, 768], P('dp', 'seq'), may hold values from -6 to 6
- segments: int32 [4, 2048], P('dp'), may hold values from 0 to 12, as said below
- parents: int32 [4, 13], P('dp'), may hold values from 0 to 4, as said below
- routes: int32 [4, 2048, 2], P('dp', 'seq'), may hold values from 0 to 7, all different within a row; in each aligned block of 512 rows (0 to 511, 512 to 1023, ..., all dimensions but the last counted through in order) at most 192 rows name the same one
- norm_gains: bfloat16 [2, 768], P(None, ('dp', 'seq')), may hold values from 0.5 to 1.5
- project: bfloat16 [3, 768, 768], P(None, ('dp', 'seq'), 'tensor'), may hold values from -0.21875 to 0.21875
- mixing: bfloat16 [768, 768], P('tensor', ('dp', 'seq')), may hold values from -1.5 to 1.5
- router: bfloat16 [768, 8], P(('dp', 'seq')), may hold values from -0.21875 to 0.21875
- expander: bfloat16 [8, 2, 768, 2048], P(None, None, ('dp', 'seq'), 'tensor'), may hold values from -0.21875 to 0.21875
- reducer: bfloat16 [8, 2048, 768], P(None, 'tensor', ('dp', 'seq')), may hold values from -1 to 1
- spreader: bfloat16 [2, 768, 2048], P(None, ('dp', 'seq'), 'tensor'), may hold values from -0.21875 to 0.21875
- collector: bfloat16 [2048, 768], P('tensor', ('dp', 'seq')), may hold values from -0.25 to 0.25
Outputs:
- output: bfloat16 [4, 2048, 768], P('dp', 'seq')
- input_grad: bfloat16 [4, 2048, 768], P('dp', 'seq')
- gain_grad: float32 [2, 768], P(None, ('dp', 'seq'))
- project_grad: float32 [3, 768, 768], P(None, ('dp', 'seq'), 'tensor')
- mixing_grad: float32 [768, 768], P('tensor', ('dp', 'seq'))
- router_grad: float32 [768, 8], P(('dp', 'seq'))
- expander_grad: float32 [8, 2, 768, 2048], P(None, None, ('dp', 'seq'), 'tensor')
- reducer_grad: float32 [8, 2048, 768], P(None, 'tensor', ('dp', 'seq'))
- spreader_grad: float32 [2, 768, 2048], P(None, ('dp', 'seq'), 'tensor')
- collector_grad: float32 [2048, 768], P('tensor', ('dp', 'seq'))
The draws below stay inside these ranges and needn't reach their ends.
Inputs may be any that keep to these rules, and one draw needn't show every extreme that they name: `segments`: along each tree the segment numbers never fall; segment 0, the trunk, holds the first quarter to half of the tree's 2048 tokens; any other segment may be empty. `parents`: segments 0 to 4 have parent 0 (the trunk is its own parent; 1 to 4 are branches); segments 5 to 12 are leaves whose parent is one of the branches 1 to 4. `routes`: the 2 experts of a token differ; among the 512 tokens that one device holds of one tree, no expert is named more than 192 times, and in some such block one expert is named exactly 192 times.
All inputs are finite; a program needn't handle non-finite values.
Results may differ from the reference program's by a relative error of at most 0.025.
Values may be sent and summed in bfloat16 or wider, within the bound.
No kernel may reach another device: no remote copies, remote signals or barrier semaphores. Data moves between devices by JAX's collectives and lax.ppermute only.
A program may use at most 320 MiB of HBM per device.

```python
import math
import jax
import jax.numpy as jnp
import numpy as np
from jax import lax

D = 768
HEADS = 12
HEAD_DIM = 64
FF = 2048
FF_S = 2048
EXPERTS = 8
TOPK = 2
SEGS = 13
TOK_DEV = 512
TREE_LEN = 2048
TREES = 4
CAP = 192
QB = 512


def draw_segments(key, part):
    first_key = jax.random.fold_in(key, 11)
    second_key = jax.random.fold_in(key, 12)
    trunk_end = jax.random.randint(first_key, (TREES, 1), TREE_LEN // 4, TREE_LEN // 2 + 1)
    offsets = jax.random.randint(second_key, (TREES, SEGS - 2), 0, TREE_LEN - trunk_end)
    cuts = jnp.concatenate([trunk_end, trunk_end + jnp.sort(offsets, axis=1)], 1)
    token_index = jnp.arange(TREE_LEN, dtype=jnp.int32)
    return jnp.sum((token_index[None, :, None] >= cuts[:, None, :]).astype(jnp.int32), 2)


def draw_parents(key, part):
    leaves = jax.random.randint(jax.random.fold_in(key, 21), (TREES, SEGS - 5), 1, 5)
    return jnp.concatenate([jnp.zeros((TREES, 5), jnp.int32), leaves], 1)


def spiked(values, stream_key, source, target, shards_of, factor):
    def block_of(dim):
        return (jnp.arange(values.shape[dim]) // (values.shape[dim] // shards_of)).reshape((-1,) + (1,) * (values.ndim - 1 - dim))

    first = jax.random.permutation(stream_key, shards_of)[block_of(target)]
    second = (block_of(target) + shards_of // 2) % shards_of
    return jnp.where((block_of(source) == first) | (block_of(source) == second), factor * values, values)


def levels(own_key, shape, cuts, least, top_value):
    level, own = 1.0, jax.random.fold_in(own_key, 6)
    for position, parts in cuts:
        draws = jnp.exp(jax.random.uniform(jax.random.fold_in(own, position), (parts,), jnp.float32, least / len(cuts), top_value / len(cuts)))
        level = level * jnp.repeat(draws, shape[position] // parts).reshape([-1 if axis == position else 1 for axis in range(len(shape))])
    return level


def routed_block(key, own, number, rows, count, top, most, lean):
    sequence = jax.random.permutation(key, count)
    crowded, ordinary = load_shares(count, rows * top, most, lean, True), load_shares(count, rows * top, most, lean, False)
    places = jnp.arange(count)

    def named(sizes, turn):
        used = int((sizes > 0).sum())
        fixed = max(1, used // 4)
        moved = fixed + (places - fixed + turn * (used - fixed)) % max(1, count - fixed)
        return jnp.zeros((count,), jnp.int32).at[sequence[jnp.where(places < fixed, places, moved)]].set(jnp.asarray(sizes, jnp.int32))

    sizes = jnp.where(number % 4 == 0, named(crowded, number // 4), named(ordinary, number - number // 4 - 1))
    mixed = jax.random.permutation(jax.random.fold_in(own, 3), count)
    giver, receiver = mixed[0:count // 2 * 2:2], mixed[1:count // 2 * 2:2]
    slack = jnp.minimum(sizes[giver] - 1, most - sizes[receiver]) // 2
    slack = jnp.where((giver == sequence[0]) | (receiver == sequence[0]) | (sizes[receiver] == 0), 0, jnp.maximum(slack, 0))
    moved = jax.random.randint(jax.random.fold_in(own, 4), (count // 2,), 0, 1 << 20) % (slack + 1)
    sizes = sizes.at[giver].add(-moved).at[receiver].add(moved)
    items = jnp.searchsorted(jnp.cumsum(sizes), jnp.arange(rows * top), side="right").astype(jnp.int32)
    grid = items.reshape(top, rows).T
    grid = grid[jax.random.permutation(jax.random.fold_in(own, 1), rows)]
    turn = jax.random.randint(jax.random.fold_in(own, 2), (rows, 1), 0, top)
    return jnp.take_along_axis(grid, (jnp.arange(top)[None, :] + turn) % top, axis=1)


def load_shares(number_of, total, limit, slope, full):
    portions = [(1 << 20) // math.isqrt(standing ** slope) + 1 for standing in range(1, number_of + 1)]
    largest = limit if full else min(limit, max(-(-total // number_of), total * portions[0] // sum(portions)))
    least = 1 if total - largest >= number_of - 1 else 0
    holding, surplus = [largest] + [least] * (number_of - 1), total - largest - least * (number_of - 1)
    while surplus > 0:
        movable = [i for i in range(1, number_of) if holding[i] < largest] or [i for i in range(1, number_of) if holding[i] < limit]
        pool, left = sum([portions[i] for i in movable]), surplus
        for i in movable:
            more = min(limit - holding[i], max(1, left * portions[i] // pool), surplus)
            holding[i] = holding[i] + more
            surplus = surplus - more
    return np.array(holding)


def centred(stream_key, dims, scale, bound, pieces=(), kind=jnp.bfloat16):
    values = jax.random.normal(stream_key, dims, jnp.float32) * scale
    if len(pieces) > 0:
        values = levels(stream_key, dims, pieces, -0.22, 0.18) * values
    return jnp.clip(values, min=-bound, max=bound).astype(kind)


def bell_draw_with(stream_key, shape, scale, bound, cuts, heavy, held_as=jnp.bfloat16):
    array = scale * jax.random.normal(stream_key, shape, jnp.float32)
    if cuts:
        array = array * levels(stream_key, shape, cuts, -0.22, 0.18)
    return jnp.clip(spiked(array, jax.random.fold_in(stream_key, 3), *heavy), -bound, bound).astype(held_as)


def setup_inputs(seed: int = 0) -> dict:
    arg_keys = jax.random.split(jax.random.key(seed), 14)
    tokens = centred(arg_keys[0], (TREES, TREE_LEN, D), 1.0, 6.0, ((0, 2), (1, 4)))
    cotangent = bell_draw_with(arg_keys[1], (TREES, TREE_LEN, D), 1.0, 6.0, ((0, 2), (1, 4)), (1, 2, 4, 2.0))
    segments = draw_segments(jax.random.fold_in(arg_keys[13], 71), 0)
    parents = draw_parents(jax.random.fold_in(arg_keys[13], 71), 0)
    routes_keys = jax.random.split(jax.random.fold_in(arg_keys[4], 1), TREES * TREE_LEN // TOK_DEV)
    routes_turns = jax.random.permutation(jax.random.fold_in(arg_keys[4], 3), TREES * TREE_LEN // TOK_DEV)
    routes = jax.vmap(lambda own, number: routed_block(jax.random.fold_in(arg_keys[4], 2), own, number, TOK_DEV, EXPERTS, TOPK, CAP, 1))(routes_keys, routes_turns).reshape((TREES, TREE_LEN, TOPK))
    norm_gains = jnp.clip(1.0 + 0.1 * jax.random.normal(arg_keys[5], (2, D), jnp.float32), 0.5, 1.5).astype(jnp.bfloat16)
    project = centred(arg_keys[6], (3, D, D), D ** -0.5, 0.21875, ((1, 8), (2, 4)))
    mixing = centred(arg_keys[7], (D, D), (HEAD_DIM // 4) ** -0.5, 1.5, ((0, 4), (1, 8)))
    router = centred(arg_keys[8], (D, EXPERTS), D ** -0.5, 0.21875, ((0, 8),))
    expander = centred(arg_keys[9], (EXPERTS, 2, D, FF), D ** -0.5, 0.21875, ((2, 8), (3, 4)))
    reducer = centred(arg_keys[10], (EXPERTS, FF, D), (FF // 64) ** -0.5, 1.0, ((1, 4), (2, 8)))
    spreader = centred(arg_keys[11], (2, D, FF_S), D ** -0.5, 0.21875, ((1, 8), (2, 4)))
    collector = centred(arg_keys[12], (FF_S, D), (FF_S // 4) ** -0.5, 0.25, ((0, 4), (1, 8)))
    return {"tokens": tokens, "cotangent": cotangent, "segments": segments, "parents": parents, "routes": routes, "norm_gains": norm_gains, "project": project, "mixing": mixing, "router": router, "expander": expander, "reducer": reducer, "spreader": spreader, "collector": collector}


epsilon = 1e-05
theta = 10000.0
highest = lax.Precision.HIGHEST

@jax.custom_vjp
def low(v):
    return lax.optimization_barrier(v.astype(jnp.bfloat16)).astype(jnp.float32)

@jax.custom_vjp
def low_back(v):
    return v

def low_keep(v):
    return (low(v), None)

def low_pass(kept, grad):
    return (grad,)

def back_keep(v):
    return (v, None)

def back_low(kept, grad):
    return (low(grad),)
low.defvjp(low_keep, low_pass)
low_back.defvjp(back_keep, back_low)

def ancestry(parents):
    labels = jnp.arange(parents.shape[0], dtype=jnp.int32)
    grandparent = jnp.take(parents, parents)
    itself = labels[:, None] == labels[None, :]
    return itself | (parents[:, None] == labels[None, :]) | (grandparent[:, None] == labels[None, :])

def positions(segments, table):
    labels = jnp.arange(table.shape[0], dtype=jnp.int32)
    member = (segments[:, None] == labels[None, :]).astype(jnp.int32)
    lengths = lax.optimization_barrier(jnp.sum(member, 0))
    offsets = jnp.cumsum(lengths) - lengths
    ancestral = lax.optimization_barrier(jnp.sum(table.astype(jnp.int32) * lengths[None, :], 1)) - lengths
    moving = ancestral - offsets
    return jnp.arange(segments.shape[0], dtype=jnp.int32) + lax.optimization_barrier(jnp.sum(member * moving[None, :], 1))

def visible(row_segments, row_index, segments, table):
    labels = jnp.arange(table.shape[0], dtype=jnp.int32)
    member_rows = (row_segments[:, None] == labels[None, :]).astype(jnp.float32)
    member_keys = (segments[:, None] == labels[None, :]).astype(jnp.float32)
    reach = jnp.dot(member_rows, table.astype(jnp.float32), precision=highest)
    hits = jnp.dot(reach, member_keys.T, precision=highest)
    key_index = jnp.arange(segments.shape[0], dtype=jnp.int32)
    return (hits > 0.5) & (key_index[None, :] <= row_index[:, None])

def turn(field, place):
    half = field.shape[-1] // 2
    rates = jnp.exp(-math.log(theta) * 2.0 * jnp.arange(half, dtype=jnp.float32) / field.shape[-1])
    angle = place[:, None] * rates[None, :]
    cosine = jnp.cos(angle)[:, None, :]
    sine = jnp.sin(angle)[:, None, :]
    first_half = field[..., :half]
    second_half = field[..., half:]
    return jnp.concatenate([first_half * cosine - second_half * sine, second_half * cosine + first_half * sine], -1)

def slot_of(route_flat):
    labels = jnp.arange(EXPERTS, dtype=jnp.int32)
    member = (route_flat[:, None] == labels[None, :]).astype(jnp.int32)
    ranks = jnp.cumsum(member, 0) - 1
    return route_flat * CAP + lax.optimization_barrier(jnp.sum(ranks * member, 1))

def owner_of(slot_ids):
    count_rows = slot_ids.shape[0] // TOPK
    picked = jnp.arange(slot_ids.shape[0], dtype=jnp.int32) // TOPK
    return jnp.full((EXPERTS * CAP,), count_rows, jnp.int32).at[slot_ids].set(picked)

def take_rows(table_rows, wanted):
    return jnp.take(table_rows, wanted, axis=0)

def tree_forward(inputs, params, segments, parents, routes):
    norm_gains, project, mixing, router, expander, reducer, spreader, collector = params
    tree_length = inputs.shape[0]
    table = ancestry(parents)
    place = positions(segments, table).astype(jnp.float32)
    scale_one = lax.rsqrt(lax.optimization_barrier(jnp.mean(inputs * inputs, -1, keepdims=True)) + epsilon)
    first_in = low(inputs * scale_one * norm_gains[0])
    mapped = jnp.einsum('td,cdh->cth', first_in, project, precision=highest)
    head_shape = (tree_length, HEADS, HEAD_DIM)
    queries = low(turn(low_back(mapped[0]).reshape(head_shape), place))
    keys_all = low(turn(low_back(mapped[1]).reshape(head_shape), place))
    values_all = low(low_back(mapped[2])).reshape(head_shape)
    token_index = jnp.arange(tree_length, dtype=jnp.int32)
    blocks = tree_length // QB
    factor = HEAD_DIM ** (-0.5)

    def attend(entries):
        query_block, seg_block, index_block = entries
        seen = visible(seg_block, index_block, segments, table)
        raw = low_back(jnp.einsum('bhd,lhd->hbl', query_block, keys_all, precision=highest))
        scores = jnp.where(seen[None], raw * factor, -1e+30)
        row_peak = lax.optimization_barrier(jnp.max(scores, -1, keepdims=True))
        expo = jnp.exp(scores - row_peak)
        chances_soft = low(expo / lax.optimization_barrier(jnp.sum(expo, -1, keepdims=True)))
        return jnp.einsum('hbl,lhd->bhd', chances_soft, values_all, precision=highest)
    mixed = lax.map(jax.checkpoint(attend), (queries.reshape(blocks, QB, HEADS, HEAD_DIM), segments.reshape(blocks, QB), token_index.reshape(blocks, QB)))
    heads_out = low(low_back(mixed.reshape(tree_length, D)))
    second = inputs + low_back(jnp.dot(heads_out, mixing, precision=highest))
    scale_two = lax.rsqrt(lax.optimization_barrier(jnp.mean(second * second, -1, keepdims=True)) + epsilon)
    hidden_in = low(second * scale_two * norm_gains[1])
    logits = jnp.dot(hidden_in, router, precision=highest)
    shifted = jnp.exp(logits - lax.optimization_barrier(jnp.max(logits, -1, keepdims=True)))
    chances = shifted / lax.optimization_barrier(jnp.sum(shifted, -1, keepdims=True))
    picks = (routes[:, :, None] == jnp.arange(EXPERTS, dtype=jnp.int32)[None, None, :]).astype(jnp.float32)
    gates = lax.optimization_barrier(jnp.sum(picks * chances[:, None, :], -1))
    groups = tree_length // TOK_DEV
    slot_ids = jax.vmap(slot_of)(routes.reshape(groups, TOK_DEV * TOPK))
    owners = jax.vmap(owner_of)(slot_ids)
    padded = jnp.concatenate([hidden_in.reshape(groups, TOK_DEV, D), jnp.zeros((groups, 1, D), jnp.float32)], 1)
    routed = jax.vmap(take_rows)(padded, owners).reshape(groups, EXPERTS, CAP, D)
    raised = low_back(jnp.einsum('necd,egdf->gnecf', routed, expander, precision=highest))
    activated = low(jax.nn.silu(raised[0]) * raised[1])
    lowered = low_back(jnp.einsum('necf,efd->necd', activated, reducer, precision=highest)).reshape(groups, EXPERTS * CAP, D)
    returned = jax.vmap(take_rows)(lowered, slot_ids).reshape(tree_length, TOPK, D)
    blended = lax.optimization_barrier(jnp.sum(gates[:, :, None] * returned, 1))
    spread = low_back(jnp.einsum('td,gdf->gtf', hidden_in, spreader, precision=highest))
    common = low(jax.nn.silu(spread[0]) * spread[1])
    shared_out = low_back(jnp.dot(common, collector, precision=highest))
    return second + blended + shared_out

def reference(tokens, cotangent, segments, parents, routes, norm_gains, project, mixing, router, expander, reducer, spreader, collector):
    weights = (norm_gains.astype(jnp.float32), project.astype(jnp.float32), mixing.astype(jnp.float32), router.astype(jnp.float32), expander.astype(jnp.float32), reducer.astype(jnp.float32), spreader.astype(jnp.float32), collector.astype(jnp.float32))

    def per_tree(running, entries):
        tree_tokens, tree_cot, tree_segments, tree_parents, tree_routes = entries

        def forward(inputs, gains_in, project_in, mixing_in, router_in, expander_in, reducer_in, spreader_in, collector_in):
            params = (gains_in, project_in, mixing_in, router_in, expander_in, reducer_in, spreader_in, collector_in)
            return tree_forward(inputs, params, tree_segments, tree_parents, tree_routes)
        result, pullback = jax.vjp(forward, tree_tokens.astype(jnp.float32), weights[0], weights[1], weights[2], weights[3], weights[4], weights[5], weights[6], weights[7])
        gradients = pullback(tree_cot.astype(jnp.float32))
        updated = tuple((before + addend for before, addend in zip(running, gradients[1:])))
        return (updated, (result.astype(jnp.bfloat16), gradients[0].astype(jnp.bfloat16)))
    start = tuple((jnp.zeros(weight_arr.shape, jnp.float32) for weight_arr in weights))
    totals, (outputs, input_grads) = lax.scan(per_tree, start, (tokens, cotangent, segments, parents, routes))
    return (outputs, input_grads, totals[0], totals[1], totals[2], totals[3], totals[4], totals[5], totals[6], totals[7])
```

```python
import functools
import math
import types

import jax
import jax.numpy as jnp
from jax import lax
from jax.experimental import pallas as pl
from jax.experimental.pallas import tpu as pltpu
from jax.sharding import PartitionSpec as P

HEAD_DIM = 64
EXPERTS = 8
CAP = 192
QB = 512
DP = "dp"
SEQ = "seq"
TENSOR = "tensor"
GROUP = (DP, SEQ)


epsilon = 1e-05
theta = 10000.0
highest = lax.Precision.HIGHEST


def ancestry(parents):
    labels = jnp.arange(parents.shape[0], dtype=jnp.int32)
    grandparent = jnp.take(parents, parents)
    itself = labels[:, None] == labels[None, :]
    return (
        itself | (parents[:, None] == labels[None, :]) | (grandparent[:, None] == labels[None, :])
    )


def positions(segments, table):
    labels = jnp.arange(table.shape[0], dtype=jnp.int32)
    member = (segments[:, None] == labels[None, :]).astype(jnp.int32)
    lengths = jnp.sum(member, 0)
    offsets = jnp.cumsum(lengths) - lengths
    ancestral = jnp.sum(table.astype(jnp.int32) * lengths[None, :], 1) - lengths
    moving = ancestral - offsets
    return jnp.arange(segments.shape[0], dtype=jnp.int32) + jnp.sum(member * moving[None, :], 1)


def visible(row_segments, row_index, key_segments, key_index, table):
    labels = jnp.arange(table.shape[0], dtype=jnp.int32)
    member_rows = (row_segments[:, None] == labels[None, :]).astype(jnp.bfloat16)
    member_keys = (key_segments[:, None] == labels[None, :]).astype(jnp.bfloat16)
    reach = jnp.dot(member_rows, table.astype(jnp.bfloat16), preferred_element_type=jnp.float32)
    hits = jnp.einsum(
        "bs,ls->bl", reach.astype(jnp.bfloat16), member_keys, preferred_element_type=jnp.float32
    )
    return (hits > 0.5) & (key_index[None, :] <= row_index[:, None])


def turn(field, place, backward):
    half = field.shape[-1] // 2
    rates = jnp.exp(-math.log(theta) * 2.0 * jnp.arange(half, dtype=jnp.float32) / field.shape[-1])
    angle = place[:, None] * rates[None, :]
    cosine = jnp.cos(angle)[:, None, :]
    sine = jnp.sin(angle)[:, None, :]
    first_half = field[..., :half]
    second_half = field[..., half:]
    if backward:
        return jnp.concatenate(
            [first_half * cosine + second_half * sine, second_half * cosine - first_half * sine], -1
        )
    return jnp.concatenate(
        [first_half * cosine - second_half * sine, second_half * cosine + first_half * sine], -1
    )


def slot_of(route_flat):
    labels = jnp.arange(EXPERTS, dtype=jnp.int32)
    member = (route_flat[:, None] == labels[None, :]).astype(jnp.int32)
    ranks = jnp.cumsum(member, 0) - 1
    return route_flat * CAP + jnp.sum(ranks * member, 1)


def owner_of(slot_ids, count_rows, per_row):
    picked = jnp.arange(slot_ids.shape[0], dtype=jnp.int32) // per_row
    return jnp.full((EXPERTS * CAP,), count_rows, jnp.int32).at[slot_ids].set(picked)


def silu_slope(value):
    sigma = jax.nn.sigmoid(value)
    return sigma * (1.0 + value * (1.0 - sigma))


def block_scores(query_block, key_block, seg_block, index_block, key_segments, key_index, table):
    seen = visible(seg_block, index_block, key_segments, key_index, table)
    raw = jnp.einsum("bhd,lhd->hbl", query_block, key_block, preferred_element_type=jnp.float32)
    return jnp.where(seen[None], raw * HEAD_DIM ** (-0.5), -1e30)


def fetch(norm_gains, project, mixing, router, expander, reducer, spreader, collector):
    return (
        lax.all_gather(norm_gains, GROUP, axis=1, tiled=True),
        lax.all_gather(project, GROUP, axis=1, tiled=True),
        lax.all_gather(mixing, GROUP, axis=1, tiled=True),
        lax.all_gather(router, GROUP, axis=0, tiled=True),
        lax.all_gather(expander, GROUP, axis=2, tiled=True),
        lax.all_gather(reducer, GROUP, axis=2, tiled=True),
        lax.all_gather(spreader, GROUP, axis=1, tiled=True),
        lax.all_gather(collector, GROUP, axis=1, tiled=True),
    )


def reduce_end(grads):
    (
        gain_part,
        project_part,
        mixing_part,
        router_part,
        expander_part,
        reducer_part,
        spreader_part,
        collector_part,
    ) = grads
    return (
        lax.psum_scatter(gain_part, GROUP, scatter_dimension=1, tiled=True),
        lax.psum_scatter(project_part, GROUP, scatter_dimension=1, tiled=True),
        lax.psum_scatter(mixing_part, GROUP, scatter_dimension=1, tiled=True),
        lax.psum_scatter(router_part, GROUP, scatter_dimension=0, tiled=True),
        lax.psum_scatter(expander_part, GROUP, scatter_dimension=2, tiled=True),
        lax.psum_scatter(reducer_part, GROUP, scatter_dimension=2, tiled=True),
        lax.psum_scatter(spreader_part, GROUP, scatter_dimension=1, tiled=True),
        lax.psum_scatter(collector_part, GROUP, scatter_dimension=1, tiled=True),
    )


def forward_pass(tree_tokens, tree_segments, tree_parents, tree_routes, weights, offset):
    norm_gains, project, mixing, router, expander, reducer, spreader, collector = weights
    row_count = tree_tokens.shape[0]
    model_width = tree_tokens.shape[1]
    tree_length = tree_segments.shape[0]
    local_heads = project.shape[2] // HEAD_DIM
    table = ancestry(tree_parents)
    place = lax.dynamic_slice_in_dim(positions(tree_segments, table), offset, row_count).astype(
        jnp.float32
    )
    row_segments = lax.dynamic_slice_in_dim(tree_segments, offset, row_count)
    row_index = offset + jnp.arange(row_count, dtype=jnp.int32)
    key_index = jnp.arange(tree_length, dtype=jnp.int32)
    inputs = tree_tokens.astype(jnp.float32)
    scale_one = lax.rsqrt(jnp.mean(inputs * inputs, -1, keepdims=True) + epsilon)
    normed_one = inputs * scale_one
    first_in = (normed_one * norm_gains[0].astype(jnp.float32)).astype(jnp.bfloat16)
    mapped = jnp.einsum("td,cdh->cth", first_in, project, preferred_element_type=jnp.float32)
    head_shape = (row_count, local_heads, HEAD_DIM)
    queries = turn(mapped[0].reshape(head_shape), place, False).astype(jnp.bfloat16)
    keys_own = (
        turn(mapped[1].reshape(head_shape), place, False)
        .astype(jnp.bfloat16)
        .reshape(row_count, -1)
    )
    values_own = mapped[2].astype(jnp.bfloat16)
    keys_flat, values_flat = (
        lax.all_gather(keys_own, SEQ, axis=0, tiled=True),
        lax.all_gather(values_own, SEQ, axis=0, tiled=True),
    )
    keys_all = keys_flat.reshape(tree_length, local_heads, HEAD_DIM)
    values_all = values_flat.reshape(tree_length, local_heads, HEAD_DIM)
    blocks = row_count // QB
    query_blocks = queries.reshape(blocks, QB, local_heads, HEAD_DIM)
    seg_blocks = row_segments.reshape(blocks, QB)
    index_blocks = row_index.reshape(blocks, QB)

    def attend(entries):
        query_block, seg_block, index_block = entries
        scores = block_scores(
            query_block, keys_all, seg_block, index_block, tree_segments, key_index, table
        )
        row_peak = jnp.max(scores, -1, keepdims=True)
        expo = jnp.exp(scores - row_peak)
        row_total = jnp.sum(expo, -1, keepdims=True)
        chances_soft = expo / row_total
        mixed_block = jnp.einsum(
            "hbl,lhd->bhd",
            chances_soft.astype(jnp.bfloat16),
            values_all,
            preferred_element_type=jnp.float32,
        )
        return (mixed_block, (row_peak + jnp.log(row_total))[..., 0])

    mixed, log_totals = lax.map(attend, (query_blocks, seg_blocks, index_blocks))
    heads_out = mixed.reshape(row_count, -1).astype(jnp.bfloat16)
    attended = lax.psum(
        jnp.dot(heads_out, mixing, preferred_element_type=jnp.float32).astype(jnp.bfloat16),
        TENSOR,
    ).astype(jnp.float32)
    second = inputs + attended
    scale_two = lax.rsqrt(jnp.mean(second * second, -1, keepdims=True) + epsilon)
    normed_two = second * scale_two
    hidden_in = (normed_two * norm_gains[1].astype(jnp.float32)).astype(jnp.bfloat16)
    logits = jnp.dot(hidden_in, router, preferred_element_type=jnp.float32)
    shifted = jnp.exp(logits - jnp.max(logits, -1, keepdims=True))
    chances = shifted / jnp.sum(shifted, -1, keepdims=True)
    picks = (tree_routes[:, :, None] == jnp.arange(EXPERTS, dtype=jnp.int32)[None, None, :]).astype(
        jnp.float32
    )
    gates = jnp.sum(picks * chances[:, None, :], -1)
    per_row = tree_routes.shape[1]
    slot_ids = slot_of(tree_routes.reshape(-1))
    owners = owner_of(slot_ids, row_count, per_row)
    padded = jnp.concatenate([hidden_in, jnp.zeros((1, model_width), jnp.bfloat16)], 0)
    routed = jnp.take(padded, owners, axis=0).reshape(EXPERTS, CAP, model_width)
    raised = jnp.einsum("ecd,egdf->gecf", routed, expander, preferred_element_type=jnp.float32)
    activated = (jax.nn.silu(raised[0]) * raised[1]).astype(jnp.bfloat16)
    lowered = jnp.einsum(
        "ecf,efd->ecd", activated, reducer, preferred_element_type=jnp.float32
    ).reshape(EXPERTS * CAP, model_width)
    returned = jnp.take(lowered, slot_ids, axis=0).reshape(row_count, per_row, model_width)
    blended = jnp.sum(gates[:, :, None] * returned, 1)
    spread = jnp.einsum("td,gdf->gtf", hidden_in, spreader, preferred_element_type=jnp.float32)
    common = (jax.nn.silu(spread[0]) * spread[1]).astype(jnp.bfloat16)
    shared_out = jnp.dot(common, collector, preferred_element_type=jnp.float32)
    branches = lax.psum((blended + shared_out).astype(jnp.bfloat16), TENSOR).astype(jnp.float32)
    output_tree = (second + branches).astype(jnp.bfloat16)
    kept = types.SimpleNamespace(
        table=table,
        place=place,
        offset=offset,
        row_segments=row_segments,
        seg_blocks=seg_blocks,
        index_blocks=index_blocks,
        scale_one=scale_one,
        normed_one=normed_one,
        first_in=first_in,
        queries=queries,
        query_blocks=query_blocks,
        keys_all=keys_all,
        values_all=values_all,
        log_totals=log_totals,
        heads_out=heads_out,
        scale_two=scale_two,
        normed_two=normed_two,
        hidden_in=hidden_in,
        chances=chances,
        picks=picks,
        gates=gates,
        slot_ids=slot_ids,
        routed=routed,
        raised=raised,
        activated=activated,
        returned=returned,
        spread=spread,
        common=common,
    )
    return (kept, output_tree)


def backward_pass(tree_cot, tree_segments, kept, weights):
    norm_gains, project, mixing, router, expander, reducer, spreader, collector = weights
    upstream = tree_cot.astype(jnp.float32)
    row_count = upstream.shape[0]
    model_width = upstream.shape[1]
    shared_grad = upstream.astype(jnp.bfloat16)
    common_grad = jnp.einsum(
        "td,fd->tf", shared_grad, collector, preferred_element_type=jnp.float32
    )
    collector_part = jnp.einsum(
        "tf,td->fd", kept.common, shared_grad, preferred_element_type=jnp.float32
    )
    spread = kept.spread
    spread_grad = jnp.stack(
        [common_grad * spread[1] * silu_slope(spread[0]), common_grad * jax.nn.silu(spread[0])]
    ).astype(jnp.bfloat16)
    spreader_part = jnp.einsum(
        "td,gtf->gdf", kept.hidden_in, spread_grad, preferred_element_type=jnp.float32
    )
    hidden_grad = jnp.einsum(
        "gtf,gdf->td", spread_grad, spreader, preferred_element_type=jnp.float32
    )
    gates = kept.gates
    slot_ids = kept.slot_ids
    per_row = gates.shape[1]
    pair_grad = (
        (gates[:, :, None] * upstream[:, None, :])
        .astype(jnp.bfloat16)
        .reshape(row_count * per_row, model_width)
    )
    lowered_grad = (
        jnp.zeros((EXPERTS * CAP, model_width), jnp.bfloat16)
        .at[slot_ids]
        .set(pair_grad)
        .reshape(EXPERTS, CAP, model_width)
    )
    activated_grad = jnp.einsum(
        "ecd,efd->ecf", lowered_grad, reducer, preferred_element_type=jnp.float32
    )
    reducer_part = jnp.einsum(
        "ecf,ecd->efd", kept.activated, lowered_grad, preferred_element_type=jnp.float32
    )
    raised = kept.raised
    raised_grad = jnp.stack(
        [
            activated_grad * raised[1] * silu_slope(raised[0]),
            activated_grad * jax.nn.silu(raised[0]),
        ]
    ).astype(jnp.bfloat16)
    expander_part = jnp.einsum(
        "ecd,gecf->egdf", kept.routed, raised_grad, preferred_element_type=jnp.float32
    )
    routed_grad = jnp.einsum(
        "gecf,egdf->ecd", raised_grad, expander, preferred_element_type=jnp.float32
    ).reshape(EXPERTS * CAP, model_width)
    hidden_grad = hidden_grad + jnp.sum(
        jnp.take(routed_grad, slot_ids, axis=0).reshape(row_count, per_row, model_width), 1
    )
    gate_grad = jnp.sum(upstream[:, None, :] * kept.returned, -1)
    hidden_grad, gate_grad = (
        lax.psum(hidden_grad.astype(jnp.bfloat16), TENSOR).astype(jnp.float32),
        lax.psum(gate_grad.astype(jnp.bfloat16), TENSOR).astype(jnp.float32),
    )
    chances = kept.chances
    chance_grad = jnp.sum(kept.picks * gate_grad[:, :, None], 1)
    logit_grad = chances * (chance_grad - jnp.sum(chances * chance_grad, -1, keepdims=True))
    hidden_grad = hidden_grad + jnp.dot(logit_grad, router.astype(jnp.float32).T, precision=highest)
    router_part = jnp.dot(kept.hidden_in.astype(jnp.float32).T, logit_grad, precision=highest)
    normed_two = kept.normed_two
    gain_two = jnp.sum(hidden_grad * normed_two, 0)
    scaled_two = hidden_grad * norm_gains[1].astype(jnp.float32)
    second_grad = upstream + kept.scale_two * (
        scaled_two - normed_two * jnp.mean(scaled_two * normed_two, -1, keepdims=True)
    )
    branch_grad = second_grad.astype(jnp.bfloat16)
    mixing_part = jnp.einsum(
        "th,td->hd", kept.heads_out, branch_grad, preferred_element_type=jnp.float32
    )
    heads_grad = jnp.einsum(
        "td,hd->th", branch_grad, mixing, preferred_element_type=jnp.float32
    ).astype(jnp.bfloat16)
    keys_all = kept.keys_all
    values_all = kept.values_all
    table = kept.table
    query_blocks = kept.query_blocks
    tree_length = keys_all.shape[0]
    local_heads = keys_all.shape[1]
    key_index = jnp.arange(tree_length, dtype=jnp.int32)
    grad_blocks = heads_grad.reshape(query_blocks.shape)
    factor = HEAD_DIM ** (-0.5)

    def attend_back(carry, entries):
        keys_grad, values_grad = carry
        query_block, grad_block, log_block, seg_block, index_block = entries
        scores = block_scores(
            query_block, keys_all, seg_block, index_block, tree_segments, key_index, table
        )
        chances_soft = jnp.exp(scores - log_block[..., None])
        prob_grad = jnp.einsum(
            "bhd,lhd->hbl", grad_block, values_all, preferred_element_type=jnp.float32
        )
        centre = jnp.sum(chances_soft * prob_grad, -1, keepdims=True)
        score_grad = (chances_soft * (prob_grad - centre) * factor).astype(jnp.bfloat16)
        query_grad_block = jnp.einsum(
            "hbl,lhd->bhd", score_grad, keys_all, preferred_element_type=jnp.float32
        )
        keys_grad = keys_grad + jnp.einsum(
            "hbl,bhd->lhd", score_grad, query_block, preferred_element_type=jnp.float32
        )
        values_grad = values_grad + jnp.einsum(
            "hbl,bhd->lhd",
            chances_soft.astype(jnp.bfloat16),
            grad_block,
            preferred_element_type=jnp.float32,
        )
        return ((keys_grad, values_grad), query_grad_block)

    zero_kv = jnp.zeros((tree_length, local_heads, HEAD_DIM), jnp.float32)
    (keys_grad, values_grad), query_grad = lax.scan(
        attend_back,
        (zero_kv, zero_kv),
        (query_blocks, grad_blocks, kept.log_totals, kept.seg_blocks, kept.index_blocks),
    )
    keys_own_grad, values_own_grad = (
        lax.psum_scatter(
            keys_grad.reshape(tree_length, -1).astype(jnp.bfloat16),
            SEQ,
            scatter_dimension=0,
            tiled=True,
        ).astype(jnp.float32),
        lax.psum_scatter(
            values_grad.reshape(tree_length, -1).astype(jnp.bfloat16),
            SEQ,
            scatter_dimension=0,
            tiled=True,
        ).astype(jnp.float32),
    )
    place = kept.place
    query_back = turn(query_grad.reshape(row_count, local_heads, HEAD_DIM), place, True).reshape(
        row_count, -1
    )
    key_back = turn(keys_own_grad.reshape(row_count, local_heads, HEAD_DIM), place, True).reshape(
        row_count, -1
    )
    mapped_grad = jnp.stack([query_back, key_back, values_own_grad]).astype(jnp.bfloat16)
    project_part = jnp.einsum(
        "td,cth->cdh", kept.first_in, mapped_grad, preferred_element_type=jnp.float32
    )
    first_grad = lax.psum(
        jnp.einsum("cth,cdh->td", mapped_grad, project, preferred_element_type=jnp.float32).astype(
            jnp.bfloat16
        ),
        TENSOR,
    ).astype(jnp.float32)
    normed_one = kept.normed_one
    gain_one = jnp.sum(first_grad * normed_one, 0)
    scaled_one = first_grad * norm_gains[0].astype(jnp.float32)
    input_tree = (
        second_grad
        + kept.scale_one
        * (scaled_one - normed_one * jnp.mean(scaled_one * normed_one, -1, keepdims=True))
    ).astype(jnp.bfloat16)
    gain_part = jnp.stack([gain_one, gain_two])
    return (
        input_tree,
        (
            gain_part,
            project_part,
            mixing_part,
            router_part,
            expander_part,
            reducer_part,
            spreader_part,
            collector_part,
        ),
    )


def local(
    tokens,
    cotangent,
    segments,
    parents,
    routes,
    norm_gains,
    project,
    mixing,
    router,
    expander,
    reducer,
    spreader,
    collector,
):
    tree_count = tokens.shape[0]
    offset = lax.axis_index(SEQ) * tokens.shape[1]
    outputs = []
    input_grads = []
    running = None
    for tree_index in range(tree_count):
        forward_weights = fetch(
            norm_gains, project, mixing, router, expander, reducer, spreader, collector
        )
        kept, output_tree = forward_pass(
            tokens[tree_index],
            segments[tree_index],
            parents[tree_index],
            routes[tree_index],
            forward_weights,
            offset,
        )
        backward_weights = fetch(
            norm_gains, project, mixing, router, expander, reducer, spreader, collector
        )
        input_tree, tree_grads = backward_pass(
            cotangent[tree_index], segments[tree_index], kept, backward_weights
        )
        outputs.append(output_tree)
        input_grads.append(input_tree)
        if running is None:
            running = tree_grads
        else:
            running = tuple((before + addend for before, addend in zip(running, tree_grads)))
    running = reduce_end(running)
    return (
        jnp.stack(outputs),
        jnp.stack(input_grads),
        running[0],
        running[1],
        running[2],
        running[3],
        running[4],
        running[5],
        running[6],
        running[7],
    )


VMEM_BYTES = 56 << 20


def contract(left, right, left_dim, right_dim):
    return lax.dot_general(
        left, right, (((left_dim,), (right_dim,)), ((), ())), preferred_element_type=jnp.float32
    )


def scores_of(keys, queries, seen):
    return jnp.where(seen, contract(keys, queries, 0, 0), -1e30)


def seen_block(number, place_ref, key_bits_ref, query_bits, length):
    start = pl.multiple_of((place_ref[0] - number) * length, length)
    seen = (key_bits_ref[pl.ds(start, length), :] & query_bits) != 0
    if number == 0:
        keys = lax.broadcasted_iota(jnp.int32, seen.shape, 0)
        rows = lax.broadcasted_iota(jnp.int32, seen.shape, 1)
        seen = seen & (keys <= rows)
    return seen


def attend_kernel(count, heads, place_ref, query_ref, key_bits_ref, query_bits_ref, *refs):
    pair_refs = refs[:count]
    out_ref, log_ref, peak_ref, total_ref, mixed_ref = refs[count:]
    length = query_ref.shape[1]
    width = heads * HEAD_DIM

    def block(number):
        pair_ref = pair_refs[number]
        seen = seen_block(number, place_ref, key_bits_ref, query_bits_ref[...], length)
        for head in range(heads):
            span = slice(head * HEAD_DIM, (head + 1) * HEAD_DIM)
            value_span = slice(width + head * HEAD_DIM, width + (head + 1) * HEAD_DIM)
            row = slice(head, head + 1)
            scores = scores_of(pair_ref[span, :], query_ref[span, :], seen)
            peak = jnp.max(scores, 0, keepdims=True)
            if number:
                before = peak_ref[row, :]
                peak = jnp.maximum(before, peak)
                shrink = jnp.exp(before - peak)
            expo = jnp.exp(scores - peak)
            total = jnp.sum(expo, 0, keepdims=True)
            mixed = jnp.dot(
                pair_ref[value_span, :],
                expo.astype(jnp.bfloat16),
                preferred_element_type=jnp.float32,
            )
            if number:
                total = total + shrink * total_ref[row, :]
                mixed = mixed + shrink * mixed_ref[span, :]
            peak_ref[row, :] = peak
            total_ref[row, :] = total
            mixed_ref[span, :] = mixed

    block(0)
    for number in range(1, count):
        pl.when(place_ref[0] >= number)(lambda number=number: block(number))
    for head in range(heads):
        span = slice(head * HEAD_DIM, (head + 1) * HEAD_DIM)
        row = slice(head, head + 1)
        out_ref[span, :] = (mixed_ref[span, :] / total_ref[row, :]).astype(out_ref.dtype)
        log_ref[row, :] = peak_ref[row, :] + jnp.log(total_ref[row, :])


def attend_back_kernel(
    count,
    heads,
    place_ref,
    query_ref,
    out_ref,
    grad_ref,
    log_ref,
    key_bits_ref,
    query_bits_ref,
    *refs
):
    pair_refs = refs[:count]
    query_grad_ref = refs[count]
    pair_grad_refs = refs[count + 1 : 2 * count + 1]
    length = query_ref.shape[1]
    width = heads * HEAD_DIM

    def block(number):
        pair_ref = pair_refs[number]
        pair_grad_ref = pair_grad_refs[number]
        seen = seen_block(number, place_ref, key_bits_ref, query_bits_ref[...], length)
        for head in range(heads):
            span = slice(head * HEAD_DIM, (head + 1) * HEAD_DIM)
            value_span = slice(width + head * HEAD_DIM, width + (head + 1) * HEAD_DIM)
            row = slice(head, head + 1)
            queries = query_ref[span, :]
            grads = grad_ref[span, :]
            keys = pair_ref[span, :]
            centre = jnp.sum(
                grads.astype(jnp.float32) * out_ref[span, :].astype(jnp.float32), 0, keepdims=True
            )
            chances = jnp.exp(scores_of(keys, queries, seen) - log_ref[row, :])
            prob_grad = contract(pair_ref[value_span, :], grads, 0, 0)
            score_grad = (chances * (prob_grad - centre)).astype(jnp.bfloat16)
            value_grad = contract(grads, chances.astype(jnp.bfloat16), 1, 1)
            key_grad = contract(queries, score_grad, 1, 1)
            query_grad = jnp.dot(keys, score_grad, preferred_element_type=jnp.float32)
            pair_grad_ref[span, :] = key_grad.astype(pair_grad_ref.dtype)
            pair_grad_ref[value_span, :] = value_grad.astype(pair_grad_ref.dtype)
            if number:
                query_grad = query_grad + query_grad_ref[span, :]
            query_grad_ref[span, :] = query_grad

    block(0)
    for number in range(1, count):
        pl.when(place_ref[0] >= number)(lambda number=number: block(number))


def whole():
    return pl.BlockSpec(memory_space=pltpu.VMEM)


def scalars():
    return pl.BlockSpec(memory_space=pltpu.SMEM)


def attend(place, queries, key_bits, query_bits, pairs):
    width, length = queries.shape
    heads = width // HEAD_DIM
    count = len(pairs)
    return pl.pallas_call(
        functools.partial(attend_kernel, count, heads),
        out_shape=(
            jax.ShapeDtypeStruct((width, length), jnp.bfloat16),
            jax.ShapeDtypeStruct((heads, length), jnp.float32),
        ),
        in_specs=[scalars()] + [whole()] * (3 + count),
        out_specs=(whole(), whole()),
        scratch_shapes=[
            pltpu.VMEM((heads, length), jnp.float32),
            pltpu.VMEM((heads, length), jnp.float32),
            pltpu.VMEM((width, length), jnp.float32),
        ],
        compiler_params=pltpu.CompilerParams(vmem_limit_bytes=VMEM_BYTES),
        cost_estimate=pl.CostEstimate(
            flops=16 * count * width * length * length,
            transcendentals=count * heads * length * length,
            bytes_accessed=4 * (count + 2) * width * length,
        ),
        name="attend",
    )(place, queries, key_bits, query_bits, *pairs)


def attend_back(place, queries, outs, grads, logs, key_bits, query_bits, pairs):
    width, length = queries.shape
    heads = width // HEAD_DIM
    count = len(pairs)
    results = pl.pallas_call(
        functools.partial(attend_back_kernel, count, heads),
        out_shape=(jax.ShapeDtypeStruct((width, length), jnp.float32),)
        + (jax.ShapeDtypeStruct((2 * width, length), jnp.float32),)
        + (jax.ShapeDtypeStruct((2 * width, length), jnp.bfloat16),) * (count - 1),
        in_specs=[scalars()] + [whole()] * (6 + count),
        out_specs=(whole(),) * (count + 1),
        compiler_params=pltpu.CompilerParams(vmem_limit_bytes=VMEM_BYTES),
        cost_estimate=pl.CostEstimate(
            flops=40 * count * width * length * length,
            transcendentals=count * heads * length * length,
            bytes_accessed=8 * (count + 2) * width * length,
        ),
        name="attend_back",
    )(place, queries, outs, grads, logs, key_bits, query_bits, *pairs)
    return (results[0], results[1:])


def gated_kernel(rows_ref, grads_ref, weights_ref, lowered_ref, routed_ref, parts_ref):
    rows = rows_ref[...]
    grads = grads_ref[...]
    gate_weights = weights_ref[0, 0]
    up_weights = weights_ref[0, 1]
    down_weights = weights_ref[0, 2]
    first = jnp.dot(rows, gate_weights, preferred_element_type=jnp.float32)
    second = jnp.dot(rows, up_weights, preferred_element_type=jnp.float32)
    sigma = 1.0 / (1.0 + jnp.exp(-first))
    swish = first * sigma
    activated = (swish * second).astype(jnp.bfloat16)
    activated_grad = jnp.dot(grads, down_weights, preferred_element_type=jnp.float32)
    first_grad = (activated_grad * second * (sigma + swish * (1.0 - sigma))).astype(jnp.bfloat16)
    second_grad = (activated_grad * swish).astype(jnp.bfloat16)
    lowered = contract(activated, down_weights, 1, 1)
    routed = contract(first_grad, gate_weights, 1, 1) + contract(second_grad, up_weights, 1, 1)

    @pl.when(pl.program_id(0) == 0)
    def _():
        lowered_ref[...] = lowered
        routed_ref[...] = routed

    @pl.when(pl.program_id(0) > 0)
    def _():
        lowered_ref[...] += lowered
        routed_ref[...] += routed

    parts_ref[0, 0] = contract(rows, first_grad, 0, 0).astype(jnp.bfloat16)
    parts_ref[0, 1] = contract(rows, second_grad, 0, 0).astype(jnp.bfloat16)
    parts_ref[0, 2] = contract(grads, activated, 0, 0).astype(jnp.bfloat16)


def gated(rows, grads, weights, tile):
    count, model_width = rows.shape
    chunks, _, _, hidden = weights.shape
    tiles = hidden // tile
    fixed = pl.BlockSpec((count, model_width), lambda step: (0, 0))
    moving = pl.BlockSpec(
        (1, 3, model_width, tile), lambda step: (step // tiles, 0, 0, step % tiles)
    )
    return pl.pallas_call(
        gated_kernel,
        grid=(chunks * tiles,),
        out_shape=(
            jax.ShapeDtypeStruct((count, model_width), jnp.float32),
            jax.ShapeDtypeStruct((count, model_width), jnp.float32),
            jax.ShapeDtypeStruct(weights.shape, jnp.bfloat16),
        ),
        in_specs=[fixed, fixed, moving],
        out_specs=(fixed, fixed, moving),
        compiler_params=pltpu.CompilerParams(vmem_limit_bytes=VMEM_BYTES),
        cost_estimate=pl.CostEstimate(
            flops=18 * count * model_width * chunks * hidden,
            transcendentals=count * chunks * hidden,
            bytes_accessed=12 * count * model_width + 12 * chunks * model_width * hidden,
        ),
        name="gated",
    )(rows, grads, weights)


def swap(piece, axes, size, step):
    return lax.ppermute(piece, axes, [(i, i ^ step) for i in range(size)])


def pick(stacked, index):
    return lax.dynamic_index_in_dim(stacked, index, 0, keepdims=False)


def share(piece, axes, size):
    return [piece] + [swap(piece, axes, size, step) for step in range(1, size)]


def natural(pieces, index):
    stacked = jnp.stack(pieces)
    return [pick(stacked, index ^ other) for other in range(len(pieces))]


def turned(field, cosine, sine, backward):
    half = HEAD_DIM // 2
    shape = field.shape
    split = field.reshape(shape[0], -1, 2, half, shape[-1])
    first_half = split[:, :, 0]
    second_half = split[:, :, 1]
    if backward:
        parts = [
            first_half * cosine + second_half * sine,
            second_half * cosine - first_half * sine,
        ]
    else:
        parts = [
            first_half * cosine - second_half * sine,
            second_half * cosine + first_half * sine,
        ]
    return jnp.stack(parts, 2).reshape(shape)


def tree_tables(segments, parents):
    count = parents.shape[1]
    labels = jnp.arange(count, dtype=jnp.int32)
    is_parent = parents[:, :, None] == labels[None, None, :]
    grand = jnp.sum(jnp.where(is_parent, parents[:, None, :], 0), 2)
    itself = labels[None, :, None] == labels[None, None, :]
    table = itself | is_parent | (grand[:, :, None] == labels[None, None, :])
    member = segments[:, None, :] == labels[None, :, None]
    lengths = jnp.sum(member.astype(jnp.int32), 2)
    ahead = jnp.sum(jnp.where(labels[:, None] > labels[None, :], lengths[:, None, :], 0), 2)
    moving = jnp.sum(jnp.where(table, lengths[:, None, :], 0), 2) - lengths - ahead
    place = jnp.arange(segments.shape[1], dtype=jnp.int32) + jnp.sum(
        jnp.where(member, moving[:, :, None], 0), 1
    )
    bits = jnp.sum(jnp.where(table, jnp.left_shift(1, labels)[None, None, :], 0), 2)
    paths = jnp.sum(jnp.where(member, bits[:, :, None], 0), 1)
    return (place, paths, jnp.left_shift(1, segments))


def local_fast(
    tokens,
    cotangent,
    segments,
    parents,
    routes,
    norm_gains,
    project,
    mixing,
    router,
    expander,
    reducer,
    spreader,
    collector,
):
    bf16, f32 = jnp.bfloat16, jnp.float32
    group_size = lax.axis_size(GROUP)
    seq_size = lax.axis_size(SEQ)
    shards = lax.axis_size(TENSOR)
    member_index = lax.axis_index(GROUP)
    seq_index = lax.axis_index(SEQ)
    shard = lax.axis_index(TENSOR)
    trees, rows, model_width = tokens.shape
    part_width = project.shape[2]
    owned = project.shape[1]
    hidden = spreader.shape[2]
    slots = CAP // shards
    quarter = rows // shards
    place_arg = seq_index.astype(jnp.int32).reshape(1)

    extra = EXPERTS + 2
    pad = -extra % 128
    small = jnp.concatenate(
        [
            project[0],
            project[1],
            project[2],
            mixing.T,
            router,
            norm_gains.T,
            jnp.zeros((owned, pad), bf16),
        ],
        1,
    )
    small = lax.all_gather(small, GROUP, axis=0, tiled=True)
    project_all = small[:, : 3 * part_width]
    mixing_own = small[:, 3 * part_width : 4 * part_width].T
    router_all = small[:, 4 * part_width : 4 * part_width + EXPERTS]
    gains = small[:, 4 * part_width + EXPERTS : 4 * part_width + extra].T.astype(f32)
    mixing_all = jnp.concatenate(share(mixing_own, TENSOR, shards), 0)
    shared_weights = lax.all_gather(
        jnp.concatenate([spreader, collector.T[None]], 0), GROUP, axis=1, tiled=True
    )

    bundles = jnp.concatenate([expander, reducer.transpose(0, 2, 1)[:, None]], 1)
    arrived = [
        pick(bundles, member_index ^ step)
        if step == 0
        else swap(pick(bundles, member_index ^ step), GROUP, group_size, step)
        for step in range(group_size)
    ]
    own_expert = jnp.concatenate(natural(arrived, member_index), 1)
    expert_weights = lax.all_gather(own_expert, TENSOR, axis=0, tiled=False)

    labels = member_index ^ jnp.arange(EXPERTS, dtype=jnp.int32)
    named = jnp.any(routes[:, None, :, :] == labels[None, :, None, None], 3)
    earlier = (
        jnp.arange(rows, dtype=jnp.int32)[:, None] < jnp.arange(rows, dtype=jnp.int32)[None, :]
    )
    ranks = jnp.einsum(
        "bes,st->bet", named.astype(bf16), earlier.astype(bf16), preferred_element_type=f32
    ).astype(jnp.int32)
    slot_index = shard * slots + jnp.arange(slots, dtype=jnp.int32)
    chosen = (
        (named[:, :, None, :] & (ranks[:, :, None, :] == slot_index[None, None, :, None]))
        .astype(bf16)
        .reshape(trees, EXPERTS * slots, rows)
    )

    def send_rows(field):
        picked = jnp.einsum("bst,btd->bsd", chosen, field, preferred_element_type=f32).astype(bf16)
        picked = picked.reshape(trees, EXPERTS, slots, field.shape[-1])
        pieces = [picked[:, step] for step in range(EXPERTS)]
        pieces = pieces[:1] + [
            swap(pieces[step], GROUP, group_size, step) for step in range(1, EXPERTS)
        ]
        return jnp.stack(pieces).reshape(EXPERTS * trees * slots, field.shape[-1])

    def return_rows(field):
        pieces = field.reshape(EXPERTS, trees, slots, field.shape[-1])
        pieces = [pieces[0]] + [
            swap(pieces[step], GROUP, group_size, step) for step in range(1, EXPERTS)
        ]
        stacked = jnp.stack(pieces, 1).reshape(trees, EXPERTS * slots, field.shape[-1])
        return jnp.einsum("bst,bsd->btd", chosen, stacked, preferred_element_type=f32)

    upstream_rows = send_rows(cotangent)

    place, paths, key_bits = tree_tables(segments, parents)
    offset = seq_index * rows
    own_place = lax.dynamic_slice_in_dim(place, offset, rows, 1).astype(f32)
    own_paths = lax.dynamic_slice_in_dim(paths, offset, rows, 1)
    half = HEAD_DIM // 2
    rates = jnp.exp(-math.log(theta) * 2.0 * jnp.arange(half, dtype=f32) / HEAD_DIM)
    angle = rates[None, :, None] * own_place[:, None, :]
    cosine = jnp.cos(angle)[:, None]
    sine = jnp.sin(angle)[:, None]
    inputs = tokens.astype(f32)
    scale_one = lax.rsqrt(jnp.mean(inputs * inputs, -1, keepdims=True) + epsilon)
    first_in = (inputs * scale_one * gains[0]).astype(bf16)
    mapped = jnp.einsum("dh,btd->bht", project_all, first_in, preferred_element_type=f32)
    queries = (
        turned(mapped[:, :part_width], cosine, sine, False) * HEAD_DIM ** (-0.5)
    ).astype(bf16)
    pairs_own = jnp.concatenate(
        [
            turned(mapped[:, part_width : 2 * part_width], cosine, sine, False).astype(bf16),
            mapped[:, 2 * part_width :].astype(bf16),
        ],
        1,
    )
    pairs = []
    outs = []
    logs = []
    for tree in range(trees):
        pairs.append(
            [pairs_own[tree]]
            + [
                lax.ppermute(
                    pairs_own[tree], SEQ, [(i, i + step) for i in range(seq_size - step)]
                )
                for step in range(1, seq_size)
            ]
        )
        out, log = attend(
            place_arg, queries[tree], key_bits[tree][:, None], own_paths[tree][None], pairs[tree]
        )
        outs.append(out)
        logs.append(log)
    heads = [jnp.concatenate(share(out, TENSOR, shards), 0) for out in outs]
    second = inputs + jnp.stack(
        [
            jnp.einsum("ht,hd->td", head, mixing_all, preferred_element_type=f32)
            for head in heads
        ]
    )

    scale_two = lax.rsqrt(jnp.mean(second * second, -1, keepdims=True) + epsilon)
    hidden_in = (second * scale_two * gains[1]).astype(bf16)
    expert_rows = send_rows(hidden_in)
    flat = (trees * rows, model_width)
    shared_out, shared_back, shared_parts = gated(
        hidden_in.reshape(flat), cotangent.reshape(flat), shared_weights[None], 256
    )
    row_chances = jax.nn.softmax(jnp.dot(expert_rows, router_all, preferred_element_type=f32), -1)
    own_label = jnp.arange(EXPERTS, dtype=jnp.int32) == member_index
    row_gates = jnp.sum(jnp.where(own_label[None], row_chances, 0.0), -1, keepdims=True)
    row_grads = (row_gates * upstream_rows.astype(f32)).astype(bf16)
    lowered, routed_back, expert_parts = gated(expert_rows, row_grads, expert_weights, 256)
    gate_grads = jnp.sum(upstream_rows.astype(f32) * lowered, -1, keepdims=True)
    lanes = jnp.arange(128, dtype=jnp.int32)[None]
    back_rows = jnp.concatenate(
        [
            routed_back.astype(bf16),
            jnp.where(lanes == member_index, gate_grads, 0.0).astype(bf16),
        ],
        1,
    )
    returned_back = return_rows(back_rows)
    returned_out = return_rows((row_gates * lowered).astype(bf16))

    expert_own = lax.psum_scatter(expert_parts, TENSOR, scatter_dimension=0, tiled=False)
    blocks = expert_own.reshape(3, group_size, owned, hidden)
    blocks = [
        lax.dynamic_index_in_dim(blocks, member_index ^ step, 1, keepdims=False)
        for step in range(group_size)
    ]
    blocks = blocks[:1] + [
        swap(blocks[step], GROUP, group_size, step) for step in range(1, group_size)
    ]
    expert_grads = jnp.stack(natural(blocks, member_index)).astype(f32)
    expander_grad = expert_grads[:, :2]
    reducer_grad = expert_grads[:, 2].transpose(0, 2, 1)
    shared_grads = lax.psum_scatter(
        shared_parts[0], GROUP, scatter_dimension=1, tiled=True
    ).astype(f32)
    spreader_grad = shared_grads[:2]
    collector_grad = shared_grads[2].T

    branches = lax.psum(
        (returned_out + shared_out.reshape(trees, rows, model_width)).astype(bf16), TENSOR
    ).astype(f32)
    output = (second + branches).astype(bf16)

    def own_rows(field):
        return lax.dynamic_slice_in_dim(field, shard * quarter, quarter, 1)

    def add_shards(field):
        pieces = field.astype(bf16)
        mine = own_rows(pieces).astype(f32)
        for step in range(1, shards):
            sent = lax.dynamic_slice_in_dim(pieces, (shard ^ step) * quarter, quarter, 1)
            mine = mine + swap(sent, TENSOR, shards, step).astype(f32)
        return mine

    def spread_shards(field):
        return jnp.concatenate(natural(share(field, TENSOR, shards), shard), 1)

    summed = add_shards(
        returned_back
        + jnp.pad(shared_back.reshape(trees, rows, model_width), ((0, 0), (0, 0), (0, 128)))
    )
    chance_grad = summed[..., model_width : model_width + EXPERTS]
    quarter_second = own_rows(second)
    quarter_scale = own_rows(scale_two)
    quarter_normed = quarter_second * quarter_scale
    quarter_hidden = own_rows(hidden_in)
    logits = jnp.dot(quarter_hidden, router_all, preferred_element_type=f32)
    chances = jax.nn.softmax(logits, -1)
    logit_grad = chances * (chance_grad - jnp.sum(chances * chance_grad, -1, keepdims=True))
    hidden_grad = summed[..., :model_width] + jnp.einsum(
        "bte,de->btd", logit_grad, router_all.astype(f32), precision=highest
    )
    router_part = jnp.einsum(
        "btd,bte->ed", quarter_hidden.astype(f32), logit_grad, precision=highest
    )
    gain_two = jnp.sum(hidden_grad * quarter_normed, (0, 1))
    scaled_two = hidden_grad * gains[1]
    second_grad = own_rows(cotangent).astype(f32) + quarter_scale * (
        scaled_two - quarter_normed * jnp.mean(scaled_two * quarter_normed, -1, keepdims=True)
    )
    branch_grad = spread_shards(second_grad.astype(bf16))

    heads_grad = jnp.einsum(
        "hd,btd->bht", mixing_own, branch_grad, preferred_element_type=f32
    ).astype(bf16)
    outs_all = jnp.stack(outs)
    mixing_part = jnp.einsum("btd,bht->dh", branch_grad, outs_all, preferred_element_type=f32)
    mapped_grads = []
    for tree in range(trees):
        query_grad, pair_grads = attend_back(
            place_arg,
            queries[tree],
            outs[tree],
            heads_grad[tree],
            logs[tree],
            key_bits[tree][:, None],
            own_paths[tree][None],
            pairs[tree],
        )
        pair_grad = pair_grads[0]
        for step in range(1, seq_size):
            pair_grad = pair_grad + lax.ppermute(
                pair_grads[step], SEQ, [(i + step, i) for i in range(seq_size - step)]
            ).astype(f32)
        mapped_grads.append(
            jnp.concatenate(
                [
                    turned(
                        query_grad[None] * HEAD_DIM ** (-0.5),
                        cosine[tree : tree + 1],
                        sine[tree : tree + 1],
                        True,
                    ),
                    turned(
                        pair_grad[None, :part_width],
                        cosine[tree : tree + 1],
                        sine[tree : tree + 1],
                        True,
                    ),
                    pair_grad[None, part_width:],
                ],
                1,
            ).astype(bf16)
        )
    mapped_grad = jnp.concatenate(mapped_grads, 0)
    project_part = jnp.einsum("btd,bht->dh", first_in, mapped_grad, preferred_element_type=f32)
    first_grad = add_shards(
        jnp.einsum("bht,dh->btd", mapped_grad, project_all, preferred_element_type=f32)
    )
    quarter_scale_one = own_rows(scale_one)
    quarter_normed_one = own_rows(inputs) * quarter_scale_one
    gain_one = jnp.sum(first_grad * quarter_normed_one, (0, 1))
    scaled_one = first_grad * gains[0]
    input_grad = spread_shards(
        (
            second_grad
            + quarter_scale_one
            * (
                scaled_one
                - quarter_normed_one * jnp.mean(scaled_one * quarter_normed_one, -1, keepdims=True)
            )
        ).astype(bf16)
    )

    small_parts = jnp.concatenate([project_part, mixing_part], 1).astype(bf16)
    small_grads = lax.psum_scatter(
        small_parts, GROUP, scatter_dimension=0, tiled=True
    ).astype(f32)
    project_grad = (
        small_grads[:, : 3 * part_width].reshape(owned, 3, part_width).transpose(1, 0, 2)
    )
    mixing_grad = small_grads[:, 3 * part_width :].T
    tiny = lax.psum(
        jnp.concatenate([router_part, gain_one[None], gain_two[None]], 0),
        (DP, SEQ, TENSOR),
    )
    tiny = lax.dynamic_slice_in_dim(tiny, member_index * owned, owned, 1)
    router_grad = tiny[:EXPERTS].T
    gain_grad = tiny[EXPERTS:]
    return (
        output,
        input_grad,
        gain_grad,
        project_grad,
        mixing_grad,
        router_grad,
        expander_grad,
        reducer_grad,
        spreader_grad,
        collector_grad,
    )


def solution(mesh):
    in_specs = (
        P(DP, SEQ, None),
        P(DP, SEQ, None),
        P(DP, None),
        P(DP, None),
        P(DP, SEQ, None),
        P(None, GROUP),
        P(None, GROUP, TENSOR),
        P(TENSOR, GROUP),
        P(GROUP, None),
        P(None, None, GROUP, TENSOR),
        P(None, TENSOR, GROUP),
        P(None, GROUP, TENSOR),
        P(TENSOR, GROUP),
    )
    out_specs = (
        P(DP, SEQ, None),
        P(DP, SEQ, None),
        P(None, GROUP),
        P(None, GROUP, TENSOR),
        P(TENSOR, GROUP),
        P(GROUP, None),
        P(None, None, GROUP, TENSOR),
        P(None, TENSOR, GROUP),
        P(None, GROUP, TENSOR),
        P(TENSOR, GROUP),
    )
    sizes = mesh.shape
    group_size = sizes[DP] * sizes[SEQ]
    shards = sizes[TENSOR]
    fits = group_size == EXPERTS and shards & (shards - 1) == 0 and CAP % shards == 0
    body = local_fast if fits else local
    return jax.shard_map(body, mesh=mesh, in_specs=in_specs, out_specs=out_specs, check_vma=False)
```

```python
import functools
import math
import types

import jax
import jax.numpy as jnp
from jax import lax
from jax.experimental import pallas as pl
from jax.experimental.pallas import tpu as pltpu
from jax.sharding import PartitionSpec as P

HEAD_DIM = 64
EXPERTS = 8
CAP = 192
QB = 512
DP = "dp"
SEQ = "seq"
TENSOR = "tensor"
GROUP = (DP, SEQ)


epsilon = 1e-05
theta = 10000.0
highest = lax.Precision.HIGHEST


def ancestry(parents):
    labels = jnp.arange(parents.shape[0], dtype=jnp.int32)
    grandparent = jnp.take(parents, parents)
    itself = labels[:, None] == labels[None, :]
    return (
        itself | (parents[:, None] == labels[None, :]) | (grandparent[:, None] == labels[None, :])
    )


def positions(segments, table):
    labels = jnp.arange(table.shape[0], dtype=jnp.int32)
    member = (segments[:, None] == labels[None, :]).astype(jnp.int32)
    lengths = jnp.sum(member, 0)
    offsets = jnp.cumsum(lengths) - lengths
    ancestral = jnp.sum(table.astype(jnp.int32) * lengths[None, :], 1) - lengths
    moving = ancestral - offsets
    return jnp.arange(segments.shape[0], dtype=jnp.int32) + jnp.sum(member * moving[None, :], 1)


def visible(row_segments, row_index, key_segments, key_index, table):
    labels = jnp.arange(table.shape[0], dtype=jnp.int32)
    member_rows = (row_segments[:, None] == labels[None, :]).astype(jnp.bfloat16)
    member_keys = (key_segments[:, None] == labels[None, :]).astype(jnp.bfloat16)
    reach = jnp.dot(member_rows, table.astype(jnp.bfloat16), preferred_element_type=jnp.float32)
    hits = jnp.einsum(
        "bs,ls->bl", reach.astype(jnp.bfloat16), member_keys, preferred_element_type=jnp.float32
    )
    return (hits > 0.5) & (key_index[None, :] <= row_index[:, None])


def turn(field, place, backward):
    half = field.shape[-1] // 2
    rates = jnp.exp(-math.log(theta) * 2.0 * jnp.arange(half, dtype=jnp.float32) / field.shape[-1])
    angle = place[:, None] * rates[None, :]
    cosine = jnp.cos(angle)[:, None, :]
    sine = jnp.sin(angle)[:, None, :]
    first_half = field[..., :half]
    second_half = field[..., half:]
    if backward:
        return jnp.concatenate(
            [first_half * cosine + second_half * sine, second_half * cosine - first_half * sine], -1
        )
    return jnp.concatenate(
        [first_half * cosine - second_half * sine, second_half * cosine + first_half * sine], -1
    )


def slot_of(route_flat):
    labels = jnp.arange(EXPERTS, dtype=jnp.int32)
    member = (route_flat[:, None] == labels[None, :]).astype(jnp.int32)
    ranks = jnp.cumsum(member, 0) - 1
    return route_flat * CAP + jnp.sum(ranks * member, 1)


def owner_of(slot_ids, count_rows, per_row):
    picked = jnp.arange(slot_ids.shape[0], dtype=jnp.int32) // per_row
    return jnp.full((EXPERTS * CAP,), count_rows, jnp.int32).at[slot_ids].set(picked)


def silu_slope(value):
    sigma = jax.nn.sigmoid(value)
    return sigma * (1.0 + value * (1.0 - sigma))


def block_scores(query_block, key_block, seg_block, index_block, key_segments, key_index, table):
    seen = visible(seg_block, index_block, key_segments, key_index, table)
    raw = jnp.einsum("bhd,lhd->hbl", query_block, key_block, preferred_element_type=jnp.float32)
    return jnp.where(seen[None], raw * HEAD_DIM ** (-0.5), -1e30)


def fetch(norm_gains, project, mixing, router, expander, reducer, spreader, collector):
    return (
        lax.all_gather(norm_gains, GROUP, axis=1, tiled=True),
        lax.all_gather(project, GROUP, axis=1, tiled=True),
        lax.all_gather(mixing, GROUP, axis=1, tiled=True),
        lax.all_gather(router, GROUP, axis=0, tiled=True),
        lax.all_gather(expander, GROUP, axis=2, tiled=True),
        lax.all_gather(reducer, GROUP, axis=2, tiled=True),
        lax.all_gather(spreader, GROUP, axis=1, tiled=True),
        lax.all_gather(collector, GROUP, axis=1, tiled=True),
    )


def reduce_end(grads):
    (
        gain_part,
        project_part,
        mixing_part,
        router_part,
        expander_part,
        reducer_part,
        spreader_part,
        collector_part,
    ) = grads
    return (
        lax.psum_scatter(gain_part, GROUP, scatter_dimension=1, tiled=True),
        lax.psum_scatter(project_part, GROUP, scatter_dimension=1, tiled=True),
        lax.psum_scatter(mixing_part, GROUP, scatter_dimension=1, tiled=True),
        lax.psum_scatter(router_part, GROUP, scatter_dimension=0, tiled=True),
        lax.psum_scatter(expander_part, GROUP, scatter_dimension=2, tiled=True),
        lax.psum_scatter(reducer_part, GROUP, scatter_dimension=2, tiled=True),
        lax.psum_scatter(spreader_part, GROUP, scatter_dimension=1, tiled=True),
        lax.psum_scatter(collector_part, GROUP, scatter_dimension=1, tiled=True),
    )


def forward_pass(tree_tokens, tree_segments, tree_parents, tree_routes, weights, offset):
    norm_gains, project, mixing, router, expander, reducer, spreader, collector = weights
    row_count = tree_tokens.shape[0]
    model_width = tree_tokens.shape[1]
    tree_length = tree_segments.shape[0]
    local_heads = project.shape[2] // HEAD_DIM
    table = ancestry(tree_parents)
    place = lax.dynamic_slice_in_dim(positions(tree_segments, table), offset, row_count).astype(
        jnp.float32
    )
    row_segments = lax.dynamic_slice_in_dim(tree_segments, offset, row_count)
    row_index = offset + jnp.arange(row_count, dtype=jnp.int32)
    key_index = jnp.arange(tree_length, dtype=jnp.int32)
    inputs = tree_tokens.astype(jnp.float32)
    scale_one = lax.rsqrt(jnp.mean(inputs * inputs, -1, keepdims=True) + epsilon)
    normed_one = inputs * scale_one
    first_in = (normed_one * norm_gains[0].astype(jnp.float32)).astype(jnp.bfloat16)
    mapped = jnp.einsum("td,cdh->cth", first_in, project, preferred_element_type=jnp.float32)
    head_shape = (row_count, local_heads, HEAD_DIM)
    queries = turn(mapped[0].reshape(head_shape), place, False).astype(jnp.bfloat16)
    keys_own = (
        turn(mapped[1].reshape(head_shape), place, False)
        .astype(jnp.bfloat16)
        .reshape(row_count, -1)
    )
    values_own = mapped[2].astype(jnp.bfloat16)
    keys_flat, values_flat = (
        lax.all_gather(keys_own, SEQ, axis=0, tiled=True),
        lax.all_gather(values_own, SEQ, axis=0, tiled=True),
    )
    keys_all = keys_flat.reshape(tree_length, local_heads, HEAD_DIM)
    values_all = values_flat.reshape(tree_length, local_heads, HEAD_DIM)
    blocks = row_count // QB
    query_blocks = queries.reshape(blocks, QB, local_heads, HEAD_DIM)
    seg_blocks = row_segments.reshape(blocks, QB)
    index_blocks = row_index.reshape(blocks, QB)

    def attend(entries):
        query_block, seg_block, index_block = entries
        scores = block_scores(
            query_block, keys_all, seg_block, index_block, tree_segments, key_index, table
        )
        row_peak = jnp.max(scores, -1, keepdims=True)
        expo = jnp.exp(scores - row_peak)
        row_total = jnp.sum(expo, -1, keepdims=True)
        chances_soft = expo / row_total
        mixed_block = jnp.einsum(
            "hbl,lhd->bhd",
            chances_soft.astype(jnp.bfloat16),
            values_all,
            preferred_element_type=jnp.float32,
        )
        return (mixed_block, (row_peak + jnp.log(row_total))[..., 0])

    mixed, log_totals = lax.map(attend, (query_blocks, seg_blocks, index_blocks))
    heads_out = mixed.reshape(row_count, -1).astype(jnp.bfloat16)
    attended = lax.psum(
        jnp.dot(heads_out, mixing, preferred_element_type=jnp.float32).astype(jnp.bfloat16),
        TENSOR,
    ).astype(jnp.float32)
    second = inputs + attended
    scale_two = lax.rsqrt(jnp.mean(second * second, -1, keepdims=True) + epsilon)
    normed_two = second * scale_two
    hidden_in = (normed_two * norm_gains[1].astype(jnp.float32)).astype(jnp.bfloat16)
    logits = jnp.dot(hidden_in, router, preferred_element_type=jnp.float32)
    shifted = jnp.exp(logits - jnp.max(logits, -1, keepdims=True))
    chances = shifted / jnp.sum(shifted, -1, keepdims=True)
    picks = (tree_routes[:, :, None] == jnp.arange(EXPERTS, dtype=jnp.int32)[None, None, :]).astype(
        jnp.float32
    )
    gates = jnp.sum(picks * chances[:, None, :], -1)
    per_row = tree_routes.shape[1]
    slot_ids = slot_of(tree_routes.reshape(-1))
    owners = owner_of(slot_ids, row_count, per_row)
    padded = jnp.concatenate([hidden_in, jnp.zeros((1, model_width), jnp.bfloat16)], 0)
    routed = jnp.take(padded, owners, axis=0).reshape(EXPERTS, CAP, model_width)
    raised = jnp.einsum("ecd,egdf->gecf", routed, expander, preferred_element_type=jnp.float32)
    activated = (jax.nn.silu(raised[0]) * raised[1]).astype(jnp.bfloat16)
    lowered = jnp.einsum(
        "ecf,efd->ecd", activated, reducer, preferred_element_type=jnp.float32
    ).reshape(EXPERTS * CAP, model_width)
    returned = jnp.take(lowered, slot_ids, axis=0).reshape(row_count, per_row, model_width)
    blended = jnp.sum(gates[:, :, None] * returned, 1)
    spread = jnp.einsum("td,gdf->gtf", hidden_in, spreader, preferred_element_type=jnp.float32)
    common = (jax.nn.silu(spread[0]) * spread[1]).astype(jnp.bfloat16)
    shared_out = jnp.dot(common, collector, preferred_element_type=jnp.float32)
    branches = lax.psum((blended + shared_out).astype(jnp.bfloat16), TENSOR).astype(jnp.float32)
    output_tree = (second + branches).astype(jnp.bfloat16)
    kept = types.SimpleNamespace(
        table=table,
        place=place,
        offset=offset,
        row_segments=row_segments,
        seg_blocks=seg_blocks,
        index_blocks=index_blocks,
        scale_one=scale_one,
        normed_one=normed_one,
        first_in=first_in,
        queries=queries,
        query_blocks=query_blocks,
        keys_all=keys_all,
        values_all=values_all,
        log_totals=log_totals,
        heads_out=heads_out,
        scale_two=scale_two,
        normed_two=normed_two,
        hidden_in=hidden_in,
        chances=chances,
        picks=picks,
        gates=gates,
        slot_ids=slot_ids,
        routed=routed,
        raised=raised,
        activated=activated,
        returned=returned,
        spread=spread,
        common=common,
    )
    return (kept, output_tree)


def backward_pass(tree_cot, tree_segments, kept, weights):
    norm_gains, project, mixing, router, expander, reducer, spreader, collector = weights
    upstream = tree_cot.astype(jnp.float32)
    row_count = upstream.shape[0]
    model_width = upstream.shape[1]
    shared_grad = upstream.astype(jnp.bfloat16)
    common_grad = jnp.einsum(
        "td,fd->tf", shared_grad, collector, preferred_element_type=jnp.float32
    )
    collector_part = jnp.einsum(
        "tf,td->fd", kept.common, shared_grad, preferred_element_type=jnp.float32
    )
    spread = kept.spread
    spread_grad = jnp.stack(
        [common_grad * spread[1] * silu_slope(spread[0]), common_grad * jax.nn.silu(spread[0])]
    ).astype(jnp.bfloat16)
    spreader_part = jnp.einsum(
        "td,gtf->gdf", kept.hidden_in, spread_grad, preferred_element_type=jnp.float32
    )
    hidden_grad = jnp.einsum(
        "gtf,gdf->td", spread_grad, spreader, preferred_element_type=jnp.float32
    )
    gates = kept.gates
    slot_ids = kept.slot_ids
    per_row = gates.shape[1]
    pair_grad = (
        (gates[:, :, None] * upstream[:, None, :])
        .astype(jnp.bfloat16)
        .reshape(row_count * per_row, model_width)
    )
    lowered_grad = (
        jnp.zeros((EXPERTS * CAP, model_width), jnp.bfloat16)
        .at[slot_ids]
        .set(pair_grad)
        .reshape(EXPERTS, CAP, model_width)
    )
    activated_grad = jnp.einsum(
        "ecd,efd->ecf", lowered_grad, reducer, preferred_element_type=jnp.float32
    )
    reducer_part = jnp.einsum(
        "ecf,ecd->efd", kept.activated, lowered_grad, preferred_element_type=jnp.float32
    )
    raised = kept.raised
    raised_grad = jnp.stack(
        [
            activated_grad * raised[1] * silu_slope(raised[0]),
            activated_grad * jax.nn.silu(raised[0]),
        ]
    ).astype(jnp.bfloat16)
    expander_part = jnp.einsum(
        "ecd,gecf->egdf", kept.routed, raised_grad, preferred_element_type=jnp.float32
    )
    routed_grad = jnp.einsum(
        "gecf,egdf->ecd", raised_grad, expander, preferred_element_type=jnp.float32
    ).reshape(EXPERTS * CAP, model_width)
    hidden_grad = hidden_grad + jnp.sum(
        jnp.take(routed_grad, slot_ids, axis=0).reshape(row_count, per_row, model_width), 1
    )
    gate_grad = jnp.sum(upstream[:, None, :] * kept.returned, -1)
    hidden_grad, gate_grad = (
        lax.psum(hidden_grad.astype(jnp.bfloat16), TENSOR).astype(jnp.float32),
        lax.psum(gate_grad.astype(jnp.bfloat16), TENSOR).astype(jnp.float32),
    )
    chances = kept.chances
    chance_grad = jnp.sum(kept.picks * gate_grad[:, :, None], 1)
    logit_grad = chances * (chance_grad - jnp.sum(chances * chance_grad, -1, keepdims=True))
    hidden_grad = hidden_grad + jnp.dot(logit_grad, router.astype(jnp.float32).T, precision=highest)
    router_part = jnp.dot(kept.hidden_in.astype(jnp.float32).T, logit_grad, precision=highest)
    normed_two = kept.normed_two
    gain_two = jnp.sum(hidden_grad * normed_two, 0)
    scaled_two = hidden_grad * norm_gains[1].astype(jnp.float32)
    second_grad = upstream + kept.scale_two * (
        scaled_two - normed_two * jnp.mean(scaled_two * normed_two, -1, keepdims=True)
    )
    branch_grad = second_grad.astype(jnp.bfloat16)
    mixing_part = jnp.einsum(
        "th,td->hd", kept.heads_out, branch_grad, preferred_element_type=jnp.float32
    )
    heads_grad = jnp.einsum(
        "td,hd->th", branch_grad, mixing, preferred_element_type=jnp.float32
    ).astype(jnp.bfloat16)
    keys_all = kept.keys_all
    values_all = kept.values_all
    table = kept.table
    query_blocks = kept.query_blocks
    tree_length = keys_all.shape[0]
    local_heads = keys_all.shape[1]
    key_index = jnp.arange(tree_length, dtype=jnp.int32)
    grad_blocks = heads_grad.reshape(query_blocks.shape)
    factor = HEAD_DIM ** (-0.5)

    def attend_back(carry, entries):
        keys_grad, values_grad = carry
        query_block, grad_block, log_block, seg_block, index_block = entries
        scores = block_scores(
            query_block, keys_all, seg_block, index_block, tree_segments, key_index, table
        )
        chances_soft = jnp.exp(scores - log_block[..., None])
        prob_grad = jnp.einsum(
            "bhd,lhd->hbl", grad_block, values_all, preferred_element_type=jnp.float32
        )
        centre = jnp.sum(chances_soft * prob_grad, -1, keepdims=True)
        score_grad = (chances_soft * (prob_grad - centre) * factor).astype(jnp.bfloat16)
        query_grad_block = jnp.einsum(
            "hbl,lhd->bhd", score_grad, keys_all, preferred_element_type=jnp.float32
        )
        keys_grad = keys_grad + jnp.einsum(
            "hbl,bhd->lhd", score_grad, query_block, preferred_element_type=jnp.float32
        )
        values_grad = values_grad + jnp.einsum(
            "hbl,bhd->lhd",
            chances_soft.astype(jnp.bfloat16),
            grad_block,
            preferred_element_type=jnp.float32,
        )
        return ((keys_grad, values_grad), query_grad_block)

    zero_kv = jnp.zeros((tree_length, local_heads, HEAD_DIM), jnp.float32)
    (keys_grad, values_grad), query_grad = lax.scan(
        attend_back,
        (zero_kv, zero_kv),
        (query_blocks, grad_blocks, kept.log_totals, kept.seg_blocks, kept.index_blocks),
    )
    keys_own_grad, values_own_grad = (
        lax.psum_scatter(
            keys_grad.reshape(tree_length, -1).astype(jnp.bfloat16),
            SEQ,
            scatter_dimension=0,
            tiled=True,
        ).astype(jnp.float32),
        lax.psum_scatter(
            values_grad.reshape(tree_length, -1).astype(jnp.bfloat16),
            SEQ,
            scatter_dimension=0,
            tiled=True,
        ).astype(jnp.float32),
    )
    place = kept.place
    query_back = turn(query_grad.reshape(row_count, local_heads, HEAD_DIM), place, True).reshape(
        row_count, -1
    )
    key_back = turn(keys_own_grad.reshape(row_count, local_heads, HEAD_DIM), place, True).reshape(
        row_count, -1
    )
    mapped_grad = jnp.stack([query_back, key_back, values_own_grad]).astype(jnp.bfloat16)
    project_part = jnp.einsum(
        "td,cth->cdh", kept.first_in, mapped_grad, preferred_element_type=jnp.float32
    )
    first_grad = lax.psum(
        jnp.einsum("cth,cdh->td", mapped_grad, project, preferred_element_type=jnp.float32).astype(
            jnp.bfloat16
        ),
        TENSOR,
    ).astype(jnp.float32)
    normed_one = kept.normed_one
    gain_one = jnp.sum(first_grad * normed_one, 0)
    scaled_one = first_grad * norm_gains[0].astype(jnp.float32)
    input_tree = (
        second_grad
        + kept.scale_one
        * (scaled_one - normed_one * jnp.mean(scaled_one * normed_one, -1, keepdims=True))
    ).astype(jnp.bfloat16)
    gain_part = jnp.stack([gain_one, gain_two])
    return (
        input_tree,
        (
            gain_part,
            project_part,
            mixing_part,
            router_part,
            expander_part,
            reducer_part,
            spreader_part,
            collector_part,
        ),
    )


def local(
    tokens,
    cotangent,
    segments,
    parents,
    routes,
    norm_gains,
    project,
    mixing,
    router,
    expander,
    reducer,
    spreader,
    collector,
):
    tree_count = tokens.shape[0]
    offset = lax.axis_index(SEQ) * tokens.shape[1]
    outputs = []
    input_grads = []
    running = None
    for tree_index in range(tree_count):
        forward_weights = fetch(
            norm_gains, project, mixing, router, expander, reducer, spreader, collector
        )
        kept, output_tree = forward_pass(
            tokens[tree_index],
            segments[tree_index],
            parents[tree_index],
            routes[tree_index],
            forward_weights,
            offset,
        )
        backward_weights = fetch(
            norm_gains, project, mixing, router, expander, reducer, spreader, collector
        )
        input_tree, tree_grads = backward_pass(
            cotangent[tree_index], segments[tree_index], kept, backward_weights
        )
        outputs.append(output_tree)
        input_grads.append(input_tree)
        if running is None:
            running = tree_grads
        else:
            running = tuple((before + addend for before, addend in zip(running, tree_grads)))
    running = reduce_end(running)
    return (
        jnp.stack(outputs),
        jnp.stack(input_grads),
        running[0],
        running[1],
        running[2],
        running[3],
        running[4],
        running[5],
        running[6],
        running[7],
    )


VMEM_BYTES = 56 << 20


def contract(left, right, left_dim, right_dim):
    return lax.dot_general(
        left, right, (((left_dim,), (right_dim,)), ((), ())), preferred_element_type=jnp.float32
    )


def spans(head, width):
    if isinstance(head, int):
        start = head * HEAD_DIM
    else:
        start = pl.multiple_of(head * HEAD_DIM, HEAD_DIM)
    return (pl.ds(start, HEAD_DIM), pl.ds(width + start, HEAD_DIM), pl.ds(head, 1))


def scores_of(keys, queries, seen):
    return jnp.where(seen, contract(keys, queries, 0, 0), -1e30)


def seen_block(number, place_ref, key_bits_ref, query_bits, length):
    start = pl.multiple_of((place_ref[0] - number) * length, length)
    seen = (key_bits_ref[pl.ds(start, length), :] & query_bits) != 0
    if number == 0:
        keys = lax.broadcasted_iota(jnp.int32, seen.shape, 0)
        rows = lax.broadcasted_iota(jnp.int32, seen.shape, 1)
        seen = seen & (keys <= rows)
    return seen


def attend_kernel(number, final, heads, place_ref, query_ref, key_bits_ref, query_bits_ref, *refs):
    pair_ref = refs[0]
    if number:
        old_peak_ref, old_total_ref, old_mixed_ref = refs[1:4]
    peak_ref, total_ref, mixed_ref = refs[-3:]
    length = query_ref.shape[1]
    width = heads * HEAD_DIM

    def block():
        seen = seen_block(number, place_ref, key_bits_ref, query_bits_ref[...], length)

        def one(head, _):
            span, value_span, row = spans(head, width)
            scores = scores_of(pair_ref[span, :], query_ref[span, :], seen)
            peak = jnp.max(scores, 0, keepdims=True)
            if number:
                before = old_peak_ref[row, :]
                peak = jnp.maximum(before, peak)
                shrink = jnp.exp(before - peak)
            expo = jnp.exp(scores - peak)
            total = jnp.sum(expo, 0, keepdims=True)
            mixed = jnp.dot(
                pair_ref[value_span, :],
                expo.astype(jnp.bfloat16),
                preferred_element_type=jnp.float32,
            )
            if number:
                total = total + shrink * old_total_ref[row, :]
                mixed = mixed + shrink * old_mixed_ref[span, :]
            peak_ref[row, :] = peak
            total_ref[row, :] = total
            mixed_ref[span, :] = mixed
            return 0

        lax.fori_loop(0, heads, one, 0)

    def keep():
        peak_ref[...] = old_peak_ref[...]
        total_ref[...] = old_total_ref[...]
        mixed_ref[...] = old_mixed_ref[...]

    if number:
        pl.when(place_ref[0] >= number)(block)
        pl.when(place_ref[0] < number)(keep)
    else:
        block()
    if final:
        out_ref, log_ref = refs[4:6]
        for head in range(heads):
            span, _, row = spans(head, width)
            out_ref[span, :] = (mixed_ref[span, :] / total_ref[row, :]).astype(out_ref.dtype)
            log_ref[row, :] = peak_ref[row, :] + jnp.log(total_ref[row, :])


def attend_back_kernel(
    number,
    heads,
    place_ref,
    query_ref,
    out_ref,
    grad_ref,
    log_ref,
    key_bits_ref,
    query_bits_ref,
    pair_ref,
    *refs
):
    query_grad_ref, pair_grad_ref = refs[-2:]
    length = query_ref.shape[1]
    width = heads * HEAD_DIM

    def block():
        seen = seen_block(number, place_ref, key_bits_ref, query_bits_ref[...], length)

        def one(head, _):
            span, value_span, row = spans(head, width)
            queries = query_ref[span, :]
            grads = grad_ref[span, :]
            keys = pair_ref[span, :]
            centre = jnp.sum(
                grads.astype(jnp.float32) * out_ref[span, :].astype(jnp.float32), 0, keepdims=True
            )
            chances = jnp.exp(scores_of(keys, queries, seen) - log_ref[row, :])
            prob_grad = contract(pair_ref[value_span, :], grads, 0, 0)
            score_grad = (chances * (prob_grad - centre)).astype(jnp.bfloat16)
            value_grad = contract(grads, chances.astype(jnp.bfloat16), 1, 1)
            key_grad = contract(queries, score_grad, 1, 1)
            query_grad = jnp.dot(keys, score_grad, preferred_element_type=jnp.float32)
            pair_grad_ref[span, :] = key_grad.astype(pair_grad_ref.dtype)
            pair_grad_ref[value_span, :] = value_grad.astype(pair_grad_ref.dtype)
            if len(refs) > 2:
                query_grad = query_grad + refs[0][span, :]
            query_grad_ref[span, :] = query_grad
            return 0

        lax.fori_loop(0, heads, one, 0)

    def empty():
        pair_grad_ref[...] = jnp.zeros_like(pair_grad_ref)
        if len(refs) > 2:
            query_grad_ref[...] = refs[0][...]
        else:
            query_grad_ref[...] = jnp.zeros_like(query_grad_ref)

    if number:
        pl.when(place_ref[0] >= number)(block)
        pl.when(place_ref[0] < number)(empty)
    else:
        block()


def per_tree(array):
    return pl.BlockSpec((None,) + array.shape[1:], lambda tree: (tree, 0, 0))


def attend_call(kernel, name, place, operands, results, flops):
    trees, width, length = operands[0].shape
    return pl.pallas_call(
        kernel,
        grid=(trees,),
        out_shape=results,
        in_specs=[pl.BlockSpec(memory_space=pltpu.SMEM)] + [per_tree(value) for value in operands],
        out_specs=tuple(per_tree(value) for value in results),
        compiler_params=pltpu.CompilerParams(vmem_limit_bytes=VMEM_BYTES),
        cost_estimate=pl.CostEstimate(
            flops=flops * trees * width * length * length,
            transcendentals=trees * width * length * length // HEAD_DIM,
            bytes_accessed=16 * trees * width * length,
        ),
        name=name,
    )(place, *operands)


def attend(number, final, place, queries, key_bits, query_bits, pair, state):
    trees, width, length = queries.shape
    heads = width // HEAD_DIM
    row = jax.ShapeDtypeStruct((trees, heads, length), jnp.float32)
    field = jax.ShapeDtypeStruct(queries.shape, jnp.float32)
    results = (row, row, field)
    if final:
        results = (jax.ShapeDtypeStruct(queries.shape, jnp.bfloat16), row) + results
    return attend_call(
        functools.partial(attend_kernel, number, final, heads),
        "attend",
        place,
        (queries, key_bits, query_bits, pair) + tuple(state),
        results,
        16,
    )


def attend_back(number, kind, place, operands):
    trees, width, length = operands[0].shape
    heads = width // HEAD_DIM
    return attend_call(
        functools.partial(attend_back_kernel, number, heads),
        "attend_back",
        place,
        operands,
        (
            jax.ShapeDtypeStruct((trees, width, length), jnp.float32),
            jax.ShapeDtypeStruct((trees, 2 * width, length), kind),
        ),
        40,
    )


def gated_kernel(rows_ref, grads_ref, weights_ref, lowered_ref, routed_ref, parts_ref):
    rows = rows_ref[...]
    grads = grads_ref[...]
    gate_weights = weights_ref[0, 0]
    up_weights = weights_ref[0, 1]
    down_weights = weights_ref[0, 2]
    first = jnp.dot(rows, gate_weights, preferred_element_type=jnp.float32)
    second = jnp.dot(rows, up_weights, preferred_element_type=jnp.float32)
    sigma = 1.0 / (1.0 + jnp.exp(-first))
    swish = first * sigma
    activated = (swish * second).astype(jnp.bfloat16)
    activated_grad = jnp.dot(grads, down_weights, preferred_element_type=jnp.float32)
    first_grad = (activated_grad * second * (sigma + swish * (1.0 - sigma))).astype(jnp.bfloat16)
    second_grad = (activated_grad * swish).astype(jnp.bfloat16)
    lowered = contract(activated, down_weights, 1, 1)
    routed = contract(first_grad, gate_weights, 1, 1) + contract(second_grad, up_weights, 1, 1)

    @pl.when(pl.program_id(0) == 0)
    def _():
        lowered_ref[...] = lowered
        routed_ref[...] = routed

    @pl.when(pl.program_id(0) > 0)
    def _():
        lowered_ref[...] += lowered
        routed_ref[...] += routed

    parts_ref[0, 0] = contract(rows, first_grad, 0, 0).astype(jnp.bfloat16)
    parts_ref[0, 1] = contract(rows, second_grad, 0, 0).astype(jnp.bfloat16)
    parts_ref[0, 2] = contract(grads, activated, 0, 0).astype(jnp.bfloat16)


def gated(rows, grads, weights, tile):
    count, model_width = rows.shape
    chunks, _, _, hidden = weights.shape
    tiles = hidden // tile
    fixed = pl.BlockSpec((count, model_width), lambda step: (0, 0))
    moving = pl.BlockSpec(
        (1, 3, model_width, tile), lambda step: (step // tiles, 0, 0, step % tiles)
    )
    return pl.pallas_call(
        gated_kernel,
        grid=(chunks * tiles,),
        out_shape=(
            jax.ShapeDtypeStruct((count, model_width), jnp.float32),
            jax.ShapeDtypeStruct((count, model_width), jnp.float32),
            jax.ShapeDtypeStruct(weights.shape, jnp.bfloat16),
        ),
        in_specs=[fixed, fixed, moving],
        out_specs=(fixed, fixed, moving),
        compiler_params=pltpu.CompilerParams(vmem_limit_bytes=VMEM_BYTES),
        cost_estimate=pl.CostEstimate(
            flops=18 * count * model_width * chunks * hidden,
            transcendentals=count * chunks * hidden,
            bytes_accessed=12 * count * model_width + 12 * chunks * model_width * hidden,
        ),
        name="gated",
    )(rows, grads, weights)


def swap(piece, axes, size, step):
    return lax.ppermute(piece, axes, [(i, i ^ step) for i in range(size)])


def pick(stacked, index):
    return lax.dynamic_index_in_dim(stacked, index, 0, keepdims=False)


def share(piece, axes, size):
    return [piece] + [swap(piece, axes, size, step) for step in range(1, size)]


def natural(pieces, index):
    stacked = jnp.stack(pieces)
    return [pick(stacked, index ^ other) for other in range(len(pieces))]


def tied(*values):
    return lax.optimization_barrier(values)


def route(blocks):
    return lax.all_to_all(blocks, GROUP, split_axis=0, concat_axis=0)


def turned(field, cosine, sine, backward):
    half = HEAD_DIM // 2
    shape = field.shape
    split = field.reshape(shape[0], -1, 2, half, shape[-1])
    first_half = split[:, :, 0]
    second_half = split[:, :, 1]
    if backward:
        parts = [
            first_half * cosine + second_half * sine,
            second_half * cosine - first_half * sine,
        ]
    else:
        parts = [
            first_half * cosine - second_half * sine,
            second_half * cosine + first_half * sine,
        ]
    return jnp.stack(parts, 2).reshape(shape)


def tree_tables(segments, parents):
    count = parents.shape[1]
    labels = jnp.arange(count, dtype=jnp.int32)
    is_parent = parents[:, :, None] == labels[None, None, :]
    grand = jnp.sum(jnp.where(is_parent, parents[:, None, :], 0), 2)
    itself = labels[None, :, None] == labels[None, None, :]
    table = itself | is_parent | (grand[:, :, None] == labels[None, None, :])
    member = segments[:, None, :] == labels[None, :, None]
    lengths = jnp.sum(member.astype(jnp.int32), 2)
    ahead = jnp.sum(jnp.where(labels[:, None] > labels[None, :], lengths[:, None, :], 0), 2)
    moving = jnp.sum(jnp.where(table, lengths[:, None, :], 0), 2) - lengths - ahead
    place = jnp.arange(segments.shape[1], dtype=jnp.int32) + jnp.sum(
        jnp.where(member, moving[:, :, None], 0), 1
    )
    bits = jnp.sum(jnp.where(table, jnp.left_shift(1, labels)[None, None, :], 0), 2)
    paths = jnp.sum(jnp.where(member, bits[:, :, None], 0), 1)
    return (place, paths, jnp.left_shift(1, segments))


def local_fast(
    tokens,
    cotangent,
    segments,
    parents,
    routes,
    norm_gains,
    project,
    mixing,
    router,
    expander,
    reducer,
    spreader,
    collector,
):
    bf16, f32 = jnp.bfloat16, jnp.float32
    group_size = lax.axis_size(GROUP)
    seq_size = lax.axis_size(SEQ)
    shards = lax.axis_size(TENSOR)
    member_index = lax.axis_index(GROUP)
    seq_index = lax.axis_index(SEQ)
    shard = lax.axis_index(TENSOR)
    trees, rows, model_width = tokens.shape
    part_width = project.shape[2]
    owned = project.shape[1]
    hidden = spreader.shape[2]
    slots = CAP // shards
    quarter = rows // shards
    place_arg = seq_index.astype(jnp.int32).reshape(1)

    extra = EXPERTS + 2
    pad = -extra % 128
    small = jnp.concatenate(
        [
            project[0],
            project[1],
            project[2],
            mixing.T,
            router,
            norm_gains.T,
            jnp.zeros((owned, pad), bf16),
        ],
        1,
    )
    small = lax.all_gather(small, GROUP, axis=0, tiled=True)
    project_all = small[:, : 3 * part_width]
    mixing_own = small[:, 3 * part_width : 4 * part_width].T
    router_all = small[:, 4 * part_width : 4 * part_width + EXPERTS]
    gains = small[:, 4 * part_width + EXPERTS : 4 * part_width + extra].T.astype(f32)
    mixing_all = jnp.concatenate(share(mixing_own, TENSOR, shards), 0)
    labels = jnp.arange(EXPERTS, dtype=jnp.int32)
    named = jnp.any(routes[:, None, :, :] == labels[None, :, None, None], 3)
    earlier = (
        jnp.arange(rows, dtype=jnp.int32)[:, None] < jnp.arange(rows, dtype=jnp.int32)[None, :]
    )
    ranks = jnp.einsum(
        "bes,st->bet", named.astype(bf16), earlier.astype(bf16), preferred_element_type=f32
    ).astype(jnp.int32)
    slot_index = shard * slots + jnp.arange(slots, dtype=jnp.int32)
    chosen = (
        (named[:, :, None, :] & (ranks[:, :, None, :] == slot_index[None, None, :, None]))
        .astype(bf16)
        .reshape(trees, EXPERTS * slots, rows)
    )

    def send_rows(field):
        picked = jnp.einsum("bst,btd->bsd", chosen, field, preferred_element_type=f32).astype(bf16)
        picked = picked.reshape(trees, EXPERTS, slots, field.shape[-1]).swapaxes(0, 1)
        return route(picked).reshape(EXPERTS * trees * slots, field.shape[-1])

    def return_rows(field):
        back = route(field.reshape(EXPERTS, trees, slots, field.shape[-1])).swapaxes(0, 1)
        back = back.reshape(trees, EXPERTS * slots, field.shape[-1])
        return jnp.einsum("bst,bsd->btd", chosen, back, preferred_element_type=f32)

    place, paths, key_bits = tree_tables(segments, parents)
    offset = seq_index * rows
    own_place = lax.dynamic_slice_in_dim(place, offset, rows, 1).astype(f32)
    own_paths = lax.dynamic_slice_in_dim(paths, offset, rows, 1)
    half = HEAD_DIM // 2
    rates = jnp.exp(-math.log(theta) * 2.0 * jnp.arange(half, dtype=f32) / HEAD_DIM)
    angle = rates[None, :, None] * own_place[:, None, :]
    cosine = jnp.cos(angle)[:, None]
    sine = jnp.sin(angle)[:, None]
    inputs = tokens.astype(f32)
    scale_one = lax.rsqrt(jnp.mean(inputs * inputs, -1, keepdims=True) + epsilon)
    first_in = (inputs * scale_one * gains[0]).astype(bf16)
    mapped = jnp.einsum("dh,btd->bht", project_all, first_in, preferred_element_type=f32)
    queries = (
        turned(mapped[:, :part_width], cosine, sine, False) * HEAD_DIM ** (-0.5)
    ).astype(bf16)
    pairs_own = jnp.concatenate(
        [
            turned(mapped[:, part_width : 2 * part_width], cosine, sine, False).astype(bf16),
            mapped[:, 2 * part_width :].astype(bf16),
        ],
        1,
    )
    pairs = [pairs_own]
    for _ in range(1, seq_size):
        pairs.append(lax.ppermute(pairs[-1], SEQ, [(i, i + 1) for i in range(seq_size - 1)]))
    key_column = key_bits[:, :, None]
    path_row = own_paths[:, None, :]
    state = ()
    for number in range(seq_size):
        state = attend(
            number,
            number == seq_size - 1,
            place_arg,
            queries,
            key_column,
            path_row,
            pairs[number],
            state,
        )
    outs, logs = state[:2]

    bundles = jnp.concatenate([expander, reducer.transpose(0, 2, 1)[:, None]], 1)
    own_expert = route(bundles).swapaxes(0, 1).reshape(3, model_width, hidden)
    expert_weights = lax.all_gather(own_expert, TENSOR, axis=0, tiled=False)
    shared_bundle = jnp.concatenate([spreader, collector.T[None]], 0)
    shared_bundle, expert_weights = tied(shared_bundle, expert_weights)
    shared_weights = lax.all_gather(
        shared_bundle, GROUP, axis=1, tiled=True
    )
    heads = jnp.concatenate(
        [outs] + [swap(outs, TENSOR, shards, step) for step in range(1, shards)], 1
    )
    upstream_rows = send_rows(cotangent)
    heads, upstream_rows = tied(heads, upstream_rows)
    second = inputs + jnp.einsum("bht,hd->btd", heads, mixing_all, preferred_element_type=f32)

    scale_two = lax.rsqrt(jnp.mean(second * second, -1, keepdims=True) + epsilon)
    hidden_in = (second * scale_two * gains[1]).astype(bf16)
    expert_rows, shared_weights = tied(send_rows(hidden_in), shared_weights)
    row_chances = jax.nn.softmax(jnp.dot(expert_rows, router_all, preferred_element_type=f32), -1)
    own_label = jnp.arange(EXPERTS, dtype=jnp.int32) == member_index
    row_gates = jnp.sum(jnp.where(own_label[None], row_chances, 0.0), -1, keepdims=True)
    row_grads = (row_gates * upstream_rows.astype(f32)).astype(bf16)
    lowered, routed_back, expert_parts = gated(expert_rows, row_grads, expert_weights, 256)
    flat = (trees * rows, model_width)
    shared_out, shared_back, shared_parts = gated(
        hidden_in.reshape(flat),
        cotangent.reshape(flat),
        shared_weights[None],
        256,
    )
    expert_own = lax.psum_scatter(expert_parts, TENSOR, scatter_dimension=0, tiled=False)
    gate_grads = jnp.sum(upstream_rows.astype(f32) * lowered, -1, keepdims=True)
    lanes = jnp.arange(128, dtype=jnp.int32)[None]
    back_rows = jnp.concatenate(
        [
            routed_back.astype(bf16),
            jnp.where(lanes == member_index, gate_grads, 0.0).astype(bf16),
        ],
        1,
    )
    returned_back = return_rows(back_rows)
    def own_rows(field):
        return lax.dynamic_slice_in_dim(field, shard * quarter, quarter, 1)

    def add_shards(field):
        pieces = field.astype(bf16)
        mine = own_rows(pieces).astype(f32)
        for step in range(1, shards):
            sent = lax.dynamic_slice_in_dim(pieces, (shard ^ step) * quarter, quarter, 1)
            mine = mine + swap(sent, TENSOR, shards, step).astype(f32)
        return mine

    def spread_shards(field):
        return jnp.concatenate(natural(share(field, TENSOR, shards), shard), 1)

    summed = add_shards(
        returned_back
        + jnp.pad(shared_back.reshape(trees, rows, model_width), ((0, 0), (0, 0), (0, 128)))
    )
    summed, expert_own = tied(summed, expert_own)
    chance_grad = summed[..., model_width : model_width + EXPERTS]
    quarter_second = own_rows(second)
    quarter_scale = own_rows(scale_two)
    quarter_normed = quarter_second * quarter_scale
    quarter_hidden = own_rows(hidden_in)
    logits = jnp.dot(quarter_hidden, router_all, preferred_element_type=f32)
    chances = jax.nn.softmax(logits, -1)
    logit_grad = chances * (chance_grad - jnp.sum(chances * chance_grad, -1, keepdims=True))
    hidden_grad = summed[..., :model_width] + jnp.einsum(
        "bte,de->btd", logit_grad, router_all.astype(f32), precision=highest
    )
    router_part = jnp.einsum(
        "btd,bte->de", quarter_hidden.astype(f32), logit_grad, precision=highest
    )
    gain_two = jnp.sum(hidden_grad * quarter_normed, (0, 1))
    scaled_two = hidden_grad * gains[1]
    second_grad = own_rows(cotangent).astype(f32) + quarter_scale * (
        scaled_two - quarter_normed * jnp.mean(scaled_two * quarter_normed, -1, keepdims=True)
    )
    branch_grad = spread_shards(second_grad.astype(bf16))
    returned_out = return_rows((row_gates * lowered).astype(bf16))
    branch_grad, returned_out = tied(branch_grad, returned_out)
    partial_out = (returned_out + shared_out.reshape(trees, rows, model_width)).astype(bf16)
    branches = lax.psum(partial_out, TENSOR).astype(f32)
    branches, shared_parts = tied(branches, shared_parts)
    shared_grads = lax.psum_scatter(
        shared_parts[0], GROUP, scatter_dimension=1, tiled=True
    ).astype(f32)
    spreader_grad = shared_grads[:2]
    collector_grad = shared_grads[2].T
    output = (second + branches).astype(bf16)

    heads_grad = jnp.einsum(
        "hd,btd->bht", mixing_own, branch_grad, preferred_element_type=f32
    ).astype(bf16)
    mixing_part = jnp.einsum("btd,bht->dh", branch_grad, outs, preferred_element_type=f32)
    query_grad = ()
    pair_grads = []
    for number in range(seq_size - 1, -1, -1):
        query_grad, pair_grad = attend_back(
            number,
            bf16 if number == seq_size - 1 else f32,
            place_arg,
            (queries, outs, heads_grad, logs, key_column, path_row, pairs[number])
            + ((query_grad,) if pair_grads else ()),
        )
        pair_grads.append(pair_grad)
    blocks = expert_own.reshape(3, group_size, owned, hidden).swapaxes(0, 1)
    expert_home = route(blocks)
    pair_grad, expert_home = tied(pair_grads[0], expert_home)
    expert_grads = expert_home.astype(f32)
    for addend in pair_grads[1:]:
        moved = lax.ppermute(
            pair_grad.astype(bf16), SEQ, [(i + 1, i) for i in range(seq_size - 1)]
        )
        pair_grad = addend + moved.astype(f32)
    expander_grad = expert_grads[:, :2]
    reducer_grad = expert_grads[:, 2].transpose(0, 2, 1)
    query_grad = query_grad * HEAD_DIM ** (-0.5)
    mapped_grad = jnp.concatenate(
        [
            turned(query_grad, cosine, sine, True),
            turned(pair_grad[:, :part_width], cosine, sine, True),
            pair_grad[:, part_width:],
        ],
        1,
    ).astype(bf16)
    project_part = jnp.einsum("btd,bht->dh", first_in, mapped_grad, preferred_element_type=f32)
    first_grad = add_shards(
        jnp.einsum("bht,dh->btd", mapped_grad, project_all, preferred_element_type=f32)
    )
    quarter_scale_one = own_rows(scale_one)
    quarter_normed_one = own_rows(inputs) * quarter_scale_one
    scaled_one = first_grad * gains[0]
    input_grad = spread_shards(
        (
            second_grad
            + quarter_scale_one
            * (
                scaled_one
                - quarter_normed_one * jnp.mean(scaled_one * quarter_normed_one, -1, keepdims=True)
            )
        ).astype(bf16)
    )

    small_parts = jnp.concatenate(
        [
            project_part,
            mixing_part,
            router_part,
            gain_two[:, None],
            jnp.zeros((model_width, -(4 * part_width + EXPERTS + 1) % 128), f32),
        ],
        1,
    ).astype(bf16)
    small_grads = jnp.sum(
        route(small_parts.reshape(group_size, owned, -1)).astype(f32),
        0,
    )
    project_grad = (
        small_grads[:, : 3 * part_width].reshape(owned, 3, part_width).transpose(1, 0, 2)
    )
    mixing_grad = small_grads[:, 3 * part_width : 4 * part_width].T
    rest = small_grads[:, 4 * part_width : 4 * part_width + EXPERTS + 1]
    gain_one = jnp.sum(project_grad * project.astype(f32), (0, 2)) / norm_gains[0].astype(f32)
    tiny = lax.psum(
        jnp.concatenate([rest.T, gain_one[None]], 0),
        TENSOR,
    )
    router_grad = tiny[:EXPERTS].T
    gain_grad = jnp.stack([tiny[EXPERTS + 1], tiny[EXPERTS]])
    return (
        output,
        input_grad,
        gain_grad,
        project_grad,
        mixing_grad,
        router_grad,
        expander_grad,
        reducer_grad,
        spreader_grad,
        collector_grad,
    )


def solution(mesh):
    in_specs = (
        P(DP, SEQ, None),
        P(DP, SEQ, None),
        P(DP, None),
        P(DP, None),
        P(DP, SEQ, None),
        P(None, GROUP),
        P(None, GROUP, TENSOR),
        P(TENSOR, GROUP),
        P(GROUP, None),
        P(None, None, GROUP, TENSOR),
        P(None, TENSOR, GROUP),
        P(None, GROUP, TENSOR),
        P(TENSOR, GROUP),
    )
    out_specs = (
        P(DP, SEQ, None),
        P(DP, SEQ, None),
        P(None, GROUP),
        P(None, GROUP, TENSOR),
        P(TENSOR, GROUP),
        P(GROUP, None),
        P(None, None, GROUP, TENSOR),
        P(None, TENSOR, GROUP),
        P(None, GROUP, TENSOR),
        P(TENSOR, GROUP),
    )
    sizes = mesh.shape
    group_size = sizes[DP] * sizes[SEQ]
    shards = sizes[TENSOR]
    fits = group_size == EXPERTS and shards & (shards - 1) == 0 and CAP % shards == 0
    body = local_fast if fits else local
    return jax.shard_map(body, mesh=mesh, in_specs=in_specs, out_specs=out_specs, check_vma=False)
```

```python
import functools
import math
import types

import jax
import jax.numpy as jnp
from jax import lax
from jax.experimental import pallas as pl
from jax.experimental.layout import Layout, with_layout_constraint
from jax.experimental.pallas import tpu as pltpu
from jax.sharding import PartitionSpec as P

HEAD_DIM = 64
EXPERTS = 8
CAP = 192
QB = 512
DP = "dp"
SEQ = "seq"
TENSOR = "tensor"
GROUP = (DP, SEQ)


epsilon = 1e-05
theta = 10000.0
highest = lax.Precision.HIGHEST


def ancestry(parents):
    labels = jnp.arange(parents.shape[0], dtype=jnp.int32)
    grandparent = jnp.take(parents, parents)
    itself = labels[:, None] == labels[None, :]
    return (
        itself | (parents[:, None] == labels[None, :]) | (grandparent[:, None] == labels[None, :])
    )


def positions(segments, table):
    labels = jnp.arange(table.shape[0], dtype=jnp.int32)
    member = (segments[:, None] == labels[None, :]).astype(jnp.int32)
    lengths = jnp.sum(member, 0)
    offsets = jnp.cumsum(lengths) - lengths
    ancestral = jnp.sum(table.astype(jnp.int32) * lengths[None, :], 1) - lengths
    moving = ancestral - offsets
    return jnp.arange(segments.shape[0], dtype=jnp.int32) + jnp.sum(member * moving[None, :], 1)


def visible(row_segments, row_index, key_segments, key_index, table):
    labels = jnp.arange(table.shape[0], dtype=jnp.int32)
    member_rows = (row_segments[:, None] == labels[None, :]).astype(jnp.bfloat16)
    member_keys = (key_segments[:, None] == labels[None, :]).astype(jnp.bfloat16)
    reach = jnp.dot(member_rows, table.astype(jnp.bfloat16), preferred_element_type=jnp.float32)
    hits = jnp.einsum(
        "bs,ls->bl", reach.astype(jnp.bfloat16), member_keys, preferred_element_type=jnp.float32
    )
    return (hits > 0.5) & (key_index[None, :] <= row_index[:, None])


def turn(field, place, backward):
    half = field.shape[-1] // 2
    rates = jnp.exp(-math.log(theta) * 2.0 * jnp.arange(half, dtype=jnp.float32) / field.shape[-1])
    angle = place[:, None] * rates[None, :]
    cosine = jnp.cos(angle)[:, None, :]
    sine = jnp.sin(angle)[:, None, :]
    first_half = field[..., :half]
    second_half = field[..., half:]
    if backward:
        return jnp.concatenate(
            [first_half * cosine + second_half * sine, second_half * cosine - first_half * sine], -1
        )
    return jnp.concatenate(
        [first_half * cosine - second_half * sine, second_half * cosine + first_half * sine], -1
    )


def slot_of(route_flat):
    labels = jnp.arange(EXPERTS, dtype=jnp.int32)
    member = (route_flat[:, None] == labels[None, :]).astype(jnp.int32)
    ranks = jnp.cumsum(member, 0) - 1
    return route_flat * CAP + jnp.sum(ranks * member, 1)


def owner_of(slot_ids, count_rows, per_row):
    picked = jnp.arange(slot_ids.shape[0], dtype=jnp.int32) // per_row
    return jnp.full((EXPERTS * CAP,), count_rows, jnp.int32).at[slot_ids].set(picked)


def silu_slope(value):
    sigma = jax.nn.sigmoid(value)
    return sigma * (1.0 + value * (1.0 - sigma))


def block_scores(query_block, key_block, seg_block, index_block, key_segments, key_index, table):
    seen = visible(seg_block, index_block, key_segments, key_index, table)
    raw = jnp.einsum("bhd,lhd->hbl", query_block, key_block, preferred_element_type=jnp.float32)
    return jnp.where(seen[None], raw * HEAD_DIM ** (-0.5), -1e30)


def fetch(norm_gains, project, mixing, router, expander, reducer, spreader, collector):
    return (
        lax.all_gather(norm_gains, GROUP, axis=1, tiled=True),
        lax.all_gather(project, GROUP, axis=1, tiled=True),
        lax.all_gather(mixing, GROUP, axis=1, tiled=True),
        lax.all_gather(router, GROUP, axis=0, tiled=True),
        lax.all_gather(expander, GROUP, axis=2, tiled=True),
        lax.all_gather(reducer, GROUP, axis=2, tiled=True),
        lax.all_gather(spreader, GROUP, axis=1, tiled=True),
        lax.all_gather(collector, GROUP, axis=1, tiled=True),
    )


def reduce_end(grads):
    (
        gain_part,
        project_part,
        mixing_part,
        router_part,
        expander_part,
        reducer_part,
        spreader_part,
        collector_part,
    ) = grads
    return (
        lax.psum_scatter(gain_part, GROUP, scatter_dimension=1, tiled=True),
        lax.psum_scatter(project_part, GROUP, scatter_dimension=1, tiled=True),
        lax.psum_scatter(mixing_part, GROUP, scatter_dimension=1, tiled=True),
        lax.psum_scatter(router_part, GROUP, scatter_dimension=0, tiled=True),
        lax.psum_scatter(expander_part, GROUP, scatter_dimension=2, tiled=True),
        lax.psum_scatter(reducer_part, GROUP, scatter_dimension=2, tiled=True),
        lax.psum_scatter(spreader_part, GROUP, scatter_dimension=1, tiled=True),
        lax.psum_scatter(collector_part, GROUP, scatter_dimension=1, tiled=True),
    )


def forward_pass(tree_tokens, tree_segments, tree_parents, tree_routes, weights, offset):
    norm_gains, project, mixing, router, expander, reducer, spreader, collector = weights
    row_count = tree_tokens.shape[0]
    model_width = tree_tokens.shape[1]
    tree_length = tree_segments.shape[0]
    local_heads = project.shape[2] // HEAD_DIM
    table = ancestry(tree_parents)
    place = lax.dynamic_slice_in_dim(positions(tree_segments, table), offset, row_count).astype(
        jnp.float32
    )
    row_segments = lax.dynamic_slice_in_dim(tree_segments, offset, row_count)
    row_index = offset + jnp.arange(row_count, dtype=jnp.int32)
    key_index = jnp.arange(tree_length, dtype=jnp.int32)
    inputs = tree_tokens.astype(jnp.float32)
    scale_one = lax.rsqrt(jnp.mean(inputs * inputs, -1, keepdims=True) + epsilon)
    normed_one = inputs * scale_one
    first_in = (normed_one * norm_gains[0].astype(jnp.float32)).astype(jnp.bfloat16)
    mapped = jnp.einsum("td,cdh->cth", first_in, project, preferred_element_type=jnp.float32)
    head_shape = (row_count, local_heads, HEAD_DIM)
    queries = turn(mapped[0].reshape(head_shape), place, False).astype(jnp.bfloat16)
    keys_own = (
        turn(mapped[1].reshape(head_shape), place, False)
        .astype(jnp.bfloat16)
        .reshape(row_count, -1)
    )
    values_own = mapped[2].astype(jnp.bfloat16)
    keys_flat, values_flat = (
        lax.all_gather(keys_own, SEQ, axis=0, tiled=True),
        lax.all_gather(values_own, SEQ, axis=0, tiled=True),
    )
    keys_all = keys_flat.reshape(tree_length, local_heads, HEAD_DIM)
    values_all = values_flat.reshape(tree_length, local_heads, HEAD_DIM)
    blocks = row_count // QB
    query_blocks = queries.reshape(blocks, QB, local_heads, HEAD_DIM)
    seg_blocks = row_segments.reshape(blocks, QB)
    index_blocks = row_index.reshape(blocks, QB)

    def attend(entries):
        query_block, seg_block, index_block = entries
        scores = block_scores(
            query_block, keys_all, seg_block, index_block, tree_segments, key_index, table
        )
        row_peak = jnp.max(scores, -1, keepdims=True)
        expo = jnp.exp(scores - row_peak)
        row_total = jnp.sum(expo, -1, keepdims=True)
        chances_soft = expo / row_total
        mixed_block = jnp.einsum(
            "hbl,lhd->bhd",
            chances_soft.astype(jnp.bfloat16),
            values_all,
            preferred_element_type=jnp.float32,
        )
        return (mixed_block, (row_peak + jnp.log(row_total))[..., 0])

    mixed, log_totals = lax.map(attend, (query_blocks, seg_blocks, index_blocks))
    heads_out = mixed.reshape(row_count, -1).astype(jnp.bfloat16)
    attended = lax.psum(
        jnp.dot(heads_out, mixing, preferred_element_type=jnp.float32).astype(jnp.bfloat16),
        TENSOR,
    ).astype(jnp.float32)
    second = inputs + attended
    scale_two = lax.rsqrt(jnp.mean(second * second, -1, keepdims=True) + epsilon)
    normed_two = second * scale_two
    hidden_in = (normed_two * norm_gains[1].astype(jnp.float32)).astype(jnp.bfloat16)
    logits = jnp.dot(hidden_in, router, preferred_element_type=jnp.float32)
    shifted = jnp.exp(logits - jnp.max(logits, -1, keepdims=True))
    chances = shifted / jnp.sum(shifted, -1, keepdims=True)
    picks = (tree_routes[:, :, None] == jnp.arange(EXPERTS, dtype=jnp.int32)[None, None, :]).astype(
        jnp.float32
    )
    gates = jnp.sum(picks * chances[:, None, :], -1)
    per_row = tree_routes.shape[1]
    slot_ids = slot_of(tree_routes.reshape(-1))
    owners = owner_of(slot_ids, row_count, per_row)
    padded = jnp.concatenate([hidden_in, jnp.zeros((1, model_width), jnp.bfloat16)], 0)
    routed = jnp.take(padded, owners, axis=0).reshape(EXPERTS, CAP, model_width)
    raised = jnp.einsum("ecd,egdf->gecf", routed, expander, preferred_element_type=jnp.float32)
    activated = (jax.nn.silu(raised[0]) * raised[1]).astype(jnp.bfloat16)
    lowered = jnp.einsum(
        "ecf,efd->ecd", activated, reducer, preferred_element_type=jnp.float32
    ).reshape(EXPERTS * CAP, model_width)
    returned = jnp.take(lowered, slot_ids, axis=0).reshape(row_count, per_row, model_width)
    blended = jnp.sum(gates[:, :, None] * returned, 1)
    spread = jnp.einsum("td,gdf->gtf", hidden_in, spreader, preferred_element_type=jnp.float32)
    common = (jax.nn.silu(spread[0]) * spread[1]).astype(jnp.bfloat16)
    shared_out = jnp.dot(common, collector, preferred_element_type=jnp.float32)
    branches = lax.psum((blended + shared_out).astype(jnp.bfloat16), TENSOR).astype(jnp.float32)
    output_tree = (second + branches).astype(jnp.bfloat16)
    kept = types.SimpleNamespace(
        table=table,
        place=place,
        offset=offset,
        row_segments=row_segments,
        seg_blocks=seg_blocks,
        index_blocks=index_blocks,
        scale_one=scale_one,
        normed_one=normed_one,
        first_in=first_in,
        queries=queries,
        query_blocks=query_blocks,
        keys_all=keys_all,
        values_all=values_all,
        log_totals=log_totals,
        heads_out=heads_out,
        scale_two=scale_two,
        normed_two=normed_two,
        hidden_in=hidden_in,
        chances=chances,
        picks=picks,
        gates=gates,
        slot_ids=slot_ids,
        routed=routed,
        raised=raised,
        activated=activated,
        returned=returned,
        spread=spread,
        common=common,
    )
    return (kept, output_tree)


def backward_pass(tree_cot, tree_segments, kept, weights):
    norm_gains, project, mixing, router, expander, reducer, spreader, collector = weights
    upstream = tree_cot.astype(jnp.float32)
    row_count = upstream.shape[0]
    model_width = upstream.shape[1]
    shared_grad = upstream.astype(jnp.bfloat16)
    common_grad = jnp.einsum(
        "td,fd->tf", shared_grad, collector, preferred_element_type=jnp.float32
    )
    collector_part = jnp.einsum(
        "tf,td->fd", kept.common, shared_grad, preferred_element_type=jnp.float32
    )
    spread = kept.spread
    spread_grad = jnp.stack(
        [common_grad * spread[1] * silu_slope(spread[0]), common_grad * jax.nn.silu(spread[0])]
    ).astype(jnp.bfloat16)
    spreader_part = jnp.einsum(
        "td,gtf->gdf", kept.hidden_in, spread_grad, preferred_element_type=jnp.float32
    )
    hidden_grad = jnp.einsum(
        "gtf,gdf->td", spread_grad, spreader, preferred_element_type=jnp.float32
    )
    gates = kept.gates
    slot_ids = kept.slot_ids
    per_row = gates.shape[1]
    pair_grad = (
        (gates[:, :, None] * upstream[:, None, :])
        .astype(jnp.bfloat16)
        .reshape(row_count * per_row, model_width)
    )
    lowered_grad = (
        jnp.zeros((EXPERTS * CAP, model_width), jnp.bfloat16)
        .at[slot_ids]
        .set(pair_grad)
        .reshape(EXPERTS, CAP, model_width)
    )
    activated_grad = jnp.einsum(
        "ecd,efd->ecf", lowered_grad, reducer, preferred_element_type=jnp.float32
    )
    reducer_part = jnp.einsum(
        "ecf,ecd->efd", kept.activated, lowered_grad, preferred_element_type=jnp.float32
    )
    raised = kept.raised
    raised_grad = jnp.stack(
        [
            activated_grad * raised[1] * silu_slope(raised[0]),
            activated_grad * jax.nn.silu(raised[0]),
        ]
    ).astype(jnp.bfloat16)
    expander_part = jnp.einsum(
        "ecd,gecf->egdf", kept.routed, raised_grad, preferred_element_type=jnp.float32
    )
    routed_grad = jnp.einsum(
        "gecf,egdf->ecd", raised_grad, expander, preferred_element_type=jnp.float32
    ).reshape(EXPERTS * CAP, model_width)
    hidden_grad = hidden_grad + jnp.sum(
        jnp.take(routed_grad, slot_ids, axis=0).reshape(row_count, per_row, model_width), 1
    )
    gate_grad = jnp.sum(upstream[:, None, :] * kept.returned, -1)
    hidden_grad, gate_grad = (
        lax.psum(hidden_grad.astype(jnp.bfloat16), TENSOR).astype(jnp.float32),
        lax.psum(gate_grad.astype(jnp.bfloat16), TENSOR).astype(jnp.float32),
    )
    chances = kept.chances
    chance_grad = jnp.sum(kept.picks * gate_grad[:, :, None], 1)
    logit_grad = chances * (chance_grad - jnp.sum(chances * chance_grad, -1, keepdims=True))
    hidden_grad = hidden_grad + jnp.dot(logit_grad, router.astype(jnp.float32).T, precision=highest)
    router_part = jnp.dot(kept.hidden_in.astype(jnp.float32).T, logit_grad, precision=highest)
    normed_two = kept.normed_two
    gain_two = jnp.sum(hidden_grad * normed_two, 0)
    scaled_two = hidden_grad * norm_gains[1].astype(jnp.float32)
    second_grad = upstream + kept.scale_two * (
        scaled_two - normed_two * jnp.mean(scaled_two * normed_two, -1, keepdims=True)
    )
    branch_grad = second_grad.astype(jnp.bfloat16)
    mixing_part = jnp.einsum(
        "th,td->hd", kept.heads_out, branch_grad, preferred_element_type=jnp.float32
    )
    heads_grad = jnp.einsum(
        "td,hd->th", branch_grad, mixing, preferred_element_type=jnp.float32
    ).astype(jnp.bfloat16)
    keys_all = kept.keys_all
    values_all = kept.values_all
    table = kept.table
    query_blocks = kept.query_blocks
    tree_length = keys_all.shape[0]
    local_heads = keys_all.shape[1]
    key_index = jnp.arange(tree_length, dtype=jnp.int32)
    grad_blocks = heads_grad.reshape(query_blocks.shape)
    factor = HEAD_DIM ** (-0.5)

    def attend_back(carry, entries):
        keys_grad, values_grad = carry
        query_block, grad_block, log_block, seg_block, index_block = entries
        scores = block_scores(
            query_block, keys_all, seg_block, index_block, tree_segments, key_index, table
        )
        chances_soft = jnp.exp(scores - log_block[..., None])
        prob_grad = jnp.einsum(
            "bhd,lhd->hbl", grad_block, values_all, preferred_element_type=jnp.float32
        )
        centre = jnp.sum(chances_soft * prob_grad, -1, keepdims=True)
        score_grad = (chances_soft * (prob_grad - centre) * factor).astype(jnp.bfloat16)
        query_grad_block = jnp.einsum(
            "hbl,lhd->bhd", score_grad, keys_all, preferred_element_type=jnp.float32
        )
        keys_grad = keys_grad + jnp.einsum(
            "hbl,bhd->lhd", score_grad, query_block, preferred_element_type=jnp.float32
        )
        values_grad = values_grad + jnp.einsum(
            "hbl,bhd->lhd",
            chances_soft.astype(jnp.bfloat16),
            grad_block,
            preferred_element_type=jnp.float32,
        )
        return ((keys_grad, values_grad), query_grad_block)

    zero_kv = jnp.zeros((tree_length, local_heads, HEAD_DIM), jnp.float32)
    (keys_grad, values_grad), query_grad = lax.scan(
        attend_back,
        (zero_kv, zero_kv),
        (query_blocks, grad_blocks, kept.log_totals, kept.seg_blocks, kept.index_blocks),
    )
    keys_own_grad, values_own_grad = (
        lax.psum_scatter(
            keys_grad.reshape(tree_length, -1).astype(jnp.bfloat16),
            SEQ,
            scatter_dimension=0,
            tiled=True,
        ).astype(jnp.float32),
        lax.psum_scatter(
            values_grad.reshape(tree_length, -1).astype(jnp.bfloat16),
            SEQ,
            scatter_dimension=0,
            tiled=True,
        ).astype(jnp.float32),
    )
    place = kept.place
    query_back = turn(query_grad.reshape(row_count, local_heads, HEAD_DIM), place, True).reshape(
        row_count, -1
    )
    key_back = turn(keys_own_grad.reshape(row_count, local_heads, HEAD_DIM), place, True).reshape(
        row_count, -1
    )
    mapped_grad = jnp.stack([query_back, key_back, values_own_grad]).astype(jnp.bfloat16)
    project_part = jnp.einsum(
        "td,cth->cdh", kept.first_in, mapped_grad, preferred_element_type=jnp.float32
    )
    first_grad = lax.psum(
        jnp.einsum("cth,cdh->td", mapped_grad, project, preferred_element_type=jnp.float32).astype(
            jnp.bfloat16
        ),
        TENSOR,
    ).astype(jnp.float32)
    normed_one = kept.normed_one
    gain_one = jnp.sum(first_grad * normed_one, 0)
    scaled_one = first_grad * norm_gains[0].astype(jnp.float32)
    input_tree = (
        second_grad
        + kept.scale_one
        * (scaled_one - normed_one * jnp.mean(scaled_one * normed_one, -1, keepdims=True))
    ).astype(jnp.bfloat16)
    gain_part = jnp.stack([gain_one, gain_two])
    return (
        input_tree,
        (
            gain_part,
            project_part,
            mixing_part,
            router_part,
            expander_part,
            reducer_part,
            spreader_part,
            collector_part,
        ),
    )


def local(
    tokens,
    cotangent,
    segments,
    parents,
    routes,
    norm_gains,
    project,
    mixing,
    router,
    expander,
    reducer,
    spreader,
    collector,
):
    tree_count = tokens.shape[0]
    offset = lax.axis_index(SEQ) * tokens.shape[1]
    outputs = []
    input_grads = []
    running = None
    for tree_index in range(tree_count):
        forward_weights = fetch(
            norm_gains, project, mixing, router, expander, reducer, spreader, collector
        )
        kept, output_tree = forward_pass(
            tokens[tree_index],
            segments[tree_index],
            parents[tree_index],
            routes[tree_index],
            forward_weights,
            offset,
        )
        backward_weights = fetch(
            norm_gains, project, mixing, router, expander, reducer, spreader, collector
        )
        input_tree, tree_grads = backward_pass(
            cotangent[tree_index], segments[tree_index], kept, backward_weights
        )
        outputs.append(output_tree)
        input_grads.append(input_tree)
        if running is None:
            running = tree_grads
        else:
            running = tuple((before + addend for before, addend in zip(running, tree_grads)))
    running = reduce_end(running)
    return (
        jnp.stack(outputs),
        jnp.stack(input_grads),
        running[0],
        running[1],
        running[2],
        running[3],
        running[4],
        running[5],
        running[6],
        running[7],
    )


VMEM_BYTES = 56 << 20
TILE = 256
ROWS = 256


def contract(left, right, left_dim, right_dim):
    return lax.dot_general(
        left, right, (((left_dim,), (right_dim,)), ((), ())), preferred_element_type=jnp.float32
    )


def spans(head, width):
    if isinstance(head, int):
        start = head * HEAD_DIM
    else:
        start = pl.multiple_of(head * HEAD_DIM, HEAD_DIM)
    return (pl.ds(start, HEAD_DIM), pl.ds(width + start, HEAD_DIM), pl.ds(head, 1))


def scores_of(keys, queries, seen):
    return jnp.where(seen, contract(keys, queries, 0, 0), -1e30)


def seen_block(number, place_ref, key_bits_ref, query_bits, length):
    start = pl.multiple_of((place_ref[0] - number) * length, length)
    seen = (key_bits_ref[pl.ds(start, length), :] & query_bits) != 0
    if number == 0:
        keys = lax.broadcasted_iota(jnp.int32, seen.shape, 0)
        rows = lax.broadcasted_iota(jnp.int32, seen.shape, 1)
        seen = seen & (keys <= rows)
    return seen


def attend_kernel(number, final, heads, place_ref, query_ref, key_bits_ref, query_bits_ref, *refs):
    pair_ref = refs[0]
    if number:
        old_peak_ref, old_total_ref, old_mixed_ref = refs[1:4]
    peak_ref, total_ref, mixed_ref = refs[-3:]
    length = query_ref.shape[1]
    width = heads * HEAD_DIM

    def block():
        seen = seen_block(number, place_ref, key_bits_ref, query_bits_ref[...], length)

        def one(head, _):
            span, value_span, row = spans(head, width)
            scores = scores_of(pair_ref[span, :], query_ref[span, :], seen)
            peak = jnp.max(scores, 0, keepdims=True)
            if number:
                before = old_peak_ref[row, :]
                peak = jnp.maximum(before, peak)
                shrink = jnp.exp(before - peak)
            expo = jnp.exp(scores - peak)
            total = jnp.sum(expo, 0, keepdims=True)
            mixed = jnp.dot(
                pair_ref[value_span, :],
                expo.astype(jnp.bfloat16),
                preferred_element_type=jnp.float32,
            )
            if number:
                total = total + shrink * old_total_ref[row, :]
                mixed = mixed + shrink * old_mixed_ref[span, :]
            peak_ref[row, :] = peak
            total_ref[row, :] = total
            mixed_ref[span, :] = mixed
            return 0

        lax.fori_loop(0, heads, one, 0)

    def keep():
        peak_ref[...] = old_peak_ref[...]
        total_ref[...] = old_total_ref[...]
        mixed_ref[...] = old_mixed_ref[...]

    if number:
        pl.when(place_ref[0] >= number)(block)
        pl.when(place_ref[0] < number)(keep)
    else:
        block()
    if final:
        out_ref, log_ref = refs[4:6]
        for head in range(heads):
            span, _, row = spans(head, width)
            out_ref[span, :] = (mixed_ref[span, :] / total_ref[row, :]).astype(out_ref.dtype)
            log_ref[row, :] = peak_ref[row, :] + jnp.log(total_ref[row, :])


def attend_back_kernel(
    number,
    heads,
    place_ref,
    query_ref,
    out_ref,
    grad_ref,
    log_ref,
    key_bits_ref,
    query_bits_ref,
    pair_ref,
    *refs
):
    query_grad_ref, pair_grad_ref = refs[-2:]
    length = query_ref.shape[1]
    width = heads * HEAD_DIM

    def block():
        seen = seen_block(number, place_ref, key_bits_ref, query_bits_ref[...], length)

        def one(head, _):
            span, value_span, row = spans(head, width)
            queries = query_ref[span, :]
            grads = grad_ref[span, :]
            keys = pair_ref[span, :]
            centre = jnp.sum(
                grads.astype(jnp.float32) * out_ref[span, :].astype(jnp.float32), 0, keepdims=True
            )
            chances = jnp.exp(scores_of(keys, queries, seen) - log_ref[row, :])
            prob_grad = contract(pair_ref[value_span, :], grads, 0, 0)
            score_grad = (chances * (prob_grad - centre)).astype(jnp.bfloat16)
            value_grad = contract(grads, chances.astype(jnp.bfloat16), 1, 1)
            key_grad = contract(queries, score_grad, 1, 1)
            query_grad = jnp.dot(keys, score_grad, preferred_element_type=jnp.float32)
            pair_grad_ref[span, :] = key_grad.astype(pair_grad_ref.dtype)
            pair_grad_ref[value_span, :] = value_grad.astype(pair_grad_ref.dtype)
            if len(refs) > 2:
                query_grad = query_grad + refs[0][span, :]
            query_grad_ref[span, :] = query_grad
            return 0

        lax.fori_loop(0, heads, one, 0)

    def empty():
        pair_grad_ref[...] = jnp.zeros_like(pair_grad_ref)
        if len(refs) > 2:
            query_grad_ref[...] = refs[0][...]
        else:
            query_grad_ref[...] = jnp.zeros_like(query_grad_ref)

    if number:
        pl.when(place_ref[0] >= number)(block)
        pl.when(place_ref[0] < number)(empty)
    else:
        block()


def per_tree(array):
    return pl.BlockSpec((None,) + array.shape[1:], lambda tree: (tree, 0, 0))


def attend_call(kernel, name, place, operands, results, flops):
    trees, width, length = operands[0].shape
    return pl.pallas_call(
        kernel,
        grid=(trees,),
        out_shape=results,
        in_specs=[pl.BlockSpec(memory_space=pltpu.SMEM)] + [per_tree(value) for value in operands],
        out_specs=tuple(per_tree(value) for value in results),
        compiler_params=pltpu.CompilerParams(vmem_limit_bytes=VMEM_BYTES),
        cost_estimate=pl.CostEstimate(
            flops=flops * trees * width * length * length,
            transcendentals=trees * width * length * length // HEAD_DIM,
            bytes_accessed=16 * trees * width * length,
        ),
        name=name,
    )(place, *operands)


def attend(number, final, place, queries, key_bits, query_bits, pair, state):
    trees, width, length = queries.shape
    heads = width // HEAD_DIM
    row = jax.ShapeDtypeStruct((trees, heads, length), jnp.float32)
    field = jax.ShapeDtypeStruct(queries.shape, jnp.float32)
    results = (row, row, field)
    if final:
        results = (jax.ShapeDtypeStruct(queries.shape, jnp.bfloat16), row) + results
    return attend_call(
        functools.partial(attend_kernel, number, final, heads),
        "attend",
        place,
        (queries, key_bits, query_bits, pair) + tuple(state),
        results,
        16,
    )


def attend_back(number, kind, place, operands):
    trees, width, length = operands[0].shape
    heads = width // HEAD_DIM
    return attend_call(
        functools.partial(attend_back_kernel, number, heads),
        "attend_back",
        place,
        operands,
        (
            jax.ShapeDtypeStruct((trees, width, length), jnp.float32),
            jax.ShapeDtypeStruct((trees, 2 * width, length), kind),
        ),
        40,
    )


def gated_kernel(
    rows_ref, grads_ref, weights_ref, lowered_ref, routed_ref, first_ref, second_ref, active_ref
):
    @pl.when(pl.program_id(0) == 0)
    def _():
        lowered_ref[...] = jnp.zeros_like(lowered_ref)
        routed_ref[...] = jnp.zeros_like(routed_ref)

    def some(index, _):
        part = (pl.ds(pl.multiple_of(index * ROWS, ROWS), ROWS), slice(None))
        rows = rows_ref[part]
        grads = grads_ref[part]
        gate_weights = weights_ref[0, 0]
        up_weights = weights_ref[0, 1]
        down_weights = weights_ref[0, 2]
        first = jnp.dot(rows, gate_weights, preferred_element_type=jnp.float32)
        second = jnp.dot(rows, up_weights, preferred_element_type=jnp.float32)
        sigma = 1.0 / (1.0 + jnp.exp(-first))
        swish = first * sigma
        activated = (swish * second).astype(jnp.bfloat16)
        activated_grad = jnp.dot(grads, down_weights, preferred_element_type=jnp.float32)
        first_grad = (activated_grad * second * (sigma + swish * (1.0 - sigma))).astype(
            jnp.bfloat16
        )
        second_grad = (activated_grad * swish).astype(jnp.bfloat16)
        lowered_ref[part] += contract(activated, down_weights, 1, 1)
        routed_ref[part] += contract(first_grad, gate_weights, 1, 1) + contract(
            second_grad, up_weights, 1, 1
        )
        first_ref[part] = first_grad
        second_ref[part] = second_grad
        active_ref[part] = activated
        return 0

    lax.fori_loop(0, rows_ref.shape[0] // ROWS, some, 0)


def gated(rows, grads, weights, tile):
    count, model_width = rows.shape
    chunks, _, _, hidden = weights.shape
    tiles = hidden // tile
    fixed = pl.BlockSpec((count, model_width), lambda step: (0, 0))
    moving = pl.BlockSpec(
        (1, 3, model_width, tile), lambda step: (step // tiles, 0, 0, step % tiles)
    )
    column = pl.BlockSpec((count, tile), lambda step: (0, step))
    field = jax.ShapeDtypeStruct((count, model_width), jnp.float32)
    wide = jax.ShapeDtypeStruct((count, chunks * hidden), jnp.bfloat16)
    results = pl.pallas_call(
        gated_kernel,
        grid=(chunks * tiles,),
        out_shape=(field, field, wide, wide, wide),
        in_specs=[fixed, fixed, moving],
        out_specs=(fixed, fixed, column, column, column),
        compiler_params=pltpu.CompilerParams(vmem_limit_bytes=VMEM_BYTES),
        cost_estimate=pl.CostEstimate(
            flops=12 * count * model_width * chunks * hidden,
            transcendentals=count * chunks * hidden,
            bytes_accessed=12 * count * model_width + 6 * (count + model_width) * chunks * hidden,
        ),
        name="gated",
    )(rows, grads, weights)
    return (results[0], results[1], results[2:])


def parts_kernel(
    rows_ref, grads_ref, first_ref, second_ref, active_ref, parts_ref, turned_rows, turned_grads
):
    @pl.when(pl.program_id(0) == 0)
    def _():
        turned_rows[...] = rows_ref[...].T
        turned_grads[...] = grads_ref[...].T

    def some(index, _):
        part = (pl.ds(pl.multiple_of(index * ROWS, ROWS), ROWS), slice(None))
        rows = turned_rows[part]
        parts_ref[(0, 0) + part] = contract(rows, first_ref[...], 1, 0).astype(jnp.bfloat16)
        parts_ref[(0, 1) + part] = contract(rows, second_ref[...], 1, 0).astype(jnp.bfloat16)
        parts_ref[(0, 2) + part] = contract(turned_grads[part], active_ref[...], 1, 0).astype(
            jnp.bfloat16
        )
        return 0

    lax.fori_loop(0, turned_rows.shape[0] // ROWS, some, 0)


def weight_parts(rows, grads, wide, chunks, tile):
    count, model_width = rows.shape
    hidden = wide[0].shape[1] // chunks
    tiles = hidden // tile
    fixed = pl.BlockSpec((count, model_width), lambda step: (0, 0))
    column = pl.BlockSpec((count, tile), lambda step: (0, step))
    return pl.pallas_call(
        parts_kernel,
        grid=(chunks * tiles,),
        out_shape=jax.ShapeDtypeStruct((chunks, 3, model_width, hidden), jnp.bfloat16),
        in_specs=[fixed, fixed, column, column, column],
        out_specs=pl.BlockSpec(
            (1, 3, model_width, tile), lambda step: (step // tiles, 0, 0, step % tiles)
        ),
        scratch_shapes=[pltpu.VMEM((model_width, count), jnp.bfloat16)] * 2,
        compiler_params=pltpu.CompilerParams(vmem_limit_bytes=VMEM_BYTES),
        cost_estimate=pl.CostEstimate(
            flops=6 * count * model_width * chunks * hidden,
            transcendentals=0,
            bytes_accessed=4 * count * model_width + 6 * (count + model_width) * chunks * hidden,
        ),
        name="weight_parts",
    )(rows, grads, *wide)


def swap(piece, axes, size, step):
    return lax.ppermute(piece, axes, [(i, i ^ step) for i in range(size)])


def pick(stacked, index):
    return lax.dynamic_index_in_dim(stacked, index, 0, keepdims=False)


def share(piece, axes, size, dim):
    step = size // 2
    while step:
        piece = jnp.concatenate([piece, swap(piece, axes, size, step)], dim)
        step //= 2
    return piece


def reversed_bits(index, size):
    bits = size.bit_length() - 1
    return sum(((index >> bit) & 1) << (bits - 1 - bit) for bit in range(bits))


def tied(*values):
    return lax.optimization_barrier(values)


def route(blocks):
    return lax.all_to_all(blocks, GROUP, split_axis=0, concat_axis=0)


def by_rows(field):
    order = tuple(range(field.ndim))
    return with_layout_constraint(field, Layout(major_to_minor=order))


def turned(field, cosine, sine, backward):
    half = HEAD_DIM // 2
    shape = field.shape
    split = field.reshape(shape[0], -1, 2, half, shape[-1])
    first_half = split[:, :, 0]
    second_half = split[:, :, 1]
    if backward:
        parts = [
            first_half * cosine + second_half * sine,
            second_half * cosine - first_half * sine,
        ]
    else:
        parts = [
            first_half * cosine - second_half * sine,
            second_half * cosine + first_half * sine,
        ]
    return jnp.stack(parts, 2).reshape(shape)


def tree_tables(segments, parents):
    count = parents.shape[1]
    labels = jnp.arange(count, dtype=jnp.int32)
    is_parent = parents[:, :, None] == labels[None, None, :]
    grand = jnp.sum(jnp.where(is_parent, parents[:, None, :], 0), 2)
    itself = labels[None, :, None] == labels[None, None, :]
    table = itself | is_parent | (grand[:, :, None] == labels[None, None, :])
    member = segments[:, None, :] == labels[None, :, None]
    lengths = jnp.sum(member.astype(jnp.int32), 2)
    ahead = jnp.sum(jnp.where(labels[:, None] > labels[None, :], lengths[:, None, :], 0), 2)
    moving = jnp.sum(jnp.where(table, lengths[:, None, :], 0), 2) - lengths - ahead
    place = jnp.arange(segments.shape[1], dtype=jnp.int32) + jnp.sum(
        jnp.where(member, moving[:, :, None], 0), 1
    )
    bits = jnp.sum(jnp.where(table, jnp.left_shift(1, labels)[None, None, :], 0), 2)
    paths = jnp.sum(jnp.where(member, bits[:, :, None], 0), 1)
    return (place, paths, jnp.left_shift(1, segments))


def local_fast(
    tokens,
    cotangent,
    segments,
    parents,
    routes,
    norm_gains,
    project,
    mixing,
    router,
    expander,
    reducer,
    spreader,
    collector,
):
    bf16, f32 = jnp.bfloat16, jnp.float32
    group_size = lax.axis_size(GROUP)
    seq_size = lax.axis_size(SEQ)
    shards = lax.axis_size(TENSOR)
    member_index = lax.axis_index(GROUP)
    seq_index = lax.axis_index(SEQ)
    shard = lax.axis_index(TENSOR)
    trees, rows, model_width = tokens.shape
    part_width = project.shape[2]
    owned = project.shape[1]
    hidden = spreader.shape[2]
    slots = CAP // shards
    quarter = rows // shards
    place_arg = seq_index.astype(jnp.int32).reshape(1)

    extra = EXPERTS + 2
    pad = -extra % 128
    small = jnp.concatenate(
        [
            project[0],
            project[1],
            project[2],
            mixing.T,
            router,
            norm_gains.T,
            jnp.zeros((owned, pad), bf16),
        ],
        1,
    )
    small = lax.all_gather(small, GROUP, axis=0, tiled=True)
    project_all = small[:, : 3 * part_width]
    mixing_own = small[:, 3 * part_width : 4 * part_width].T
    router_all = small[:, 4 * part_width : 4 * part_width + EXPERTS]
    gains = small[:, 4 * part_width + EXPERTS : 4 * part_width + extra].T.astype(f32)
    mixing_all = share(mixing_own, TENSOR, shards, 0)
    labels = jnp.arange(EXPERTS, dtype=jnp.int32)
    named = jnp.any(routes[:, None, :, :] == labels[None, :, None, None], 3)
    earlier = (
        jnp.arange(rows, dtype=jnp.int32)[:, None] < jnp.arange(rows, dtype=jnp.int32)[None, :]
    )
    ranks = jnp.einsum(
        "bes,st->bet", named.astype(bf16), earlier.astype(bf16), preferred_element_type=f32
    ).astype(jnp.int32)
    slot_index = shard * slots + jnp.arange(slots, dtype=jnp.int32)
    chosen = (
        (named[:, :, None, :] & (ranks[:, :, None, :] == slot_index[None, None, :, None]))
        .astype(bf16)
        .reshape(trees, EXPERTS * slots, rows)
    )

    def pick_rows(field):
        picked = jnp.einsum("bst,btd->bsd", chosen, field, preferred_element_type=f32).astype(bf16)
        return picked.reshape(trees, EXPERTS, slots, field.shape[-1]).swapaxes(0, 1)

    def send_rows(picked):
        return route(picked).reshape(EXPERTS * trees * slots, picked.shape[-1])

    def bring_rows(field):
        back = route(field.reshape(EXPERTS, trees, slots, field.shape[-1])).swapaxes(0, 1)
        return back.reshape(trees, EXPERTS * slots, field.shape[-1])

    def combine_rows(chosen, back):
        return by_rows(jnp.einsum("bst,bsd->btd", chosen, back, preferred_element_type=f32))

    place, paths, key_bits = tree_tables(segments, parents)
    offset = seq_index * rows
    own_place = lax.dynamic_slice_in_dim(place, offset, rows, 1).astype(f32)
    own_paths = lax.dynamic_slice_in_dim(paths, offset, rows, 1)
    half = HEAD_DIM // 2
    rates = jnp.exp(-math.log(theta) * 2.0 * jnp.arange(half, dtype=f32) / HEAD_DIM)
    angle = rates[None, :, None] * own_place[:, None, :]
    cosine = jnp.cos(angle)[:, None]
    sine = jnp.sin(angle)[:, None]
    inputs = tokens.astype(f32)
    scale_one = lax.rsqrt(jnp.mean(inputs * inputs, -1, keepdims=True) + epsilon)
    first_in = (inputs * scale_one * gains[0]).astype(bf16)
    mapped = jnp.einsum("dh,btd->bht", project_all, first_in, preferred_element_type=f32)
    queries = (
        turned(mapped[:, :part_width], cosine, sine, False) * HEAD_DIM ** (-0.5)
    ).astype(bf16)
    pairs_own = jnp.concatenate(
        [
            turned(mapped[:, part_width : 2 * part_width], cosine, sine, False).astype(bf16),
            mapped[:, 2 * part_width :].astype(bf16),
        ],
        1,
    )
    key_column = key_bits[:, :, None]
    path_row = own_paths[:, None, :]
    pairs = [pairs_own]
    links = [pairs_own[tree : tree + 1] for tree in range(trees)]
    shared_bundle = jnp.concatenate([spreader, collector.T[None]], 0)
    state = ()
    for number in range(seq_size):
        if number + 1 < seq_size:
            links = [
                lax.ppermute(link, SEQ, [(i, i + 1) for i in range(seq_size - 1)])
                for link in links
            ]
        else:
            picked_cotangent, pairs[-1] = tied(pick_rows(cotangent), pairs[-1])
        state = attend(
            number,
            number == seq_size - 1,
            place_arg,
            queries,
            key_column,
            path_row,
            pairs[number],
            state,
        )
        if number + 1 < seq_size:
            *links, first_state = tied(*links, state[0])
            state = (first_state,) + tuple(state[1:])
            pairs.append(jnp.concatenate(links, 0))
    outs, logs = state[:2]

    bundles = jnp.concatenate([expander, reducer.transpose(0, 2, 1)[:, None]], 1)
    own_expert = route(bundles).swapaxes(0, 1).reshape(3, model_width, hidden)
    expert_weights = lax.all_gather(own_expert, TENSOR, axis=0, tiled=False)
    outs, expert_weights = tied(outs, expert_weights)
    heads = share(outs, TENSOR, shards, 1)
    upstream_rows = send_rows(picked_cotangent)
    heads, upstream_rows = tied(heads, upstream_rows)
    second = inputs + by_rows(
        jnp.einsum("bht,hd->btd", heads, mixing_all, preferred_element_type=f32)
    )

    scale_two = lax.rsqrt(jnp.mean(second * second, -1, keepdims=True) + epsilon)
    hidden_in = (second * scale_two * gains[1]).astype(bf16)
    flat = (trees * rows, model_width)
    flat_hidden = hidden_in.reshape(flat)
    flat_cotangent = cotangent.reshape(flat)
    expert_rows = send_rows(pick_rows(hidden_in))
    expert_rows, shared_bundle = tied(expert_rows, shared_bundle)
    shared_weights = lax.all_gather(
        shared_bundle, GROUP, axis=1, tiled=True
    )
    row_chances = jax.nn.softmax(jnp.dot(expert_rows, router_all, preferred_element_type=f32), -1)
    own_label = jnp.arange(EXPERTS, dtype=jnp.int32) == member_index
    row_gates = jnp.sum(jnp.where(own_label[None], row_chances, 0.0), -1, keepdims=True)
    row_grads = (row_gates * upstream_rows.astype(f32)).astype(bf16)
    lowered, routed_back, expert_wide = gated(expert_rows, row_grads, expert_weights, TILE)
    gate_grads = jnp.sum(upstream_rows.astype(f32) * lowered, -1, keepdims=True)
    lanes = jnp.arange(128, dtype=jnp.int32)[None]
    back_rows = jnp.concatenate(
        [
            routed_back.astype(bf16),
            jnp.where(lanes == member_index, gate_grads, 0.0).astype(bf16),
        ],
        1,
    )
    flat_hidden, row_grads, back_rows = tied(flat_hidden, row_grads, back_rows)
    shared_out, shared_back, shared_wide = gated(
        flat_hidden, flat_cotangent, shared_weights[None], TILE
    )
    expert_parts = weight_parts(expert_rows, row_grads, expert_wide, shards, TILE)
    back_rows = bring_rows(back_rows)
    chosen, shared_back, expert_parts = tied(chosen, shared_back, expert_parts)
    expert_own = lax.psum_scatter(expert_parts, TENSOR, scatter_dimension=0, tiled=False)
    returned_back = combine_rows(chosen, back_rows)
    out_rows = (row_gates * lowered).astype(bf16)
    returned_back, out_rows = tied(returned_back, out_rows)
    shared_parts = weight_parts(flat_hidden, flat_cotangent, shared_wide, 1, TILE)

    def own_rows(field):
        return lax.dynamic_slice_in_dim(field, shard * quarter, quarter, 1)

    def add_shards(field):
        held = field.astype(bf16).reshape(trees, shards, quarter, field.shape[-1])
        step = 1
        while step < shards:
            paired = held.reshape(trees, -1, 2, quarter, field.shape[-1])
            bit = (shard // step) % 2
            kept = lax.dynamic_index_in_dim(paired, bit, 2, keepdims=False)
            sent = lax.dynamic_index_in_dim(paired, 1 - bit, 2, keepdims=False)
            added = kept.astype(f32) + swap(sent, TENSOR, shards, step).astype(f32)
            step *= 2
            held = added.astype(bf16) if step < shards else added
        return held[:, 0]

    def spread_shards(field):
        pieces = share(field[None], TENSOR, shards, 0)
        return jnp.concatenate(
            [pick(pieces, reversed_bits(shard ^ other, shards)) for other in range(shards)], 1
        )

    summed = add_shards(
        returned_back
        + jnp.pad(shared_back.reshape(trees, rows, model_width), ((0, 0), (0, 0), (0, 128)))
    )
    chance_grad = summed[..., model_width : model_width + EXPERTS]
    quarter_second = own_rows(second)
    quarter_scale = own_rows(scale_two)
    quarter_normed = quarter_second * quarter_scale
    quarter_hidden = own_rows(hidden_in)
    logits = jnp.dot(quarter_hidden, router_all, preferred_element_type=f32)
    chances = jax.nn.softmax(logits, -1)
    logit_grad = chances * (chance_grad - jnp.sum(chances * chance_grad, -1, keepdims=True))
    hidden_grad = summed[..., :model_width] + jnp.einsum(
        "bte,de->btd", logit_grad, router_all.astype(f32), precision=highest
    )
    router_part = jnp.einsum(
        "btd,bte->de", quarter_hidden.astype(f32), logit_grad, precision=highest
    )
    gain_two = jnp.sum(hidden_grad * quarter_normed, (0, 1))
    scaled_two = hidden_grad * gains[1]
    second_grad = own_rows(cotangent).astype(f32) + quarter_scale * (
        scaled_two - quarter_normed * jnp.mean(scaled_two * quarter_normed, -1, keepdims=True)
    )
    branch_grad = spread_shards(second_grad.astype(bf16))
    returned_out = combine_rows(chosen, bring_rows(out_rows))
    partial_out = (returned_out + shared_out.reshape(trees, rows, model_width)).astype(bf16)
    branch_grad, partial_out = tied(branch_grad, partial_out)

    heads_grad = jnp.einsum(
        "hd,btd->bht", mixing_own, branch_grad, preferred_element_type=f32
    ).astype(bf16)
    mixing_part = jnp.einsum("btd,bht->dh", branch_grad, outs, preferred_element_type=f32)
    query_grad = ()
    pair_grads = []
    for number in range(seq_size - 1, -1, -1):
        query_grad, pair_grad = attend_back(
            number,
            bf16 if number == seq_size - 1 else f32,
            place_arg,
            (queries, outs, heads_grad, logs, key_column, path_row, pairs[number])
            + ((query_grad,) if pair_grads else ()),
        )
        pair_grads.append(pair_grad)
    blocks = expert_own.reshape(3, group_size, owned, hidden).swapaxes(0, 1)
    first_home = route(blocks[:, :, : owned // 2])
    pair_grad, first_home, shared_parts = tied(pair_grads[0], first_home, shared_parts)
    branches = lax.psum(partial_out, TENSOR)
    shared_grads = lax.psum_scatter(
        shared_parts[0], GROUP, scatter_dimension=1, tiled=True
    ).astype(f32)
    own_grads = []
    for tree in range(trees):
        moving = pair_grad[tree]
        for step, addend in enumerate(pair_grads[1:]):
            moved = lax.ppermute(
                moving.astype(bf16), SEQ, [(i + 1, i) for i in range(seq_size - 1)]
            )
            if tree == trees - 1 and step == seq_size - 2:
                moved, branches = tied(moved, branches)
            moving = addend[tree] + moved.astype(f32)
        own_grads.append(moving)
    pair_grad, blocks = tied(jnp.stack(own_grads), blocks)
    query_grad = query_grad * HEAD_DIM ** (-0.5)
    mapped_grad = jnp.concatenate(
        [
            turned(query_grad, cosine, sine, True),
            turned(pair_grad[:, :part_width], cosine, sine, True),
            pair_grad[:, part_width:],
        ],
        1,
    ).astype(bf16)
    first_part = by_rows(
        jnp.einsum("bht,dh->btd", mapped_grad, project_all, preferred_element_type=f32)
    ).astype(bf16)
    first_part, mapped_grad = tied(first_part, mapped_grad)
    first_grad = add_shards(first_part)
    output = (second + branches.astype(f32)).astype(bf16)
    project_part = by_rows(
        jnp.einsum("btd,bht->dh", first_in, mapped_grad, preferred_element_type=f32)
    )
    quarter_scale_one = own_rows(scale_one)
    quarter_normed_one = own_rows(inputs) * quarter_scale_one
    scaled_one = first_grad * gains[0]
    input_grad = spread_shards(
        (
            second_grad
            + quarter_scale_one
            * (
                scaled_one
                - quarter_normed_one * jnp.mean(scaled_one * quarter_normed_one, -1, keepdims=True)
            )
        ).astype(bf16)
    )

    input_grad, shared_grads = tied(input_grad, shared_grads)
    spreader_grad = shared_grads[:2]
    collector_grad = shared_grads[2].T

    small_parts = jnp.concatenate(
        [
            project_part,
            mixing_part,
            router_part,
            gain_two[:, None],
            jnp.zeros((model_width, -(4 * part_width + EXPERTS + 1) % 128), f32),
        ],
        1,
    ).astype(bf16)
    second_home, small_parts = tied(route(blocks[:, :, owned // 2 :]), small_parts)
    expert_grads = jnp.concatenate([first_home, second_home], 2).astype(f32)
    expander_grad = expert_grads[:, :2]
    reducer_grad = expert_grads[:, 2].transpose(0, 2, 1)
    small_home = route(small_parts.reshape(group_size, owned, -1))
    small_grads = jnp.sum(
        small_home.astype(f32),
        0,
    )
    project_grad = (
        small_grads[:, : 3 * part_width].reshape(owned, 3, part_width).transpose(1, 0, 2)
    )
    mixing_grad = small_grads[:, 3 * part_width : 4 * part_width].T
    rest = small_grads[:, 4 * part_width : 4 * part_width + EXPERTS + 1]
    gain_one = jnp.sum(project_grad * project.astype(f32), (0, 2)) / norm_gains[0].astype(f32)
    tiny = lax.psum(
        jnp.concatenate([rest.T, gain_one[None]], 0),
        TENSOR,
    )
    router_grad = tiny[:EXPERTS].T
    gain_grad = jnp.stack([tiny[EXPERTS + 1], tiny[EXPERTS]])
    return (
        output,
        input_grad,
        gain_grad,
        project_grad,
        mixing_grad,
        router_grad,
        expander_grad,
        reducer_grad,
        spreader_grad,
        collector_grad,
    )


def solution(mesh):
    in_specs = (
        P(DP, SEQ, None),
        P(DP, SEQ, None),
        P(DP, None),
        P(DP, None),
        P(DP, SEQ, None),
        P(None, GROUP),
        P(None, GROUP, TENSOR),
        P(TENSOR, GROUP),
        P(GROUP, None),
        P(None, None, GROUP, TENSOR),
        P(None, TENSOR, GROUP),
        P(None, GROUP, TENSOR),
        P(TENSOR, GROUP),
    )
    out_specs = (
        P(DP, SEQ, None),
        P(DP, SEQ, None),
        P(None, GROUP),
        P(None, GROUP, TENSOR),
        P(TENSOR, GROUP),
        P(GROUP, None),
        P(None, None, GROUP, TENSOR),
        P(None, TENSOR, GROUP),
        P(None, GROUP, TENSOR),
        P(TENSOR, GROUP),
    )
    sizes = mesh.shape
    group_size = sizes[DP] * sizes[SEQ]
    shards = sizes[TENSOR]
    fits = group_size == EXPERTS and shards & (shards - 1) == 0 and CAP % shards == 0
    body = local_fast if fits else local
    return jax.shard_map(body, mesh=mesh, in_specs=in_specs, out_specs=out_specs, check_vma=False)
```

```python
import functools
import math
import types

import jax
import jax.numpy as jnp
from jax import lax
from jax.experimental import pallas as pl
from jax.experimental.layout import Layout, with_layout_constraint
from jax.experimental.pallas import tpu as pltpu
from jax.sharding import PartitionSpec as P

HEAD_DIM = 64
EXPERTS = 8
CAP = 192
QB = 512
DP = "dp"
SEQ = "seq"
TENSOR = "tensor"
GROUP = (DP, SEQ)


epsilon = 1e-05
theta = 10000.0
highest = lax.Precision.HIGHEST


def ancestry(parents):
    labels = jnp.arange(parents.shape[0], dtype=jnp.int32)
    grandparent = jnp.take(parents, parents)
    itself = labels[:, None] == labels[None, :]
    return (
        itself | (parents[:, None] == labels[None, :]) | (grandparent[:, None] == labels[None, :])
    )


def positions(segments, table):
    labels = jnp.arange(table.shape[0], dtype=jnp.int32)
    member = (segments[:, None] == labels[None, :]).astype(jnp.int32)
    lengths = jnp.sum(member, 0)
    offsets = jnp.cumsum(lengths) - lengths
    ancestral = jnp.sum(table.astype(jnp.int32) * lengths[None, :], 1) - lengths
    moving = ancestral - offsets
    return jnp.arange(segments.shape[0], dtype=jnp.int32) + jnp.sum(member * moving[None, :], 1)


def visible(row_segments, row_index, key_segments, key_index, table):
    labels = jnp.arange(table.shape[0], dtype=jnp.int32)
    member_rows = (row_segments[:, None] == labels[None, :]).astype(jnp.bfloat16)
    member_keys = (key_segments[:, None] == labels[None, :]).astype(jnp.bfloat16)
    reach = jnp.dot(member_rows, table.astype(jnp.bfloat16), preferred_element_type=jnp.float32)
    hits = jnp.einsum(
        "bs,ls->bl", reach.astype(jnp.bfloat16), member_keys, preferred_element_type=jnp.float32
    )
    return (hits > 0.5) & (key_index[None, :] <= row_index[:, None])


def turn(field, place, backward):
    half = field.shape[-1] // 2
    rates = jnp.exp(-math.log(theta) * 2.0 * jnp.arange(half, dtype=jnp.float32) / field.shape[-1])
    angle = place[:, None] * rates[None, :]
    cosine = jnp.cos(angle)[:, None, :]
    sine = jnp.sin(angle)[:, None, :]
    first_half = field[..., :half]
    second_half = field[..., half:]
    if backward:
        return jnp.concatenate(
            [first_half * cosine + second_half * sine, second_half * cosine - first_half * sine], -1
        )
    return jnp.concatenate(
        [first_half * cosine - second_half * sine, second_half * cosine + first_half * sine], -1
    )


def slot_of(route_flat):
    labels = jnp.arange(EXPERTS, dtype=jnp.int32)
    member = (route_flat[:, None] == labels[None, :]).astype(jnp.int32)
    ranks = jnp.cumsum(member, 0) - 1
    return route_flat * CAP + jnp.sum(ranks * member, 1)


def owner_of(slot_ids, count_rows, per_row):
    picked = jnp.arange(slot_ids.shape[0], dtype=jnp.int32) // per_row
    return jnp.full((EXPERTS * CAP,), count_rows, jnp.int32).at[slot_ids].set(picked)


def silu_slope(value):
    sigma = jax.nn.sigmoid(value)
    return sigma * (1.0 + value * (1.0 - sigma))


def block_scores(query_block, key_block, seg_block, index_block, key_segments, key_index, table):
    seen = visible(seg_block, index_block, key_segments, key_index, table)
    raw = jnp.einsum("bhd,lhd->hbl", query_block, key_block, preferred_element_type=jnp.float32)
    return jnp.where(seen[None], raw * HEAD_DIM ** (-0.5), -1e30)


def fetch(norm_gains, project, mixing, router, expander, reducer, spreader, collector):
    return (
        lax.all_gather(norm_gains, GROUP, axis=1, tiled=True),
        lax.all_gather(project, GROUP, axis=1, tiled=True),
        lax.all_gather(mixing, GROUP, axis=1, tiled=True),
        lax.all_gather(router, GROUP, axis=0, tiled=True),
        lax.all_gather(expander, GROUP, axis=2, tiled=True),
        lax.all_gather(reducer, GROUP, axis=2, tiled=True),
        lax.all_gather(spreader, GROUP, axis=1, tiled=True),
        lax.all_gather(collector, GROUP, axis=1, tiled=True),
    )


def reduce_end(grads):
    (
        gain_part,
        project_part,
        mixing_part,
        router_part,
        expander_part,
        reducer_part,
        spreader_part,
        collector_part,
    ) = grads
    return (
        lax.psum_scatter(gain_part, GROUP, scatter_dimension=1, tiled=True),
        lax.psum_scatter(project_part, GROUP, scatter_dimension=1, tiled=True),
        lax.psum_scatter(mixing_part, GROUP, scatter_dimension=1, tiled=True),
        lax.psum_scatter(router_part, GROUP, scatter_dimension=0, tiled=True),
        lax.psum_scatter(expander_part, GROUP, scatter_dimension=2, tiled=True),
        lax.psum_scatter(reducer_part, GROUP, scatter_dimension=2, tiled=True),
        lax.psum_scatter(spreader_part, GROUP, scatter_dimension=1, tiled=True),
        lax.psum_scatter(collector_part, GROUP, scatter_dimension=1, tiled=True),
    )


def forward_pass(tree_tokens, tree_segments, tree_parents, tree_routes, weights, offset):
    norm_gains, project, mixing, router, expander, reducer, spreader, collector = weights
    row_count = tree_tokens.shape[0]
    model_width = tree_tokens.shape[1]
    tree_length = tree_segments.shape[0]
    local_heads = project.shape[2] // HEAD_DIM
    table = ancestry(tree_parents)
    place = lax.dynamic_slice_in_dim(positions(tree_segments, table), offset, row_count).astype(
        jnp.float32
    )
    row_segments = lax.dynamic_slice_in_dim(tree_segments, offset, row_count)
    row_index = offset + jnp.arange(row_count, dtype=jnp.int32)
    key_index = jnp.arange(tree_length, dtype=jnp.int32)
    inputs = tree_tokens.astype(jnp.float32)
    scale_one = lax.rsqrt(jnp.mean(inputs * inputs, -1, keepdims=True) + epsilon)
    normed_one = inputs * scale_one
    first_in = (normed_one * norm_gains[0].astype(jnp.float32)).astype(jnp.bfloat16)
    mapped = jnp.einsum("td,cdh->cth", first_in, project, preferred_element_type=jnp.float32)
    head_shape = (row_count, local_heads, HEAD_DIM)
    queries = turn(mapped[0].reshape(head_shape), place, False).astype(jnp.bfloat16)
    keys_own = (
        turn(mapped[1].reshape(head_shape), place, False)
        .astype(jnp.bfloat16)
        .reshape(row_count, -1)
    )
    values_own = mapped[2].astype(jnp.bfloat16)
    keys_flat, values_flat = (
        lax.all_gather(keys_own, SEQ, axis=0, tiled=True),
        lax.all_gather(values_own, SEQ, axis=0, tiled=True),
    )
    keys_all = keys_flat.reshape(tree_length, local_heads, HEAD_DIM)
    values_all = values_flat.reshape(tree_length, local_heads, HEAD_DIM)
    blocks = row_count // QB
    query_blocks = queries.reshape(blocks, QB, local_heads, HEAD_DIM)
    seg_blocks = row_segments.reshape(blocks, QB)
    index_blocks = row_index.reshape(blocks, QB)

    def attend(entries):
        query_block, seg_block, index_block = entries
        scores = block_scores(
            query_block, keys_all, seg_block, index_block, tree_segments, key_index, table
        )
        row_peak = jnp.max(scores, -1, keepdims=True)
        expo = jnp.exp(scores - row_peak)
        row_total = jnp.sum(expo, -1, keepdims=True)
        chances_soft = expo / row_total
        mixed_block = jnp.einsum(
            "hbl,lhd->bhd",
            chances_soft.astype(jnp.bfloat16),
            values_all,
            preferred_element_type=jnp.float32,
        )
        return (mixed_block, (row_peak + jnp.log(row_total))[..., 0])

    mixed, log_totals = lax.map(attend, (query_blocks, seg_blocks, index_blocks))
    heads_out = mixed.reshape(row_count, -1).astype(jnp.bfloat16)
    attended = lax.psum(
        jnp.dot(heads_out, mixing, preferred_element_type=jnp.float32).astype(jnp.bfloat16),
        TENSOR,
    ).astype(jnp.float32)
    second = inputs + attended
    scale_two = lax.rsqrt(jnp.mean(second * second, -1, keepdims=True) + epsilon)
    normed_two = second * scale_two
    hidden_in = (normed_two * norm_gains[1].astype(jnp.float32)).astype(jnp.bfloat16)
    logits = jnp.dot(hidden_in, router, preferred_element_type=jnp.float32)
    shifted = jnp.exp(logits - jnp.max(logits, -1, keepdims=True))
    chances = shifted / jnp.sum(shifted, -1, keepdims=True)
    picks = (tree_routes[:, :, None] == jnp.arange(EXPERTS, dtype=jnp.int32)[None, None, :]).astype(
        jnp.float32
    )
    gates = jnp.sum(picks * chances[:, None, :], -1)
    per_row = tree_routes.shape[1]
    slot_ids = slot_of(tree_routes.reshape(-1))
    owners = owner_of(slot_ids, row_count, per_row)
    padded = jnp.concatenate([hidden_in, jnp.zeros((1, model_width), jnp.bfloat16)], 0)
    routed = jnp.take(padded, owners, axis=0).reshape(EXPERTS, CAP, model_width)
    raised = jnp.einsum("ecd,egdf->gecf", routed, expander, preferred_element_type=jnp.float32)
    activated = (jax.nn.silu(raised[0]) * raised[1]).astype(jnp.bfloat16)
    lowered = jnp.einsum(
        "ecf,efd->ecd", activated, reducer, preferred_element_type=jnp.float32
    ).reshape(EXPERTS * CAP, model_width)
    returned = jnp.take(lowered, slot_ids, axis=0).reshape(row_count, per_row, model_width)
    blended = jnp.sum(gates[:, :, None] * returned, 1)
    spread = jnp.einsum("td,gdf->gtf", hidden_in, spreader, preferred_element_type=jnp.float32)
    common = (jax.nn.silu(spread[0]) * spread[1]).astype(jnp.bfloat16)
    shared_out = jnp.dot(common, collector, preferred_element_type=jnp.float32)
    branches = lax.psum((blended + shared_out).astype(jnp.bfloat16), TENSOR).astype(jnp.float32)
    output_tree = (second + branches).astype(jnp.bfloat16)
    kept = types.SimpleNamespace(
        table=table,
        place=place,
        offset=offset,
        row_segments=row_segments,
        seg_blocks=seg_blocks,
        index_blocks=index_blocks,
        scale_one=scale_one,
        normed_one=normed_one,
        first_in=first_in,
        queries=queries,
        query_blocks=query_blocks,
        keys_all=keys_all,
        values_all=values_all,
        log_totals=log_totals,
        heads_out=heads_out,
        scale_two=scale_two,
        normed_two=normed_two,
        hidden_in=hidden_in,
        chances=chances,
        picks=picks,
        gates=gates,
        slot_ids=slot_ids,
        routed=routed,
        raised=raised,
        activated=activated,
        returned=returned,
        spread=spread,
        common=common,
    )
    return (kept, output_tree)


def backward_pass(tree_cot, tree_segments, kept, weights):
    norm_gains, project, mixing, router, expander, reducer, spreader, collector = weights
    upstream = tree_cot.astype(jnp.float32)
    row_count = upstream.shape[0]
    model_width = upstream.shape[1]
    shared_grad = upstream.astype(jnp.bfloat16)
    common_grad = jnp.einsum(
        "td,fd->tf", shared_grad, collector, preferred_element_type=jnp.float32
    )
    collector_part = jnp.einsum(
        "tf,td->fd", kept.common, shared_grad, preferred_element_type=jnp.float32
    )
    spread = kept.spread
    spread_grad = jnp.stack(
        [common_grad * spread[1] * silu_slope(spread[0]), common_grad * jax.nn.silu(spread[0])]
    ).astype(jnp.bfloat16)
    spreader_part = jnp.einsum(
        "td,gtf->gdf", kept.hidden_in, spread_grad, preferred_element_type=jnp.float32
    )
    hidden_grad = jnp.einsum(
        "gtf,gdf->td", spread_grad, spreader, preferred_element_type=jnp.float32
    )
    gates = kept.gates
    slot_ids = kept.slot_ids
    per_row = gates.shape[1]
    pair_grad = (
        (gates[:, :, None] * upstream[:, None, :])
        .astype(jnp.bfloat16)
        .reshape(row_count * per_row, model_width)
    )
    lowered_grad = (
        jnp.zeros((EXPERTS * CAP, model_width), jnp.bfloat16)
        .at[slot_ids]
        .set(pair_grad)
        .reshape(EXPERTS, CAP, model_width)
    )
    activated_grad = jnp.einsum(
        "ecd,efd->ecf", lowered_grad, reducer, preferred_element_type=jnp.float32
    )
    reducer_part = jnp.einsum(
        "ecf,ecd->efd", kept.activated, lowered_grad, preferred_element_type=jnp.float32
    )
    raised = kept.raised
    raised_grad = jnp.stack(
        [
            activated_grad * raised[1] * silu_slope(raised[0]),
            activated_grad * jax.nn.silu(raised[0]),
        ]
    ).astype(jnp.bfloat16)
    expander_part = jnp.einsum(
        "ecd,gecf->egdf", kept.routed, raised_grad, preferred_element_type=jnp.float32
    )
    routed_grad = jnp.einsum(
        "gecf,egdf->ecd", raised_grad, expander, preferred_element_type=jnp.float32
    ).reshape(EXPERTS * CAP, model_width)
    hidden_grad = hidden_grad + jnp.sum(
        jnp.take(routed_grad, slot_ids, axis=0).reshape(row_count, per_row, model_width), 1
    )
    gate_grad = jnp.sum(upstream[:, None, :] * kept.returned, -1)
    hidden_grad, gate_grad = (
        lax.psum(hidden_grad.astype(jnp.bfloat16), TENSOR).astype(jnp.float32),
        lax.psum(gate_grad.astype(jnp.bfloat16), TENSOR).astype(jnp.float32),
    )
    chances = kept.chances
    chance_grad = jnp.sum(kept.picks * gate_grad[:, :, None], 1)
    logit_grad = chances * (chance_grad - jnp.sum(chances * chance_grad, -1, keepdims=True))
    hidden_grad = hidden_grad + jnp.dot(logit_grad, router.astype(jnp.float32).T, precision=highest)
    router_part = jnp.dot(kept.hidden_in.astype(jnp.float32).T, logit_grad, precision=highest)
    normed_two = kept.normed_two
    gain_two = jnp.sum(hidden_grad * normed_two, 0)
    scaled_two = hidden_grad * norm_gains[1].astype(jnp.float32)
    second_grad = upstream + kept.scale_two * (
        scaled_two - normed_two * jnp.mean(scaled_two * normed_two, -1, keepdims=True)
    )
    branch_grad = second_grad.astype(jnp.bfloat16)
    mixing_part = jnp.einsum(
        "th,td->hd", kept.heads_out, branch_grad, preferred_element_type=jnp.float32
    )
    heads_grad = jnp.einsum(
        "td,hd->th", branch_grad, mixing, preferred_element_type=jnp.float32
    ).astype(jnp.bfloat16)
    keys_all = kept.keys_all
    values_all = kept.values_all
    table = kept.table
    query_blocks = kept.query_blocks
    tree_length = keys_all.shape[0]
    local_heads = keys_all.shape[1]
    key_index = jnp.arange(tree_length, dtype=jnp.int32)
    grad_blocks = heads_grad.reshape(query_blocks.shape)
    factor = HEAD_DIM ** (-0.5)

    def attend_back(carry, entries):
        keys_grad, values_grad = carry
        query_block, grad_block, log_block, seg_block, index_block = entries
        scores = block_scores(
            query_block, keys_all, seg_block, index_block, tree_segments, key_index, table
        )
        chances_soft = jnp.exp(scores - log_block[..., None])
        prob_grad = jnp.einsum(
            "bhd,lhd->hbl", grad_block, values_all, preferred_element_type=jnp.float32
        )
        centre = jnp.sum(chances_soft * prob_grad, -1, keepdims=True)
        score_grad = (chances_soft * (prob_grad - centre) * factor).astype(jnp.bfloat16)
        query_grad_block = jnp.einsum(
            "hbl,lhd->bhd", score_grad, keys_all, preferred_element_type=jnp.float32
        )
        keys_grad = keys_grad + jnp.einsum(
            "hbl,bhd->lhd", score_grad, query_block, preferred_element_type=jnp.float32
        )
        values_grad = values_grad + jnp.einsum(
            "hbl,bhd->lhd",
            chances_soft.astype(jnp.bfloat16),
            grad_block,
            preferred_element_type=jnp.float32,
        )
        return ((keys_grad, values_grad), query_grad_block)

    zero_kv = jnp.zeros((tree_length, local_heads, HEAD_DIM), jnp.float32)
    (keys_grad, values_grad), query_grad = lax.scan(
        attend_back,
        (zero_kv, zero_kv),
        (query_blocks, grad_blocks, kept.log_totals, kept.seg_blocks, kept.index_blocks),
    )
    keys_own_grad, values_own_grad = (
        lax.psum_scatter(
            keys_grad.reshape(tree_length, -1).astype(jnp.bfloat16),
            SEQ,
            scatter_dimension=0,
            tiled=True,
        ).astype(jnp.float32),
        lax.psum_scatter(
            values_grad.reshape(tree_length, -1).astype(jnp.bfloat16),
            SEQ,
            scatter_dimension=0,
            tiled=True,
        ).astype(jnp.float32),
    )
    place = kept.place
    query_back = turn(query_grad.reshape(row_count, local_heads, HEAD_DIM), place, True).reshape(
        row_count, -1
    )
    key_back = turn(keys_own_grad.reshape(row_count, local_heads, HEAD_DIM), place, True).reshape(
        row_count, -1
    )
    mapped_grad = jnp.stack([query_back, key_back, values_own_grad]).astype(jnp.bfloat16)
    project_part = jnp.einsum(
        "td,cth->cdh", kept.first_in, mapped_grad, preferred_element_type=jnp.float32
    )
    first_grad = lax.psum(
        jnp.einsum("cth,cdh->td", mapped_grad, project, preferred_element_type=jnp.float32).astype(
            jnp.bfloat16
        ),
        TENSOR,
    ).astype(jnp.float32)
    normed_one = kept.normed_one
    gain_one = jnp.sum(first_grad * normed_one, 0)
    scaled_one = first_grad * norm_gains[0].astype(jnp.float32)
    input_tree = (
        second_grad
        + kept.scale_one
        * (scaled_one - normed_one * jnp.mean(scaled_one * normed_one, -1, keepdims=True))
    ).astype(jnp.bfloat16)
    gain_part = jnp.stack([gain_one, gain_two])
    return (
        input_tree,
        (
            gain_part,
            project_part,
            mixing_part,
            router_part,
            expander_part,
            reducer_part,
            spreader_part,
            collector_part,
        ),
    )


def local(
    tokens,
    cotangent,
    segments,
    parents,
    routes,
    norm_gains,
    project,
    mixing,
    router,
    expander,
    reducer,
    spreader,
    collector,
):
    tree_count = tokens.shape[0]
    offset = lax.axis_index(SEQ) * tokens.shape[1]
    outputs = []
    input_grads = []
    running = None
    for tree_index in range(tree_count):
        forward_weights = fetch(
            norm_gains, project, mixing, router, expander, reducer, spreader, collector
        )
        kept, output_tree = forward_pass(
            tokens[tree_index],
            segments[tree_index],
            parents[tree_index],
            routes[tree_index],
            forward_weights,
            offset,
        )
        backward_weights = fetch(
            norm_gains, project, mixing, router, expander, reducer, spreader, collector
        )
        input_tree, tree_grads = backward_pass(
            cotangent[tree_index], segments[tree_index], kept, backward_weights
        )
        outputs.append(output_tree)
        input_grads.append(input_tree)
        if running is None:
            running = tree_grads
        else:
            running = tuple((before + addend for before, addend in zip(running, tree_grads)))
    running = reduce_end(running)
    return (
        jnp.stack(outputs),
        jnp.stack(input_grads),
        running[0],
        running[1],
        running[2],
        running[3],
        running[4],
        running[5],
        running[6],
        running[7],
    )


VMEM_BYTES = 56 << 20
TILE = 256
ROWS = 256


def contract(left, right, left_dim, right_dim):
    return lax.dot_general(
        left, right, (((left_dim,), (right_dim,)), ((), ())), preferred_element_type=jnp.float32
    )


def spans(head, width):
    if isinstance(head, int):
        start = head * HEAD_DIM
    else:
        start = pl.multiple_of(head * HEAD_DIM, HEAD_DIM)
    return (pl.ds(start, HEAD_DIM), pl.ds(width + start, HEAD_DIM), pl.ds(head, 1))


def scores_of(keys, queries, seen):
    return jnp.where(seen, contract(keys, queries, 0, 0), -1e30)


def seen_block(number, place_ref, key_bits_ref, query_bits, length):
    start = pl.multiple_of((place_ref[0] - number) * length, length)
    seen = (key_bits_ref[pl.ds(start, length), :] & query_bits) != 0
    if number == 0:
        keys = lax.broadcasted_iota(jnp.int32, seen.shape, 0)
        rows = lax.broadcasted_iota(jnp.int32, seen.shape, 1)
        seen = seen & (keys <= rows)
    return seen


def attend_kernel(number, final, heads, place_ref, query_ref, key_bits_ref, query_bits_ref, *refs):
    pair_ref = refs[0]
    if number:
        old_peak_ref, old_total_ref, old_mixed_ref = refs[1:4]
    peak_ref, total_ref, mixed_ref = refs[-3:]
    length = query_ref.shape[1]
    width = heads * HEAD_DIM

    def block():
        seen = seen_block(number, place_ref, key_bits_ref, query_bits_ref[...], length)

        def one(head, _):
            span, value_span, row = spans(head, width)
            scores = scores_of(pair_ref[span, :], query_ref[span, :], seen)
            peak = jnp.max(scores, 0, keepdims=True)
            if number:
                before = old_peak_ref[row, :]
                peak = jnp.maximum(before, peak)
                shrink = jnp.exp(before - peak)
            expo = jnp.exp(scores - peak)
            total = jnp.sum(expo, 0, keepdims=True)
            mixed = jnp.dot(
                pair_ref[value_span, :],
                expo.astype(jnp.bfloat16),
                preferred_element_type=jnp.float32,
            )
            if number:
                total = total + shrink * old_total_ref[row, :]
                mixed = mixed + shrink * old_mixed_ref[span, :]
            peak_ref[row, :] = peak
            total_ref[row, :] = total
            mixed_ref[span, :] = mixed
            return 0

        lax.fori_loop(0, heads, one, 0)

    def keep():
        peak_ref[...] = old_peak_ref[...]
        total_ref[...] = old_total_ref[...]
        mixed_ref[...] = old_mixed_ref[...]

    if number:
        pl.when(place_ref[0] >= number)(block)
        pl.when(place_ref[0] < number)(keep)
    else:
        block()
    if final:
        out_ref, log_ref = refs[4:6]
        for head in range(heads):
            span, _, row = spans(head, width)
            out_ref[span, :] = (mixed_ref[span, :] / total_ref[row, :]).astype(out_ref.dtype)
            log_ref[row, :] = peak_ref[row, :] + jnp.log(total_ref[row, :])


def attend_back_kernel(
    number,
    heads,
    place_ref,
    query_ref,
    out_ref,
    grad_ref,
    log_ref,
    key_bits_ref,
    query_bits_ref,
    pair_ref,
    *refs
):
    query_grad_ref, pair_grad_ref = refs[-2:]
    length = query_ref.shape[1]
    width = heads * HEAD_DIM

    def block():
        seen = seen_block(number, place_ref, key_bits_ref, query_bits_ref[...], length)

        def one(head, _):
            span, value_span, row = spans(head, width)
            queries = query_ref[span, :]
            grads = grad_ref[span, :]
            keys = pair_ref[span, :]
            centre = jnp.sum(
                grads.astype(jnp.float32) * out_ref[span, :].astype(jnp.float32), 0, keepdims=True
            )
            chances = jnp.exp(scores_of(keys, queries, seen) - log_ref[row, :])
            prob_grad = contract(pair_ref[value_span, :], grads, 0, 0)
            score_grad = (chances * (prob_grad - centre)).astype(jnp.bfloat16)
            value_grad = contract(grads, chances.astype(jnp.bfloat16), 1, 1)
            key_grad = contract(queries, score_grad, 1, 1)
            query_grad = jnp.dot(keys, score_grad, preferred_element_type=jnp.float32)
            pair_grad_ref[span, :] = key_grad.astype(pair_grad_ref.dtype)
            pair_grad_ref[value_span, :] = value_grad.astype(pair_grad_ref.dtype)
            if len(refs) > 2:
                query_grad = query_grad + refs[0][span, :]
            query_grad_ref[span, :] = query_grad
            return 0

        lax.fori_loop(0, heads, one, 0)

    def empty():
        pair_grad_ref[...] = jnp.zeros_like(pair_grad_ref)
        if len(refs) > 2:
            query_grad_ref[...] = refs[0][...]
        else:
            query_grad_ref[...] = jnp.zeros_like(query_grad_ref)

    if number:
        pl.when(place_ref[0] >= number)(block)
        pl.when(place_ref[0] < number)(empty)
    else:
        block()


def per_tree(array):
    return pl.BlockSpec((None,) + array.shape[1:], lambda tree: (tree, 0, 0))


def attend_call(kernel, name, place, operands, results, flops):
    trees, width, length = operands[0].shape
    return pl.pallas_call(
        kernel,
        grid=(trees,),
        out_shape=results,
        in_specs=[pl.BlockSpec(memory_space=pltpu.SMEM)] + [per_tree(value) for value in operands],
        out_specs=tuple(per_tree(value) for value in results),
        compiler_params=pltpu.CompilerParams(vmem_limit_bytes=VMEM_BYTES),
        cost_estimate=pl.CostEstimate(
            flops=flops * trees * width * length * length,
            transcendentals=trees * width * length * length // HEAD_DIM,
            bytes_accessed=16 * trees * width * length,
        ),
        name=name,
    )(place, *operands)


def attend(number, final, place, queries, key_bits, query_bits, pair, state):
    trees, width, length = queries.shape
    heads = width // HEAD_DIM
    row = jax.ShapeDtypeStruct((trees, heads, length), jnp.float32)
    field = jax.ShapeDtypeStruct(queries.shape, jnp.float32)
    results = (row, row, field)
    if final:
        results = (jax.ShapeDtypeStruct(queries.shape, jnp.bfloat16), row) + results
    return attend_call(
        functools.partial(attend_kernel, number, final, heads),
        "attend",
        place,
        (queries, key_bits, query_bits, pair) + tuple(state),
        results,
        16,
    )


def attend_back(number, kind, place, operands):
    trees, width, length = operands[0].shape
    heads = width // HEAD_DIM
    return attend_call(
        functools.partial(attend_back_kernel, number, heads),
        "attend_back",
        place,
        operands,
        (
            jax.ShapeDtypeStruct((trees, width, length), jnp.float32),
            jax.ShapeDtypeStruct((trees, 2 * width, length), kind),
        ),
        40,
    )


def gated_kernel(
    rows_ref, grads_ref, weights_ref, lowered_ref, routed_ref, first_ref, second_ref, active_ref
):
    @pl.when(pl.program_id(0) == 0)
    def _():
        lowered_ref[...] = jnp.zeros_like(lowered_ref)
        routed_ref[...] = jnp.zeros_like(routed_ref)

    def some(index, _):
        part = (pl.ds(pl.multiple_of(index * ROWS, ROWS), ROWS), slice(None))
        rows = rows_ref[part]
        grads = grads_ref[part]
        gate_weights = weights_ref[0, 0]
        up_weights = weights_ref[0, 1]
        down_weights = weights_ref[0, 2]
        first = jnp.dot(rows, gate_weights, preferred_element_type=jnp.float32)
        second = jnp.dot(rows, up_weights, preferred_element_type=jnp.float32)
        sigma = 1.0 / (1.0 + jnp.exp(-first))
        swish = first * sigma
        activated = (swish * second).astype(jnp.bfloat16)
        activated_grad = jnp.dot(grads, down_weights, preferred_element_type=jnp.float32)
        first_grad = (activated_grad * second * (sigma + swish * (1.0 - sigma))).astype(
            jnp.bfloat16
        )
        second_grad = (activated_grad * swish).astype(jnp.bfloat16)
        lowered_ref[part] += contract(activated, down_weights, 1, 1)
        routed_ref[part] += contract(first_grad, gate_weights, 1, 1) + contract(
            second_grad, up_weights, 1, 1
        )
        first_ref[part] = first_grad
        second_ref[part] = second_grad
        active_ref[part] = activated
        return 0

    lax.fori_loop(0, rows_ref.shape[0] // ROWS, some, 0)


def gated(rows, grads, weights, tile):
    count, model_width = rows.shape
    chunks, _, _, hidden = weights.shape
    tiles = hidden // tile
    fixed = pl.BlockSpec((count, model_width), lambda step: (0, 0))
    moving = pl.BlockSpec(
        (1, 3, model_width, tile), lambda step: (step // tiles, 0, 0, step % tiles)
    )
    column = pl.BlockSpec((count, tile), lambda step: (0, step))
    field = jax.ShapeDtypeStruct((count, model_width), jnp.float32)
    wide = jax.ShapeDtypeStruct((count, chunks * hidden), jnp.bfloat16)
    results = pl.pallas_call(
        gated_kernel,
        grid=(chunks * tiles,),
        out_shape=(field, field, wide, wide, wide),
        in_specs=[fixed, fixed, moving],
        out_specs=(fixed, fixed, column, column, column),
        compiler_params=pltpu.CompilerParams(vmem_limit_bytes=VMEM_BYTES),
        cost_estimate=pl.CostEstimate(
            flops=12 * count * model_width * chunks * hidden,
            transcendentals=count * chunks * hidden,
            bytes_accessed=12 * count * model_width + 6 * (count + model_width) * chunks * hidden,
        ),
        name="gated",
    )(rows, grads, weights)
    return (results[0], results[1], results[2:])


def parts_kernel(
    rows_ref, grads_ref, first_ref, second_ref, active_ref, parts_ref, turned_rows, turned_grads
):
    owned = parts_ref.shape[3]

    @pl.when(pl.program_id(0) == 0)
    def _():
        turned_rows[...] = rows_ref[...].T
        turned_grads[...] = grads_ref[...].T

    def some(index, _):
        part = (pl.ds(pl.multiple_of(index * 2 * owned, 2 * owned), 2 * owned), slice(None))
        rows = turned_rows[part]
        results = (
            contract(rows, first_ref[...], 1, 0),
            contract(rows, second_ref[...], 1, 0),
            contract(turned_grads[part], active_ref[...], 1, 0),
        )
        for kind, result in enumerate(results):
            for half in range(2):
                piece = result[half * owned : (half + 1) * owned]
                parts_ref[0, 2 * index + half, kind] = piece.astype(jnp.bfloat16)
        return 0

    lax.fori_loop(0, parts_ref.shape[1] // 2, some, 0)


def weight_parts(rows, grads, wide, chunks, owners, tile):
    count, model_width = rows.shape
    hidden = wide[0].shape[1] // chunks
    tiles = hidden // tile
    owned = model_width // owners
    fixed = pl.BlockSpec((count, model_width), lambda step: (0, 0))
    column = pl.BlockSpec((count, tile), lambda step: (0, step))
    return pl.pallas_call(
        parts_kernel,
        grid=(chunks * tiles,),
        out_shape=jax.ShapeDtypeStruct((chunks, owners, 3, owned, hidden), jnp.bfloat16),
        in_specs=[fixed, fixed, column, column, column],
        out_specs=pl.BlockSpec(
            (1, owners, 3, owned, tile), lambda step: (step // tiles, 0, 0, 0, step % tiles)
        ),
        scratch_shapes=[pltpu.VMEM((model_width, count), jnp.bfloat16)] * 2,
        compiler_params=pltpu.CompilerParams(vmem_limit_bytes=VMEM_BYTES),
        cost_estimate=pl.CostEstimate(
            flops=6 * count * model_width * chunks * hidden,
            transcendentals=0,
            bytes_accessed=4 * count * model_width + 6 * (count + model_width) * chunks * hidden,
        ),
        name="weight_parts",
    )(rows, grads, *wide)


def swap(piece, axes, size, step):
    return lax.ppermute(piece, axes, [(i, i ^ step) for i in range(size)])


def pick(stacked, index):
    return lax.dynamic_index_in_dim(stacked, index, 0, keepdims=False)


def share(piece, axes, size, dim):
    step = size // 2
    while step:
        piece = jnp.concatenate([piece, swap(piece, axes, size, step)], dim)
        step //= 2
    return piece


def reversed_bits(index, size):
    bits = size.bit_length() - 1
    return sum(((index >> bit) & 1) << (bits - 1 - bit) for bit in range(bits))


def tied(*values):
    return lax.optimization_barrier(values)


def route(blocks):
    return lax.all_to_all(blocks, GROUP, split_axis=0, concat_axis=0)


def by_rows(field):
    order = tuple(range(field.ndim))
    return with_layout_constraint(field, Layout(major_to_minor=order))


def turned(field, cosine, sine, backward):
    half = HEAD_DIM // 2
    shape = field.shape
    split = field.reshape(shape[0], -1, 2, half, shape[-1])
    first_half = split[:, :, 0]
    second_half = split[:, :, 1]
    if backward:
        parts = [
            first_half * cosine + second_half * sine,
            second_half * cosine - first_half * sine,
        ]
    else:
        parts = [
            first_half * cosine - second_half * sine,
            second_half * cosine + first_half * sine,
        ]
    return jnp.stack(parts, 2).reshape(shape)


def tree_tables(segments, parents):
    count = parents.shape[1]
    labels = jnp.arange(count, dtype=jnp.int32)
    is_parent = parents[:, :, None] == labels[None, None, :]
    grand = jnp.sum(jnp.where(is_parent, parents[:, None, :], 0), 2)
    itself = labels[None, :, None] == labels[None, None, :]
    table = itself | is_parent | (grand[:, :, None] == labels[None, None, :])
    member = segments[:, None, :] == labels[None, :, None]
    lengths = jnp.sum(member.astype(jnp.int32), 2)
    ahead = jnp.sum(jnp.where(labels[:, None] > labels[None, :], lengths[:, None, :], 0), 2)
    moving = jnp.sum(jnp.where(table, lengths[:, None, :], 0), 2) - lengths - ahead
    place = jnp.arange(segments.shape[1], dtype=jnp.int32) + jnp.sum(
        jnp.where(member, moving[:, :, None], 0), 1
    )
    bits = jnp.sum(jnp.where(table, jnp.left_shift(1, labels)[None, None, :], 0), 2)
    paths = jnp.sum(jnp.where(member, bits[:, :, None], 0), 1)
    return (place, paths, jnp.left_shift(1, segments))


def local_fast(
    tokens,
    cotangent,
    segments,
    parents,
    routes,
    norm_gains,
    project,
    mixing,
    router,
    expander,
    reducer,
    spreader,
    collector,
):
    bf16, f32 = jnp.bfloat16, jnp.float32
    group_size = lax.axis_size(GROUP)
    seq_size = lax.axis_size(SEQ)
    shards = lax.axis_size(TENSOR)
    member_index = lax.axis_index(GROUP)
    seq_index = lax.axis_index(SEQ)
    shard = lax.axis_index(TENSOR)
    trees, rows, model_width = tokens.shape
    part_width = project.shape[2]
    owned = project.shape[1]
    hidden = spreader.shape[2]
    slots = CAP // shards
    quarter = rows // shards
    place_arg = seq_index.astype(jnp.int32).reshape(1)

    extra = EXPERTS + 2
    pad = -extra % 128
    small = jnp.concatenate(
        [
            project[0],
            project[1],
            project[2],
            mixing.T,
            router,
            norm_gains.T,
            jnp.zeros((owned, pad), bf16),
        ],
        1,
    )
    small = lax.all_gather(small, GROUP, axis=0, tiled=True)
    project_all = small[:, : 3 * part_width]
    mixing_own = small[:, 3 * part_width : 4 * part_width].T
    router_all = small[:, 4 * part_width : 4 * part_width + EXPERTS]
    gains = small[:, 4 * part_width + EXPERTS : 4 * part_width + extra].T.astype(f32)
    mixing_all = share(mixing_own, TENSOR, shards, 0)
    labels = jnp.arange(EXPERTS, dtype=jnp.int32)
    named = jnp.any(routes[:, None, :, :] == labels[None, :, None, None], 3)
    earlier = (
        jnp.arange(rows, dtype=jnp.int32)[:, None] < jnp.arange(rows, dtype=jnp.int32)[None, :]
    )
    ranks = jnp.einsum(
        "bes,st->bet", named.astype(bf16), earlier.astype(bf16), preferred_element_type=f32
    ).astype(jnp.int32)
    slot_index = shard * slots + jnp.arange(slots, dtype=jnp.int32)
    chosen = (
        (named[:, :, None, :] & (ranks[:, :, None, :] == slot_index[None, None, :, None]))
        .astype(bf16)
        .reshape(trees, EXPERTS * slots, rows)
    )

    def pick_rows(field):
        picked = jnp.einsum("bst,btd->bsd", chosen, field, preferred_element_type=f32).astype(bf16)
        return picked.reshape(trees, EXPERTS, slots, field.shape[-1]).swapaxes(0, 1)

    def send_rows(picked):
        return route(picked).reshape(EXPERTS * trees * slots, picked.shape[-1])

    def bring_rows(field):
        back = route(field.reshape(EXPERTS, trees, slots, field.shape[-1])).swapaxes(0, 1)
        return back.reshape(trees, EXPERTS * slots, field.shape[-1])

    def combine_rows(chosen, back):
        return by_rows(jnp.einsum("bst,bsd->btd", chosen, back, preferred_element_type=f32))

    place, paths, key_bits = tree_tables(segments, parents)
    offset = seq_index * rows
    own_place = lax.dynamic_slice_in_dim(place, offset, rows, 1).astype(f32)
    own_paths = lax.dynamic_slice_in_dim(paths, offset, rows, 1)
    half = HEAD_DIM // 2
    rates = jnp.exp(-math.log(theta) * 2.0 * jnp.arange(half, dtype=f32) / HEAD_DIM)
    angle = rates[None, :, None] * own_place[:, None, :]
    cosine = jnp.cos(angle)[:, None]
    sine = jnp.sin(angle)[:, None]
    inputs = tokens.astype(f32)
    scale_one = lax.rsqrt(jnp.mean(inputs * inputs, -1, keepdims=True) + epsilon)
    first_in = (inputs * scale_one * gains[0]).astype(bf16)
    mapped = jnp.einsum("dh,btd->bht", project_all, first_in, preferred_element_type=f32)
    queries = (
        turned(mapped[:, :part_width], cosine, sine, False) * HEAD_DIM ** (-0.5)
    ).astype(bf16)
    pairs_own = jnp.concatenate(
        [
            turned(mapped[:, part_width : 2 * part_width], cosine, sine, False).astype(bf16),
            mapped[:, 2 * part_width :].astype(bf16),
        ],
        1,
    )
    key_column = key_bits[:, :, None]
    path_row = own_paths[:, None, :]
    pairs = [pairs_own]
    links = [pairs_own[tree : tree + 1] for tree in range(trees)]
    shared_bundle = jnp.concatenate([spreader, collector.T[None]], 0)
    state = ()
    for number in range(seq_size):
        if number + 1 < seq_size:
            links = [
                lax.ppermute(link, SEQ, [(i, i + 1) for i in range(seq_size - 1)])
                for link in links
            ]
        else:
            picked_cotangent, pairs[-1] = tied(pick_rows(cotangent), pairs[-1])
        state = attend(
            number,
            number == seq_size - 1,
            place_arg,
            queries,
            key_column,
            path_row,
            pairs[number],
            state,
        )
        if number + 1 < seq_size:
            *links, first_state = tied(*links, state[0])
            state = (first_state,) + tuple(state[1:])
            pairs.append(jnp.concatenate(links, 0))
    outs, logs = state[:2]

    bundles = jnp.concatenate([expander, reducer.transpose(0, 2, 1)[:, None]], 1)
    own_expert = route(bundles).swapaxes(0, 1).reshape(3, model_width, hidden)
    expert_weights = lax.all_gather(own_expert, TENSOR, axis=0, tiled=False)
    outs, expert_weights = tied(outs, expert_weights)
    heads = share(outs, TENSOR, shards, 1)
    upstream_rows = send_rows(picked_cotangent)
    heads, upstream_rows = tied(heads, upstream_rows)
    second = inputs + by_rows(
        jnp.einsum("bht,hd->btd", heads, mixing_all, preferred_element_type=f32)
    )

    scale_two = lax.rsqrt(jnp.mean(second * second, -1, keepdims=True) + epsilon)
    hidden_in = (second * scale_two * gains[1]).astype(bf16)
    flat = (trees * rows, model_width)
    flat_hidden = hidden_in.reshape(flat)
    flat_cotangent = cotangent.reshape(flat)
    expert_rows = send_rows(pick_rows(hidden_in))
    expert_rows, shared_bundle = tied(expert_rows, shared_bundle)
    shared_weights = lax.all_gather(
        shared_bundle, GROUP, axis=1, tiled=True
    )
    row_chances = jax.nn.softmax(jnp.dot(expert_rows, router_all, preferred_element_type=f32), -1)
    own_label = jnp.arange(EXPERTS, dtype=jnp.int32) == member_index
    row_gates = jnp.sum(jnp.where(own_label[None], row_chances, 0.0), -1, keepdims=True)
    row_grads = (row_gates * upstream_rows.astype(f32)).astype(bf16)
    lowered, routed_back, expert_wide = gated(expert_rows, row_grads, expert_weights, TILE)
    gate_grads = jnp.sum(upstream_rows.astype(f32) * lowered, -1, keepdims=True)
    lanes = jnp.arange(128, dtype=jnp.int32)[None]
    back_rows = jnp.concatenate(
        [
            routed_back.astype(bf16),
            jnp.where(lanes == member_index, gate_grads, 0.0).astype(bf16),
        ],
        1,
    )
    flat_hidden, row_grads, back_rows = tied(flat_hidden, row_grads, back_rows)
    shared_out, shared_back, shared_wide = gated(
        flat_hidden, flat_cotangent, shared_weights[None], TILE
    )
    expert_parts = weight_parts(
        expert_rows, row_grads, expert_wide, shards, group_size, TILE
    )
    back_rows = bring_rows(back_rows)
    chosen, shared_back = tied(chosen, shared_back)
    returned_back = combine_rows(chosen, back_rows)
    out_rows = (row_gates * lowered).astype(bf16)
    shared_parts = weight_parts(
        flat_hidden, flat_cotangent, shared_wide, 1, group_size, TILE
    )

    def own_rows(field):
        return lax.dynamic_slice_in_dim(field, shard * quarter, quarter, 1)

    def add_shards(field):
        held = field.astype(bf16).reshape(trees, shards, quarter, field.shape[-1])
        step = 1
        while step < shards:
            paired = held.reshape(trees, -1, 2, quarter, field.shape[-1])
            bit = (shard // step) % 2
            kept = lax.dynamic_index_in_dim(paired, bit, 2, keepdims=False)
            sent = lax.dynamic_index_in_dim(paired, 1 - bit, 2, keepdims=False)
            added = kept.astype(f32) + swap(sent, TENSOR, shards, step).astype(f32)
            step *= 2
            held = added.astype(bf16) if step < shards else added
        return held[:, 0]

    def spread_shards(field):
        pieces = share(field[None], TENSOR, shards, 0)
        return jnp.concatenate(
            [pick(pieces, reversed_bits(shard ^ other, shards)) for other in range(shards)], 1
        )

    summed = add_shards(
        returned_back
        + jnp.pad(shared_back.reshape(trees, rows, model_width), ((0, 0), (0, 0), (0, 128)))
    )
    summed, shared_parts, out_rows = tied(summed, shared_parts, out_rows)
    chance_grad = summed[..., model_width : model_width + EXPERTS]
    quarter_second = own_rows(second)
    quarter_scale = own_rows(scale_two)
    quarter_normed = quarter_second * quarter_scale
    quarter_hidden = own_rows(hidden_in)
    logits = jnp.dot(quarter_hidden, router_all, preferred_element_type=f32)
    chances = jax.nn.softmax(logits, -1)
    logit_grad = chances * (chance_grad - jnp.sum(chances * chance_grad, -1, keepdims=True))
    hidden_grad = summed[..., :model_width] + jnp.einsum(
        "bte,de->btd", logit_grad, router_all.astype(f32), precision=highest
    )
    router_part = jnp.einsum(
        "btd,bte->de", quarter_hidden.astype(f32), logit_grad, precision=highest
    )
    gain_two = jnp.sum(hidden_grad * quarter_normed, (0, 1))
    scaled_two = hidden_grad * gains[1]
    second_grad = own_rows(cotangent).astype(f32) + quarter_scale * (
        scaled_two - quarter_normed * jnp.mean(scaled_two * quarter_normed, -1, keepdims=True)
    )
    branch_grad = spread_shards(second_grad.astype(bf16))
    returned_out = combine_rows(chosen, bring_rows(out_rows))
    partial_out = (returned_out + shared_out.reshape(trees, rows, model_width)).astype(bf16)

    heads_grad = jnp.einsum(
        "hd,btd->bht", mixing_own, branch_grad, preferred_element_type=f32
    ).astype(bf16)
    mixing_part = jnp.einsum("btd,bht->dh", branch_grad, outs, preferred_element_type=f32)
    query_grad = ()
    pair_grads = []
    for number in range(seq_size - 1, -1, -1):
        query_grad, pair_grad = attend_back(
            number,
            bf16 if number == seq_size - 1 else f32,
            place_arg,
            (queries, outs, heads_grad, logs, key_column, path_row, pairs[number])
            + ((query_grad,) if pair_grads else ()),
        )
        pair_grads.append(pair_grad)
    pair_grad = pair_grads[0]
    shared_grads = lax.psum_scatter(
        shared_parts[0], GROUP, scatter_dimension=0, tiled=True
    )[0].astype(f32)
    own_grads = []
    for tree in range(trees):
        moving = pair_grad[tree]
        for step, addend in enumerate(pair_grads[1:]):
            moved = lax.ppermute(
                moving.astype(bf16), SEQ, [(i + 1, i) for i in range(seq_size - 1)]
            )
            if tree == 0 and step == 0:
                moved, expert_parts = tied(moved, expert_parts)
                expert_own = lax.psum_scatter(
                    expert_parts, TENSOR, scatter_dimension=0, tiled=False
                )
            moving = addend[tree] + moved.astype(f32)
        own_grads.append(moving)
    pair_grad, shared_grads, partial_out = tied(jnp.stack(own_grads), shared_grads, partial_out)
    output = spread_shards((quarter_second + add_shards(partial_out)).astype(bf16))
    spreader_grad = shared_grads[:2]
    collector_grad = shared_grads[2].T
    query_grad = query_grad * HEAD_DIM ** (-0.5)
    mapped_grad = jnp.concatenate(
        [
            turned(query_grad, cosine, sine, True),
            turned(pair_grad[:, :part_width], cosine, sine, True),
            pair_grad[:, part_width:],
        ],
        1,
    ).astype(bf16)
    first_part = by_rows(
        jnp.einsum("bht,dh->btd", mapped_grad, project_all, preferred_element_type=f32)
    ).astype(bf16)
    first_part, mapped_grad = tied(first_part, mapped_grad)
    first_grad = add_shards(first_part)
    project_part = by_rows(
        jnp.einsum("btd,bht->dh", first_in, mapped_grad, preferred_element_type=f32)
    )
    quarter_scale_one = own_rows(scale_one)
    quarter_normed_one = own_rows(inputs) * quarter_scale_one
    scaled_one = first_grad * gains[0]
    input_grad = spread_shards(
        (
            second_grad
            + quarter_scale_one
            * (
                scaled_one
                - quarter_normed_one * jnp.mean(scaled_one * quarter_normed_one, -1, keepdims=True)
            )
        ).astype(bf16)
    )


    small_parts = jnp.concatenate(
        [
            project_part,
            mixing_part,
            router_part,
            gain_two[:, None],
            jnp.zeros((model_width, -(4 * part_width + EXPERTS + 1) % 128), f32),
        ],
        1,
    ).astype(bf16)
    small_home = route(small_parts.reshape(group_size, owned, -1))
    small_home, expert_own = tied(small_home, expert_own)
    expert_grads = route(expert_own).astype(f32)
    expander_grad = expert_grads[:, :2]
    reducer_grad = expert_grads[:, 2].transpose(0, 2, 1)
    small_grads = jnp.sum(
        small_home.astype(f32),
        0,
    )
    project_grad = (
        small_grads[:, : 3 * part_width].reshape(owned, 3, part_width).transpose(1, 0, 2)
    )
    mixing_grad = small_grads[:, 3 * part_width : 4 * part_width].T
    rest = small_grads[:, 4 * part_width : 4 * part_width + EXPERTS + 1]
    gain_one = jnp.sum(project_grad * project.astype(f32), (0, 2)) / norm_gains[0].astype(f32)
    tiny = lax.psum(
        jnp.concatenate([rest.T, gain_one[None]], 0),
        TENSOR,
    )
    tiny, input_grad = tied(tiny, input_grad)
    router_grad = tiny[:EXPERTS].T
    gain_grad = jnp.stack([tiny[EXPERTS + 1], tiny[EXPERTS]])
    return (
        output,
        input_grad,
        gain_grad,
        project_grad,
        mixing_grad,
        router_grad,
        expander_grad,
        reducer_grad,
        spreader_grad,
        collector_grad,
    )


def solution(mesh):
    in_specs = (
        P(DP, SEQ, None),
        P(DP, SEQ, None),
        P(DP, None),
        P(DP, None),
        P(DP, SEQ, None),
        P(None, GROUP),
        P(None, GROUP, TENSOR),
        P(TENSOR, GROUP),
        P(GROUP, None),
        P(None, None, GROUP, TENSOR),
        P(None, TENSOR, GROUP),
        P(None, GROUP, TENSOR),
        P(TENSOR, GROUP),
    )
    out_specs = (
        P(DP, SEQ, None),
        P(DP, SEQ, None),
        P(None, GROUP),
        P(None, GROUP, TENSOR),
        P(TENSOR, GROUP),
        P(GROUP, None),
        P(None, None, GROUP, TENSOR),
        P(None, TENSOR, GROUP),
        P(None, GROUP, TENSOR),
        P(TENSOR, GROUP),
    )
    sizes = mesh.shape
    group_size = sizes[DP] * sizes[SEQ]
    shards = sizes[TENSOR]
    fits = group_size == EXPERTS and shards & (shards - 1) == 0 and CAP % shards == 0
    body = local_fast if fits else local
    return jax.shard_map(body, mesh=mesh, in_specs=in_specs, out_specs=out_specs, check_vma=False)
```

```python
import functools
import math
import types

import jax
import jax.numpy as jnp
from jax import lax
from jax.experimental import pallas as pl
from jax.experimental.layout import Layout, with_layout_constraint
from jax.experimental.pallas import tpu as pltpu
from jax.sharding import PartitionSpec as P

HEAD_DIM = 64
EXPERTS = 8
CAP = 192
QB = 512
DP = "dp"
SEQ = "seq"
TENSOR = "tensor"
GROUP = (DP, SEQ)


epsilon = 1e-05
theta = 10000.0
highest = lax.Precision.HIGHEST


def ancestry(parents):
    labels = jnp.arange(parents.shape[0], dtype=jnp.int32)
    grandparent = jnp.take(parents, parents)
    itself = labels[:, None] == labels[None, :]
    return (
        itself | (parents[:, None] == labels[None, :]) | (grandparent[:, None] == labels[None, :])
    )


def positions(segments, table):
    labels = jnp.arange(table.shape[0], dtype=jnp.int32)
    member = (segments[:, None] == labels[None, :]).astype(jnp.int32)
    lengths = jnp.sum(member, 0)
    offsets = jnp.cumsum(lengths) - lengths
    ancestral = jnp.sum(table.astype(jnp.int32) * lengths[None, :], 1) - lengths
    moving = ancestral - offsets
    return jnp.arange(segments.shape[0], dtype=jnp.int32) + jnp.sum(member * moving[None, :], 1)


def visible(row_segments, row_index, key_segments, key_index, table):
    labels = jnp.arange(table.shape[0], dtype=jnp.int32)
    member_rows = (row_segments[:, None] == labels[None, :]).astype(jnp.bfloat16)
    member_keys = (key_segments[:, None] == labels[None, :]).astype(jnp.bfloat16)
    reach = jnp.dot(member_rows, table.astype(jnp.bfloat16), preferred_element_type=jnp.float32)
    hits = jnp.einsum(
        "bs,ls->bl", reach.astype(jnp.bfloat16), member_keys, preferred_element_type=jnp.float32
    )
    return (hits > 0.5) & (key_index[None, :] <= row_index[:, None])


def turn(field, place, backward):
    half = field.shape[-1] // 2
    rates = jnp.exp(-math.log(theta) * 2.0 * jnp.arange(half, dtype=jnp.float32) / field.shape[-1])
    angle = place[:, None] * rates[None, :]
    cosine = jnp.cos(angle)[:, None, :]
    sine = jnp.sin(angle)[:, None, :]
    first_half = field[..., :half]
    second_half = field[..., half:]
    if backward:
        return jnp.concatenate(
            [first_half * cosine + second_half * sine, second_half * cosine - first_half * sine], -1
        )
    return jnp.concatenate(
        [first_half * cosine - second_half * sine, second_half * cosine + first_half * sine], -1
    )


def slot_of(route_flat):
    labels = jnp.arange(EXPERTS, dtype=jnp.int32)
    member = (route_flat[:, None] == labels[None, :]).astype(jnp.int32)
    ranks = jnp.cumsum(member, 0) - 1
    return route_flat * CAP + jnp.sum(ranks * member, 1)


def owner_of(slot_ids, count_rows, per_row):
    picked = jnp.arange(slot_ids.shape[0], dtype=jnp.int32) // per_row
    return jnp.full((EXPERTS * CAP,), count_rows, jnp.int32).at[slot_ids].set(picked)


def silu_slope(value):
    sigma = jax.nn.sigmoid(value)
    return sigma * (1.0 + value * (1.0 - sigma))


def block_scores(query_block, key_block, seg_block, index_block, key_segments, key_index, table):
    seen = visible(seg_block, index_block, key_segments, key_index, table)
    raw = jnp.einsum("bhd,lhd->hbl", query_block, key_block, preferred_element_type=jnp.float32)
    return jnp.where(seen[None], raw * HEAD_DIM ** (-0.5), -1e30)


def fetch(norm_gains, project, mixing, router, expander, reducer, spreader, collector):
    return (
        lax.all_gather(norm_gains, GROUP, axis=1, tiled=True),
        lax.all_gather(project, GROUP, axis=1, tiled=True),
        lax.all_gather(mixing, GROUP, axis=1, tiled=True),
        lax.all_gather(router, GROUP, axis=0, tiled=True),
        lax.all_gather(expander, GROUP, axis=2, tiled=True),
        lax.all_gather(reducer, GROUP, axis=2, tiled=True),
        lax.all_gather(spreader, GROUP, axis=1, tiled=True),
        lax.all_gather(collector, GROUP, axis=1, tiled=True),
    )


def reduce_end(grads):
    (
        gain_part,
        project_part,
        mixing_part,
        router_part,
        expander_part,
        reducer_part,
        spreader_part,
        collector_part,
    ) = grads
    return (
        lax.psum_scatter(gain_part, GROUP, scatter_dimension=1, tiled=True),
        lax.psum_scatter(project_part, GROUP, scatter_dimension=1, tiled=True),
        lax.psum_scatter(mixing_part, GROUP, scatter_dimension=1, tiled=True),
        lax.psum_scatter(router_part, GROUP, scatter_dimension=0, tiled=True),
        lax.psum_scatter(expander_part, GROUP, scatter_dimension=2, tiled=True),
        lax.psum_scatter(reducer_part, GROUP, scatter_dimension=2, tiled=True),
        lax.psum_scatter(spreader_part, GROUP, scatter_dimension=1, tiled=True),
        lax.psum_scatter(collector_part, GROUP, scatter_dimension=1, tiled=True),
    )


def forward_pass(tree_tokens, tree_segments, tree_parents, tree_routes, weights, offset):
    norm_gains, project, mixing, router, expander, reducer, spreader, collector = weights
    row_count = tree_tokens.shape[0]
    model_width = tree_tokens.shape[1]
    tree_length = tree_segments.shape[0]
    local_heads = project.shape[2] // HEAD_DIM
    table = ancestry(tree_parents)
    place = lax.dynamic_slice_in_dim(positions(tree_segments, table), offset, row_count).astype(
        jnp.float32
    )
    row_segments = lax.dynamic_slice_in_dim(tree_segments, offset, row_count)
    row_index = offset + jnp.arange(row_count, dtype=jnp.int32)
    key_index = jnp.arange(tree_length, dtype=jnp.int32)
    inputs = tree_tokens.astype(jnp.float32)
    scale_one = lax.rsqrt(jnp.mean(inputs * inputs, -1, keepdims=True) + epsilon)
    normed_one = inputs * scale_one
    first_in = (normed_one * norm_gains[0].astype(jnp.float32)).astype(jnp.bfloat16)
    mapped = jnp.einsum("td,cdh->cth", first_in, project, preferred_element_type=jnp.float32)
    head_shape = (row_count, local_heads, HEAD_DIM)
    queries = turn(mapped[0].reshape(head_shape), place, False).astype(jnp.bfloat16)
    keys_own = (
        turn(mapped[1].reshape(head_shape), place, False)
        .astype(jnp.bfloat16)
        .reshape(row_count, -1)
    )
    values_own = mapped[2].astype(jnp.bfloat16)
    keys_flat, values_flat = (
        lax.all_gather(keys_own, SEQ, axis=0, tiled=True),
        lax.all_gather(values_own, SEQ, axis=0, tiled=True),
    )
    keys_all = keys_flat.reshape(tree_length, local_heads, HEAD_DIM)
    values_all = values_flat.reshape(tree_length, local_heads, HEAD_DIM)
    blocks = row_count // QB
    query_blocks = queries.reshape(blocks, QB, local_heads, HEAD_DIM)
    seg_blocks = row_segments.reshape(blocks, QB)
    index_blocks = row_index.reshape(blocks, QB)

    def attend(entries):
        query_block, seg_block, index_block = entries
        scores = block_scores(
            query_block, keys_all, seg_block, index_block, tree_segments, key_index, table
        )
        row_peak = jnp.max(scores, -1, keepdims=True)
        expo = jnp.exp(scores - row_peak)
        row_total = jnp.sum(expo, -1, keepdims=True)
        chances_soft = expo / row_total
        mixed_block = jnp.einsum(
            "hbl,lhd->bhd",
            chances_soft.astype(jnp.bfloat16),
            values_all,
            preferred_element_type=jnp.float32,
        )
        return (mixed_block, (row_peak + jnp.log(row_total))[..., 0])

    mixed, log_totals = lax.map(attend, (query_blocks, seg_blocks, index_blocks))
    heads_out = mixed.reshape(row_count, -1).astype(jnp.bfloat16)
    attended = lax.psum(
        jnp.dot(heads_out, mixing, preferred_element_type=jnp.float32).astype(jnp.bfloat16),
        TENSOR,
    ).astype(jnp.float32)
    second = inputs + attended
    scale_two = lax.rsqrt(jnp.mean(second * second, -1, keepdims=True) + epsilon)
    normed_two = second * scale_two
    hidden_in = (normed_two * norm_gains[1].astype(jnp.float32)).astype(jnp.bfloat16)
    logits = jnp.dot(hidden_in, router, preferred_element_type=jnp.float32)
    shifted = jnp.exp(logits - jnp.max(logits, -1, keepdims=True))
    chances = shifted / jnp.sum(shifted, -1, keepdims=True)
    picks = (tree_routes[:, :, None] == jnp.arange(EXPERTS, dtype=jnp.int32)[None, None, :]).astype(
        jnp.float32
    )
    gates = jnp.sum(picks * chances[:, None, :], -1)
    per_row = tree_routes.shape[1]
    slot_ids = slot_of(tree_routes.reshape(-1))
    owners = owner_of(slot_ids, row_count, per_row)
    padded = jnp.concatenate([hidden_in, jnp.zeros((1, model_width), jnp.bfloat16)], 0)
    routed = jnp.take(padded, owners, axis=0).reshape(EXPERTS, CAP, model_width)
    raised = jnp.einsum("ecd,egdf->gecf", routed, expander, preferred_element_type=jnp.float32)
    activated = (jax.nn.silu(raised[0]) * raised[1]).astype(jnp.bfloat16)
    lowered = jnp.einsum(
        "ecf,efd->ecd", activated, reducer, preferred_element_type=jnp.float32
    ).reshape(EXPERTS * CAP, model_width)
    returned = jnp.take(lowered, slot_ids, axis=0).reshape(row_count, per_row, model_width)
    blended = jnp.sum(gates[:, :, None] * returned, 1)
    spread = jnp.einsum("td,gdf->gtf", hidden_in, spreader, preferred_element_type=jnp.float32)
    common = (jax.nn.silu(spread[0]) * spread[1]).astype(jnp.bfloat16)
    shared_out = jnp.dot(common, collector, preferred_element_type=jnp.float32)
    branches = lax.psum((blended + shared_out).astype(jnp.bfloat16), TENSOR).astype(jnp.float32)
    output_tree = (second + branches).astype(jnp.bfloat16)
    kept = types.SimpleNamespace(
        table=table,
        place=place,
        offset=offset,
        row_segments=row_segments,
        seg_blocks=seg_blocks,
        index_blocks=index_blocks,
        scale_one=scale_one,
        normed_one=normed_one,
        first_in=first_in,
        queries=queries,
        query_blocks=query_blocks,
        keys_all=keys_all,
        values_all=values_all,
        log_totals=log_totals,
        heads_out=heads_out,
        scale_two=scale_two,
        normed_two=normed_two,
        hidden_in=hidden_in,
        chances=chances,
        picks=picks,
        gates=gates,
        slot_ids=slot_ids,
        routed=routed,
        raised=raised,
        activated=activated,
        returned=returned,
        spread=spread,
        common=common,
    )
    return (kept, output_tree)


def backward_pass(tree_cot, tree_segments, kept, weights):
    norm_gains, project, mixing, router, expander, reducer, spreader, collector = weights
    upstream = tree_cot.astype(jnp.float32)
    row_count = upstream.shape[0]
    model_width = upstream.shape[1]
    shared_grad = upstream.astype(jnp.bfloat16)
    common_grad = jnp.einsum(
        "td,fd->tf", shared_grad, collector, preferred_element_type=jnp.float32
    )
    collector_part = jnp.einsum(
        "tf,td->fd", kept.common, shared_grad, preferred_element_type=jnp.float32
    )
    spread = kept.spread
    spread_grad = jnp.stack(
        [common_grad * spread[1] * silu_slope(spread[0]), common_grad * jax.nn.silu(spread[0])]
    ).astype(jnp.bfloat16)
    spreader_part = jnp.einsum(
        "td,gtf->gdf", kept.hidden_in, spread_grad, preferred_element_type=jnp.float32
    )
    hidden_grad = jnp.einsum(
        "gtf,gdf->td", spread_grad, spreader, preferred_element_type=jnp.float32
    )
    gates = kept.gates
    slot_ids = kept.slot_ids
    per_row = gates.shape[1]
    pair_grad = (
        (gates[:, :, None] * upstream[:, None, :])
        .astype(jnp.bfloat16)
        .reshape(row_count * per_row, model_width)
    )
    lowered_grad = (
        jnp.zeros((EXPERTS * CAP, model_width), jnp.bfloat16)
        .at[slot_ids]
        .set(pair_grad)
        .reshape(EXPERTS, CAP, model_width)
    )
    activated_grad = jnp.einsum(
        "ecd,efd->ecf", lowered_grad, reducer, preferred_element_type=jnp.float32
    )
    reducer_part = jnp.einsum(
        "ecf,ecd->efd", kept.activated, lowered_grad, preferred_element_type=jnp.float32
    )
    raised = kept.raised
    raised_grad = jnp.stack(
        [
            activated_grad * raised[1] * silu_slope(raised[0]),
            activated_grad * jax.nn.silu(raised[0]),
        ]
    ).astype(jnp.bfloat16)
    expander_part = jnp.einsum(
        "ecd,gecf->egdf", kept.routed, raised_grad, preferred_element_type=jnp.float32
    )
    routed_grad = jnp.einsum(
        "gecf,egdf->ecd", raised_grad, expander, preferred_element_type=jnp.float32
    ).reshape(EXPERTS * CAP, model_width)
    hidden_grad = hidden_grad + jnp.sum(
        jnp.take(routed_grad, slot_ids, axis=0).reshape(row_count, per_row, model_width), 1
    )
    gate_grad = jnp.sum(upstream[:, None, :] * kept.returned, -1)
    hidden_grad, gate_grad = (
        lax.psum(hidden_grad.astype(jnp.bfloat16), TENSOR).astype(jnp.float32),
        lax.psum(gate_grad.astype(jnp.bfloat16), TENSOR).astype(jnp.float32),
    )
    chances = kept.chances
    chance_grad = jnp.sum(kept.picks * gate_grad[:, :, None], 1)
    logit_grad = chances * (chance_grad - jnp.sum(chances * chance_grad, -1, keepdims=True))
    hidden_grad = hidden_grad + jnp.dot(logit_grad, router.astype(jnp.float32).T, precision=highest)
    router_part = jnp.dot(kept.hidden_in.astype(jnp.float32).T, logit_grad, precision=highest)
    normed_two = kept.normed_two
    gain_two = jnp.sum(hidden_grad * normed_two, 0)
    scaled_two = hidden_grad * norm_gains[1].astype(jnp.float32)
    second_grad = upstream + kept.scale_two * (
        scaled_two - normed_two * jnp.mean(scaled_two * normed_two, -1, keepdims=True)
    )
    branch_grad = second_grad.astype(jnp.bfloat16)
    mixing_part = jnp.einsum(
        "th,td->hd", kept.heads_out, branch_grad, preferred_element_type=jnp.float32
    )
    heads_grad = jnp.einsum(
        "td,hd->th", branch_grad, mixing, preferred_element_type=jnp.float32
    ).astype(jnp.bfloat16)
    keys_all = kept.keys_all
    values_all = kept.values_all
    table = kept.table
    query_blocks = kept.query_blocks
    tree_length = keys_all.shape[0]
    local_heads = keys_all.shape[1]
    key_index = jnp.arange(tree_length, dtype=jnp.int32)
    grad_blocks = heads_grad.reshape(query_blocks.shape)
    factor = HEAD_DIM ** (-0.5)

    def attend_back(carry, entries):
        keys_grad, values_grad = carry
        query_block, grad_block, log_block, seg_block, index_block = entries
        scores = block_scores(
            query_block, keys_all, seg_block, index_block, tree_segments, key_index, table
        )
        chances_soft = jnp.exp(scores - log_block[..., None])
        prob_grad = jnp.einsum(
            "bhd,lhd->hbl", grad_block, values_all, preferred_element_type=jnp.float32
        )
        centre = jnp.sum(chances_soft * prob_grad, -1, keepdims=True)
        score_grad = (chances_soft * (prob_grad - centre) * factor).astype(jnp.bfloat16)
        query_grad_block = jnp.einsum(
            "hbl,lhd->bhd", score_grad, keys_all, preferred_element_type=jnp.float32
        )
        keys_grad = keys_grad + jnp.einsum(
            "hbl,bhd->lhd", score_grad, query_block, preferred_element_type=jnp.float32
        )
        values_grad = values_grad + jnp.einsum(
            "hbl,bhd->lhd",
            chances_soft.astype(jnp.bfloat16),
            grad_block,
            preferred_element_type=jnp.float32,
        )
        return ((keys_grad, values_grad), query_grad_block)

    zero_kv = jnp.zeros((tree_length, local_heads, HEAD_DIM), jnp.float32)
    (keys_grad, values_grad), query_grad = lax.scan(
        attend_back,
        (zero_kv, zero_kv),
        (query_blocks, grad_blocks, kept.log_totals, kept.seg_blocks, kept.index_blocks),
    )
    keys_own_grad, values_own_grad = (
        lax.psum_scatter(
            keys_grad.reshape(tree_length, -1).astype(jnp.bfloat16),
            SEQ,
            scatter_dimension=0,
            tiled=True,
        ).astype(jnp.float32),
        lax.psum_scatter(
            values_grad.reshape(tree_length, -1).astype(jnp.bfloat16),
            SEQ,
            scatter_dimension=0,
            tiled=True,
        ).astype(jnp.float32),
    )
    place = kept.place
    query_back = turn(query_grad.reshape(row_count, local_heads, HEAD_DIM), place, True).reshape(
        row_count, -1
    )
    key_back = turn(keys_own_grad.reshape(row_count, local_heads, HEAD_DIM), place, True).reshape(
        row_count, -1
    )
    mapped_grad = jnp.stack([query_back, key_back, values_own_grad]).astype(jnp.bfloat16)
    project_part = jnp.einsum(
        "td,cth->cdh", kept.first_in, mapped_grad, preferred_element_type=jnp.float32
    )
    first_grad = lax.psum(
        jnp.einsum("cth,cdh->td", mapped_grad, project, preferred_element_type=jnp.float32).astype(
            jnp.bfloat16
        ),
        TENSOR,
    ).astype(jnp.float32)
    normed_one = kept.normed_one
    gain_one = jnp.sum(first_grad * normed_one, 0)
    scaled_one = first_grad * norm_gains[0].astype(jnp.float32)
    input_tree = (
        second_grad
        + kept.scale_one
        * (scaled_one - normed_one * jnp.mean(scaled_one * normed_one, -1, keepdims=True))
    ).astype(jnp.bfloat16)
    gain_part = jnp.stack([gain_one, gain_two])
    return (
        input_tree,
        (
            gain_part,
            project_part,
            mixing_part,
            router_part,
            expander_part,
            reducer_part,
            spreader_part,
            collector_part,
        ),
    )


def local(
    tokens,
    cotangent,
    segments,
    parents,
    routes,
    norm_gains,
    project,
    mixing,
    router,
    expander,
    reducer,
    spreader,
    collector,
):
    tree_count = tokens.shape[0]
    offset = lax.axis_index(SEQ) * tokens.shape[1]
    outputs = []
    input_grads = []
    running = None
    for tree_index in range(tree_count):
        forward_weights = fetch(
            norm_gains, project, mixing, router, expander, reducer, spreader, collector
        )
        kept, output_tree = forward_pass(
            tokens[tree_index],
            segments[tree_index],
            parents[tree_index],
            routes[tree_index],
            forward_weights,
            offset,
        )
        backward_weights = fetch(
            norm_gains, project, mixing, router, expander, reducer, spreader, collector
        )
        input_tree, tree_grads = backward_pass(
            cotangent[tree_index], segments[tree_index], kept, backward_weights
        )
        outputs.append(output_tree)
        input_grads.append(input_tree)
        if running is None:
            running = tree_grads
        else:
            running = tuple((before + addend for before, addend in zip(running, tree_grads)))
    running = reduce_end(running)
    return (
        jnp.stack(outputs),
        jnp.stack(input_grads),
        running[0],
        running[1],
        running[2],
        running[3],
        running[4],
        running[5],
        running[6],
        running[7],
    )


VMEM_BYTES = 56 << 20
TILE = 256
ROWS = 256


def contract(left, right, left_dim, right_dim):
    return lax.dot_general(
        left, right, (((left_dim,), (right_dim,)), ((), ())), preferred_element_type=jnp.float32
    )


def spans(head, width):
    if isinstance(head, int):
        start = head * HEAD_DIM
    else:
        start = pl.multiple_of(head * HEAD_DIM, HEAD_DIM)
    return (pl.ds(start, HEAD_DIM), pl.ds(width + start, HEAD_DIM), pl.ds(head, 1))


def scores_of(keys, queries, seen):
    return jnp.where(seen, contract(keys, queries, 0, 0), -1e30)


def seen_block(number, place_ref, key_bits_ref, query_bits, length):
    start = pl.multiple_of((place_ref[0] - number) * length, length)
    seen = (key_bits_ref[pl.ds(start, length), :] & query_bits) != 0
    if number == 0:
        keys = lax.broadcasted_iota(jnp.int32, seen.shape, 0)
        rows = lax.broadcasted_iota(jnp.int32, seen.shape, 1)
        seen = seen & (keys <= rows)
    return seen


def attend_kernel(number, final, heads, place_ref, query_ref, key_bits_ref, query_bits_ref, *refs):
    pair_ref = refs[0]
    if number:
        old_peak_ref, old_total_ref, old_mixed_ref = refs[1:4]
    peak_ref, total_ref, mixed_ref = refs[-3:]
    length = query_ref.shape[1]
    width = heads * HEAD_DIM

    def block():
        seen = seen_block(number, place_ref, key_bits_ref, query_bits_ref[...], length)

        def one(head, _):
            span, value_span, row = spans(head, width)
            scores = scores_of(pair_ref[span, :], query_ref[span, :], seen)
            peak = jnp.max(scores, 0, keepdims=True)
            if number:
                before = old_peak_ref[row, :]
                peak = jnp.maximum(before, peak)
                shrink = jnp.exp(before - peak)
            expo = jnp.exp(scores - peak)
            total = jnp.sum(expo, 0, keepdims=True)
            mixed = jnp.dot(
                pair_ref[value_span, :],
                expo.astype(jnp.bfloat16),
                preferred_element_type=jnp.float32,
            )
            if number:
                total = total + shrink * old_total_ref[row, :]
                mixed = mixed + shrink * old_mixed_ref[span, :]
            peak_ref[row, :] = peak
            total_ref[row, :] = total
            mixed_ref[span, :] = mixed
            return 0

        lax.fori_loop(0, heads, one, 0)

    def keep():
        peak_ref[...] = old_peak_ref[...]
        total_ref[...] = old_total_ref[...]
        mixed_ref[...] = old_mixed_ref[...]

    if number:
        pl.when(place_ref[0] >= number)(block)
        pl.when(place_ref[0] < number)(keep)
    else:
        block()
    if final:
        out_ref, log_ref = refs[4:6]
        for head in range(heads):
            span, _, row = spans(head, width)
            out_ref[span, :] = (mixed_ref[span, :] / total_ref[row, :]).astype(out_ref.dtype)
            log_ref[row, :] = peak_ref[row, :] + jnp.log(total_ref[row, :])


def attend_back_kernel(
    number,
    heads,
    place_ref,
    query_ref,
    out_ref,
    grad_ref,
    log_ref,
    key_bits_ref,
    query_bits_ref,
    pair_ref,
    *refs
):
    query_grad_ref, pair_grad_ref = refs[-2:]
    length = query_ref.shape[1]
    width = heads * HEAD_DIM

    def block():
        seen = seen_block(number, place_ref, key_bits_ref, query_bits_ref[...], length)

        def one(head, _):
            span, value_span, row = spans(head, width)
            queries = query_ref[span, :]
            grads = grad_ref[span, :]
            keys = pair_ref[span, :]
            centre = jnp.sum(
                grads.astype(jnp.float32) * out_ref[span, :].astype(jnp.float32), 0, keepdims=True
            )
            chances = jnp.exp(scores_of(keys, queries, seen) - log_ref[row, :])
            prob_grad = contract(pair_ref[value_span, :], grads, 0, 0)
            score_grad = (chances * (prob_grad - centre)).astype(jnp.bfloat16)
            value_grad = contract(grads, chances.astype(jnp.bfloat16), 1, 1)
            key_grad = contract(queries, score_grad, 1, 1)
            query_grad = jnp.dot(keys, score_grad, preferred_element_type=jnp.float32)
            pair_grad_ref[span, :] = key_grad.astype(pair_grad_ref.dtype)
            pair_grad_ref[value_span, :] = value_grad.astype(pair_grad_ref.dtype)
            if len(refs) > 2:
                query_grad = query_grad + refs[0][span, :]
            query_grad_ref[span, :] = query_grad
            return 0

        lax.fori_loop(0, heads, one, 0)

    def empty():
        pair_grad_ref[...] = jnp.zeros_like(pair_grad_ref)
        if len(refs) > 2:
            query_grad_ref[...] = refs[0][...]
        else:
            query_grad_ref[...] = jnp.zeros_like(query_grad_ref)

    if number:
        pl.when(place_ref[0] >= number)(block)
        pl.when(place_ref[0] < number)(empty)
    else:
        block()


def per_tree(array):
    return pl.BlockSpec((None,) + array.shape[1:], lambda tree: (tree, 0, 0))


def attend_call(kernel, name, place, operands, results, flops):
    trees, width, length = operands[0].shape
    return pl.pallas_call(
        kernel,
        grid=(trees,),
        out_shape=results,
        in_specs=[pl.BlockSpec(memory_space=pltpu.SMEM)] + [per_tree(value) for value in operands],
        out_specs=tuple(per_tree(value) for value in results),
        compiler_params=pltpu.CompilerParams(vmem_limit_bytes=VMEM_BYTES),
        cost_estimate=pl.CostEstimate(
            flops=flops * trees * width * length * length,
            transcendentals=trees * width * length * length // HEAD_DIM,
            bytes_accessed=16 * trees * width * length,
        ),
        name=name,
    )(place, *operands)


def attend(number, final, place, queries, key_bits, query_bits, pair, state):
    trees, width, length = queries.shape
    heads = width // HEAD_DIM
    row = jax.ShapeDtypeStruct((trees, heads, length), jnp.float32)
    field = jax.ShapeDtypeStruct(queries.shape, jnp.float32)
    results = (row, row, field)
    if final:
        results = (jax.ShapeDtypeStruct(queries.shape, jnp.bfloat16), row) + results
    return attend_call(
        functools.partial(attend_kernel, number, final, heads),
        "attend",
        place,
        (queries, key_bits, query_bits, pair) + tuple(state),
        results,
        16,
    )


def attend_back(number, kind, place, operands):
    trees, width, length = operands[0].shape
    heads = width // HEAD_DIM
    return attend_call(
        functools.partial(attend_back_kernel, number, heads),
        "attend_back",
        place,
        operands,
        (
            jax.ShapeDtypeStruct((trees, width, length), jnp.float32),
            jax.ShapeDtypeStruct((trees, 2 * width, length), kind),
        ),
        40,
    )


def gated_kernel(
    rows_ref, grads_ref, weights_ref, lowered_ref, routed_ref, first_ref, second_ref, active_ref
):
    @pl.when(pl.program_id(0) == 0)
    def _():
        lowered_ref[...] = jnp.zeros_like(lowered_ref)
        routed_ref[...] = jnp.zeros_like(routed_ref)

    def some(index, _):
        part = (pl.ds(pl.multiple_of(index * ROWS, ROWS), ROWS), slice(None))
        rows = rows_ref[part]
        grads = grads_ref[part]
        gate_weights = weights_ref[0, 0]
        up_weights = weights_ref[0, 1]
        down_weights = weights_ref[0, 2]
        first = jnp.dot(rows, gate_weights, preferred_element_type=jnp.float32)
        second = jnp.dot(rows, up_weights, preferred_element_type=jnp.float32)
        sigma = 1.0 / (1.0 + jnp.exp(-first))
        swish = first * sigma
        activated = (swish * second).astype(jnp.bfloat16)
        activated_grad = jnp.dot(grads, down_weights, preferred_element_type=jnp.float32)
        first_grad = (activated_grad * second * (sigma + swish * (1.0 - sigma))).astype(
            jnp.bfloat16
        )
        second_grad = (activated_grad * swish).astype(jnp.bfloat16)
        lowered_ref[part] += contract(activated, down_weights, 1, 1)
        routed_ref[part] += contract(first_grad, gate_weights, 1, 1) + contract(
            second_grad, up_weights, 1, 1
        )
        first_ref[part] = first_grad
        second_ref[part] = second_grad
        active_ref[part] = activated
        return 0

    lax.fori_loop(0, rows_ref.shape[0] // ROWS, some, 0)


def gated(rows, grads, weights, tile):
    count, model_width = rows.shape
    chunks, _, _, hidden = weights.shape
    tiles = hidden // tile
    fixed = pl.BlockSpec((count, model_width), lambda step: (0, 0))
    moving = pl.BlockSpec(
        (1, 3, model_width, tile), lambda step: (step // tiles, 0, 0, step % tiles)
    )
    column = pl.BlockSpec((count, tile), lambda step: (0, step))
    field = jax.ShapeDtypeStruct((count, model_width), jnp.float32)
    wide = jax.ShapeDtypeStruct((count, chunks * hidden), jnp.bfloat16)
    results = pl.pallas_call(
        gated_kernel,
        grid=(chunks * tiles,),
        out_shape=(field, field, wide, wide, wide),
        in_specs=[fixed, fixed, moving],
        out_specs=(fixed, fixed, column, column, column),
        compiler_params=pltpu.CompilerParams(vmem_limit_bytes=VMEM_BYTES),
        cost_estimate=pl.CostEstimate(
            flops=12 * count * model_width * chunks * hidden,
            transcendentals=count * chunks * hidden,
            bytes_accessed=12 * count * model_width + 6 * (count + model_width) * chunks * hidden,
        ),
        name="gated",
    )(rows, grads, weights)
    return (results[0], results[1], results[2:])


def parts_kernel(
    rows_ref, grads_ref, first_ref, second_ref, active_ref, parts_ref, turned_rows, turned_grads
):
    owned = parts_ref.shape[3]

    @pl.when(pl.program_id(0) == 0)
    def _():
        turned_rows[...] = rows_ref[...].T
        turned_grads[...] = grads_ref[...].T

    def some(index, _):
        part = (pl.ds(pl.multiple_of(index * 2 * owned, 2 * owned), 2 * owned), slice(None))
        rows = turned_rows[part]
        results = (
            contract(rows, first_ref[...], 1, 0),
            contract(rows, second_ref[...], 1, 0),
            contract(turned_grads[part], active_ref[...], 1, 0),
        )
        for kind, result in enumerate(results):
            for half in range(2):
                piece = result[half * owned : (half + 1) * owned]
                parts_ref[0, 2 * index + half, kind] = piece.astype(jnp.bfloat16)
        return 0

    lax.fori_loop(0, parts_ref.shape[1] // 2, some, 0)


def weight_parts(rows, grads, wide, chunks, owners, tile):
    count, model_width = rows.shape
    hidden = wide[0].shape[1] // chunks
    tiles = hidden // tile
    owned = model_width // owners
    fixed = pl.BlockSpec((count, model_width), lambda step: (0, 0))
    column = pl.BlockSpec((count, tile), lambda step: (0, step))
    return pl.pallas_call(
        parts_kernel,
        grid=(chunks * tiles,),
        out_shape=jax.ShapeDtypeStruct((chunks, owners, 3, owned, hidden), jnp.bfloat16),
        in_specs=[fixed, fixed, column, column, column],
        out_specs=pl.BlockSpec(
            (1, owners, 3, owned, tile), lambda step: (step // tiles, 0, 0, 0, step % tiles)
        ),
        scratch_shapes=[pltpu.VMEM((model_width, count), jnp.bfloat16)] * 2,
        compiler_params=pltpu.CompilerParams(vmem_limit_bytes=VMEM_BYTES),
        cost_estimate=pl.CostEstimate(
            flops=6 * count * model_width * chunks * hidden,
            transcendentals=0,
            bytes_accessed=4 * count * model_width + 6 * (count + model_width) * chunks * hidden,
        ),
        name="weight_parts",
    )(rows, grads, *wide)


def swap(piece, axes, size, step):
    return lax.ppermute(piece, axes, [(i, i ^ step) for i in range(size)])


def pick(stacked, index):
    return lax.dynamic_index_in_dim(stacked, index, 0, keepdims=False)


def share(piece, axes, size, dim):
    step = size // 2
    while step:
        piece = jnp.concatenate([piece, swap(piece, axes, size, step)], dim)
        step //= 2
    return piece


def reversed_bits(index, size):
    bits = size.bit_length() - 1
    return sum(((index >> bit) & 1) << (bits - 1 - bit) for bit in range(bits))


def tied(*values):
    return lax.optimization_barrier(values)


def route(blocks):
    return lax.all_to_all(blocks, GROUP, split_axis=0, concat_axis=0)


def by_rows(field):
    order = tuple(range(field.ndim))
    return with_layout_constraint(field, Layout(major_to_minor=order))


def turned(field, cosine, sine, backward):
    half = HEAD_DIM // 2
    shape = field.shape
    split = field.reshape(shape[0], -1, 2, half, shape[-1])
    first_half = split[:, :, 0]
    second_half = split[:, :, 1]
    if backward:
        parts = [
            first_half * cosine + second_half * sine,
            second_half * cosine - first_half * sine,
        ]
    else:
        parts = [
            first_half * cosine - second_half * sine,
            second_half * cosine + first_half * sine,
        ]
    return jnp.stack(parts, 2).reshape(shape)


def tree_tables(segments, parents):
    count = parents.shape[1]
    labels = jnp.arange(count, dtype=jnp.int32)
    is_parent = parents[:, :, None] == labels[None, None, :]
    grand = jnp.sum(jnp.where(is_parent, parents[:, None, :], 0), 2)
    itself = labels[None, :, None] == labels[None, None, :]
    table = itself | is_parent | (grand[:, :, None] == labels[None, None, :])
    member = segments[:, None, :] == labels[None, :, None]
    lengths = jnp.sum(member.astype(jnp.int32), 2)
    ahead = jnp.sum(jnp.where(labels[:, None] > labels[None, :], lengths[:, None, :], 0), 2)
    moving = jnp.sum(jnp.where(table, lengths[:, None, :], 0), 2) - lengths - ahead
    place = jnp.arange(segments.shape[1], dtype=jnp.int32) + jnp.sum(
        jnp.where(member, moving[:, :, None], 0), 1
    )
    bits = jnp.sum(jnp.where(table, jnp.left_shift(1, labels)[None, None, :], 0), 2)
    paths = jnp.sum(jnp.where(member, bits[:, :, None], 0), 1)
    return (place, paths, jnp.left_shift(1, segments))


def local_fast(
    tokens,
    cotangent,
    segments,
    parents,
    routes,
    norm_gains,
    project,
    mixing,
    router,
    expander,
    reducer,
    spreader,
    collector,
):
    bf16, f32 = jnp.bfloat16, jnp.float32
    group_size = lax.axis_size(GROUP)
    seq_size = lax.axis_size(SEQ)
    shards = lax.axis_size(TENSOR)
    member_index = lax.axis_index(GROUP)
    seq_index = lax.axis_index(SEQ)
    shard = lax.axis_index(TENSOR)
    trees, rows, model_width = tokens.shape
    part_width = project.shape[2]
    owned = project.shape[1]
    hidden = spreader.shape[2]
    slots = CAP // shards
    quarter = rows // shards
    place_arg = seq_index.astype(jnp.int32).reshape(1)

    extra = EXPERTS + 2
    pad = -extra % 128
    small = jnp.concatenate(
        [
            project[0],
            project[1],
            project[2],
            mixing.T,
            router,
            norm_gains.T,
            jnp.zeros((owned, pad), bf16),
        ],
        1,
    )
    small = lax.all_gather(small, GROUP, axis=0, tiled=True)
    project_all = small[:, : 3 * part_width]
    mixing_own = small[:, 3 * part_width : 4 * part_width].T
    router_all = small[:, 4 * part_width : 4 * part_width + EXPERTS]
    gains = small[:, 4 * part_width + EXPERTS : 4 * part_width + extra].T.astype(f32)
    mixing_all = share(mixing_own, TENSOR, shards, 0)
    labels = jnp.arange(EXPERTS, dtype=jnp.int32)
    named = jnp.any(routes[:, None, :, :] == labels[None, :, None, None], 3)
    earlier = (
        jnp.arange(rows, dtype=jnp.int32)[:, None] < jnp.arange(rows, dtype=jnp.int32)[None, :]
    )
    ranks = jnp.einsum(
        "bes,st->bet", named.astype(bf16), earlier.astype(bf16), preferred_element_type=f32
    ).astype(jnp.int32)
    slot_index = shard * slots + jnp.arange(slots, dtype=jnp.int32)
    chosen = (
        (named[:, :, None, :] & (ranks[:, :, None, :] == slot_index[None, None, :, None]))
        .astype(bf16)
        .reshape(trees, EXPERTS * slots, rows)
    )

    def pick_rows(field):
        picked = jnp.einsum("bst,btd->bsd", chosen, field, preferred_element_type=f32).astype(bf16)
        return picked.reshape(trees, EXPERTS, slots, field.shape[-1]).swapaxes(0, 1)

    def send_rows(picked):
        return route(picked).reshape(EXPERTS * trees * slots, picked.shape[-1])

    def bring_rows(field):
        back = route(field.reshape(EXPERTS, trees, slots, field.shape[-1])).swapaxes(0, 1)
        return back.reshape(trees, EXPERTS * slots, field.shape[-1])

    def combine_rows(chosen, back):
        return by_rows(jnp.einsum("bst,bsd->btd", chosen, back, preferred_element_type=f32))

    place, paths, key_bits = tree_tables(segments, parents)
    offset = seq_index * rows
    own_place = lax.dynamic_slice_in_dim(place, offset, rows, 1).astype(f32)
    own_paths = lax.dynamic_slice_in_dim(paths, offset, rows, 1)
    half = HEAD_DIM // 2
    rates = jnp.exp(-math.log(theta) * 2.0 * jnp.arange(half, dtype=f32) / HEAD_DIM)
    angle = rates[None, :, None] * own_place[:, None, :]
    cosine = jnp.cos(angle)[:, None]
    sine = jnp.sin(angle)[:, None]
    inputs = tokens.astype(f32)
    scale_one = lax.rsqrt(jnp.mean(inputs * inputs, -1, keepdims=True) + epsilon)
    first_in = (inputs * scale_one * gains[0]).astype(bf16)
    mapped = jnp.einsum("dh,btd->bht", project_all, first_in, preferred_element_type=f32)
    queries = (
        turned(mapped[:, :part_width], cosine, sine, False) * HEAD_DIM ** (-0.5)
    ).astype(bf16)
    pairs_own = jnp.concatenate(
        [
            turned(mapped[:, part_width : 2 * part_width], cosine, sine, False).astype(bf16),
            mapped[:, 2 * part_width :].astype(bf16),
        ],
        1,
    )
    key_column = key_bits[:, :, None]
    path_row = own_paths[:, None, :]
    pairs = [pairs_own]
    links = [pairs_own[tree : tree + 1] for tree in range(trees)]
    shared_bundle = jnp.concatenate([spreader, collector.T[None]], 0)
    state = ()
    for number in range(seq_size):
        if number + 1 < seq_size:
            links = [
                lax.ppermute(link, SEQ, [(i, i + 1) for i in range(seq_size - 1)])
                for link in links
            ]
        else:
            picked_cotangent, pairs[-1] = tied(pick_rows(cotangent), pairs[-1])
        state = attend(
            number,
            number == seq_size - 1,
            place_arg,
            queries,
            key_column,
            path_row,
            pairs[number],
            state,
        )
        if number + 1 < seq_size:
            *links, first_state = tied(*links, state[0])
            state = (first_state,) + tuple(state[1:])
            pairs.append(jnp.concatenate(links, 0))
    outs, logs = state[:2]

    bundles = jnp.concatenate([expander, reducer.transpose(0, 2, 1)[:, None]], 1)
    own_expert = route(bundles).swapaxes(0, 1).reshape(3, model_width, hidden)
    expert_weights = lax.all_gather(own_expert, TENSOR, axis=0, tiled=False)
    outs, expert_weights = tied(outs, expert_weights)
    heads = share(outs, TENSOR, shards, 1)
    upstream_rows = send_rows(picked_cotangent)
    heads, upstream_rows = tied(heads, upstream_rows)
    second = inputs + by_rows(
        jnp.einsum("bht,hd->btd", heads, mixing_all, preferred_element_type=f32)
    )

    scale_two = lax.rsqrt(jnp.mean(second * second, -1, keepdims=True) + epsilon)
    hidden_in = (second * scale_two * gains[1]).astype(bf16)
    flat = (trees * rows, model_width)
    flat_hidden = hidden_in.reshape(flat)
    flat_cotangent = cotangent.reshape(flat)
    expert_rows = send_rows(pick_rows(hidden_in))
    expert_rows, shared_bundle = tied(expert_rows, shared_bundle)
    shared_weights = lax.all_gather(
        shared_bundle, GROUP, axis=1, tiled=True
    )
    row_chances = jax.nn.softmax(jnp.dot(expert_rows, router_all, preferred_element_type=f32), -1)
    own_label = jnp.arange(EXPERTS, dtype=jnp.int32) == member_index
    row_gates = jnp.sum(jnp.where(own_label[None], row_chances, 0.0), -1, keepdims=True)
    row_grads = (row_gates * upstream_rows.astype(f32)).astype(bf16)
    lowered, routed_back, expert_wide = gated(expert_rows, row_grads, expert_weights, TILE)
    gate_grads = jnp.sum(upstream_rows.astype(f32) * lowered, -1, keepdims=True)
    lanes = jnp.arange(128, dtype=jnp.int32)[None]
    back_rows = jnp.concatenate(
        [
            routed_back.astype(bf16),
            jnp.where(lanes == member_index, gate_grads, 0.0).astype(bf16),
        ],
        1,
    )
    flat_hidden, row_grads, back_rows = tied(flat_hidden, row_grads, back_rows)
    shared_out, shared_back, shared_wide = gated(
        flat_hidden, flat_cotangent, shared_weights[None], TILE
    )
    expert_parts = weight_parts(
        expert_rows, row_grads, expert_wide, shards, group_size, TILE
    )
    back_rows = bring_rows(back_rows)
    chosen, shared_back = tied(chosen, shared_back)
    returned_back = combine_rows(chosen, back_rows)
    out_rows = (row_gates * lowered).astype(bf16)
    shared_parts = weight_parts(
        flat_hidden, flat_cotangent, shared_wide, 1, group_size, TILE
    )

    def own_rows(field):
        return lax.dynamic_slice_in_dim(field, shard * quarter, quarter, 1)

    def add_shards(field):
        held = field.astype(bf16).reshape(trees, shards, quarter, field.shape[-1])
        step = 1
        while step < shards:
            paired = held.reshape(trees, -1, 2, quarter, field.shape[-1])
            bit = (shard // step) % 2
            kept = lax.dynamic_index_in_dim(paired, bit, 2, keepdims=False)
            sent = lax.dynamic_index_in_dim(paired, 1 - bit, 2, keepdims=False)
            added = kept.astype(f32) + swap(sent, TENSOR, shards, step).astype(f32)
            step *= 2
            held = added.astype(bf16) if step < shards else added
        return held[:, 0]

    def spread_shards(field):
        pieces = share(field[None], TENSOR, shards, 0)
        return jnp.concatenate(
            [pick(pieces, reversed_bits(shard ^ other, shards)) for other in range(shards)], 1
        )

    summed = add_shards(
        returned_back
        + jnp.pad(shared_back.reshape(trees, rows, model_width), ((0, 0), (0, 0), (0, 128)))
    )
    summed, shared_parts, out_rows = tied(summed, shared_parts, out_rows)
    chance_grad = summed[..., model_width : model_width + EXPERTS]
    quarter_second = own_rows(second)
    quarter_scale = own_rows(scale_two)
    quarter_normed = quarter_second * quarter_scale
    quarter_hidden = own_rows(hidden_in)
    logits = jnp.dot(quarter_hidden, router_all, preferred_element_type=f32)
    chances = jax.nn.softmax(logits, -1)
    logit_grad = chances * (chance_grad - jnp.sum(chances * chance_grad, -1, keepdims=True))
    hidden_grad = summed[..., :model_width] + jnp.einsum(
        "bte,de->btd", logit_grad, router_all.astype(f32), precision=highest
    )
    router_part = jnp.einsum(
        "btd,bte->de", quarter_hidden.astype(f32), logit_grad, precision=highest
    )
    gain_two = jnp.sum(hidden_grad * quarter_normed, (0, 1))
    scaled_two = hidden_grad * gains[1]
    second_grad = own_rows(cotangent).astype(f32) + quarter_scale * (
        scaled_two - quarter_normed * jnp.mean(scaled_two * quarter_normed, -1, keepdims=True)
    )
    branch_grad = spread_shards(second_grad.astype(bf16))
    returned_out = combine_rows(chosen, bring_rows(out_rows))
    partial_out = (returned_out + shared_out.reshape(trees, rows, model_width)).astype(bf16)

    heads_grad = jnp.einsum(
        "hd,btd->bht", mixing_own, branch_grad, preferred_element_type=f32
    ).astype(bf16)
    mixing_part = jnp.einsum("btd,bht->dh", branch_grad, outs, preferred_element_type=f32)
    def block_back(number, query_grad):
        return attend_back(
            number,
            bf16 if number == seq_size - 1 else f32,
            place_arg,
            (queries, outs, heads_grad, logs, key_column, path_row, pairs[number]) + query_grad,
        )

    query_grad, pair_grad = block_back(seq_size - 1, ())
    shared_grads = lax.psum_scatter(
        shared_parts[0], GROUP, scatter_dimension=0, tiled=True
    )[0].astype(f32)
    moving = [pair_grad[tree] for tree in range(trees)]
    for step in range(seq_size - 1):
        query_grad, pair_grad = block_back(seq_size - 2 - step, (query_grad,))
        moved = [
            lax.ppermute(grads.astype(bf16), SEQ, [(i + 1, i) for i in range(seq_size - 1)])
            for grads in moving
        ]
        if step == 0:
            *moved, expert_parts = tied(*moved, expert_parts)
            expert_own = lax.psum_scatter(expert_parts, TENSOR, scatter_dimension=0, tiled=False)
        moving = [pair_grad[tree] + moved[tree].astype(f32) for tree in range(trees)]
        if step < seq_size - 2:
            query_grad, *moving = tied(query_grad, *moving)
    own_grads = moving
    pair_grad, shared_grads, partial_out = tied(jnp.stack(own_grads), shared_grads, partial_out)
    output = spread_shards((quarter_second + add_shards(partial_out)).astype(bf16))
    spreader_grad = shared_grads[:2]
    collector_grad = shared_grads[2].T
    query_grad = query_grad * HEAD_DIM ** (-0.5)
    mapped_grad = jnp.concatenate(
        [
            turned(query_grad, cosine, sine, True),
            turned(pair_grad[:, :part_width], cosine, sine, True),
            pair_grad[:, part_width:],
        ],
        1,
    ).astype(bf16)
    first_part = by_rows(
        jnp.einsum("bht,dh->btd", mapped_grad, project_all, preferred_element_type=f32)
    ).astype(bf16)
    first_part, mapped_grad = tied(first_part, mapped_grad)
    first_grad = add_shards(first_part)
    project_part = by_rows(
        jnp.einsum("btd,bht->dh", first_in, mapped_grad, preferred_element_type=f32)
    )
    quarter_scale_one = own_rows(scale_one)
    quarter_normed_one = own_rows(inputs) * quarter_scale_one
    scaled_one = first_grad * gains[0]
    input_grad = spread_shards(
        (
            second_grad
            + quarter_scale_one
            * (
                scaled_one
                - quarter_normed_one * jnp.mean(scaled_one * quarter_normed_one, -1, keepdims=True)
            )
        ).astype(bf16)
    )


    small_parts = jnp.concatenate(
        [
            project_part,
            mixing_part,
            router_part,
            gain_two[:, None],
            jnp.zeros((model_width, -(4 * part_width + EXPERTS + 1) % 128), f32),
        ],
        1,
    ).astype(bf16)
    small_home = route(small_parts.reshape(group_size, owned, -1))
    small_home, expert_own = tied(small_home, expert_own)
    expert_grads = route(expert_own).astype(f32)
    expander_grad = expert_grads[:, :2]
    reducer_grad = expert_grads[:, 2].transpose(0, 2, 1)
    small_grads = jnp.sum(
        small_home.astype(f32),
        0,
    )
    project_grad = (
        small_grads[:, : 3 * part_width].reshape(owned, 3, part_width).transpose(1, 0, 2)
    )
    mixing_grad = small_grads[:, 3 * part_width : 4 * part_width].T
    rest = small_grads[:, 4 * part_width : 4 * part_width + EXPERTS + 1]
    gain_one = jnp.sum(project_grad * project.astype(f32), (0, 2)) / norm_gains[0].astype(f32)
    tiny = lax.psum(
        jnp.concatenate([rest.T, gain_one[None]], 0),
        TENSOR,
    )
    tiny, input_grad = tied(tiny, input_grad)
    router_grad = tiny[:EXPERTS].T
    gain_grad = jnp.stack([tiny[EXPERTS + 1], tiny[EXPERTS]])
    return (
        output,
        input_grad,
        gain_grad,
        project_grad,
        mixing_grad,
        router_grad,
        expander_grad,
        reducer_grad,
        spreader_grad,
        collector_grad,
    )


def solution(mesh):
    in_specs = (
        P(DP, SEQ, None),
        P(DP, SEQ, None),
        P(DP, None),
        P(DP, None),
        P(DP, SEQ, None),
        P(None, GROUP),
        P(None, GROUP, TENSOR),
        P(TENSOR, GROUP),
        P(GROUP, None),
        P(None, None, GROUP, TENSOR),
        P(None, TENSOR, GROUP),
        P(None, GROUP, TENSOR),
        P(TENSOR, GROUP),
    )
    out_specs = (
        P(DP, SEQ, None),
        P(DP, SEQ, None),
        P(None, GROUP),
        P(None, GROUP, TENSOR),
        P(TENSOR, GROUP),
        P(GROUP, None),
        P(None, None, GROUP, TENSOR),
        P(None, TENSOR, GROUP),
        P(None, GROUP, TENSOR),
        P(TENSOR, GROUP),
    )
    sizes = mesh.shape
    group_size = sizes[DP] * sizes[SEQ]
    shards = sizes[TENSOR]
    fits = group_size == EXPERTS and shards & (shards - 1) == 0 and CAP % shards == 0
    body = local_fast if fits else local
    return jax.shard_map(body, mesh=mesh, in_specs=in_specs, out_specs=out_specs, check_vma=False)
```

```python
import functools
import math
import types

import jax
import jax.numpy as jnp
from jax import lax
from jax.experimental import pallas as pl
from jax.experimental.layout import Layout, with_layout_constraint
from jax.experimental.pallas import tpu as pltpu
from jax.sharding import PartitionSpec as P

HEAD_DIM = 64
EXPERTS = 8
CAP = 192
QB = 512
DP = "dp"
SEQ = "seq"
TENSOR = "tensor"
GROUP = (DP, SEQ)


epsilon = 1e-05
theta = 10000.0
highest = lax.Precision.HIGHEST


def ancestry(parents):
    labels = jnp.arange(parents.shape[0], dtype=jnp.int32)
    grandparent = jnp.take(parents, parents)
    itself = labels[:, None] == labels[None, :]
    return (
        itself | (parents[:, None] == labels[None, :]) | (grandparent[:, None] == labels[None, :])
    )


def positions(segments, table):
    labels = jnp.arange(table.shape[0], dtype=jnp.int32)
    member = (segments[:, None] == labels[None, :]).astype(jnp.int32)
    lengths = jnp.sum(member, 0)
    offsets = jnp.cumsum(lengths) - lengths
    ancestral = jnp.sum(table.astype(jnp.int32) * lengths[None, :], 1) - lengths
    moving = ancestral - offsets
    return jnp.arange(segments.shape[0], dtype=jnp.int32) + jnp.sum(member * moving[None, :], 1)


def visible(row_segments, row_index, key_segments, key_index, table):
    labels = jnp.arange(table.shape[0], dtype=jnp.int32)
    member_rows = (row_segments[:, None] == labels[None, :]).astype(jnp.bfloat16)
    member_keys = (key_segments[:, None] == labels[None, :]).astype(jnp.bfloat16)
    reach = jnp.dot(member_rows, table.astype(jnp.bfloat16), preferred_element_type=jnp.float32)
    hits = jnp.einsum(
        "bs,ls->bl", reach.astype(jnp.bfloat16), member_keys, preferred_element_type=jnp.float32
    )
    return (hits > 0.5) & (key_index[None, :] <= row_index[:, None])


def turn(field, place, backward):
    half = field.shape[-1] // 2
    rates = jnp.exp(-math.log(theta) * 2.0 * jnp.arange(half, dtype=jnp.float32) / field.shape[-1])
    angle = place[:, None] * rates[None, :]
    cosine = jnp.cos(angle)[:, None, :]
    sine = jnp.sin(angle)[:, None, :]
    first_half = field[..., :half]
    second_half = field[..., half:]
    if backward:
        return jnp.concatenate(
            [first_half * cosine + second_half * sine, second_half * cosine - first_half * sine], -1
        )
    return jnp.concatenate(
        [first_half * cosine - second_half * sine, second_half * cosine + first_half * sine], -1
    )


def slot_of(route_flat):
    labels = jnp.arange(EXPERTS, dtype=jnp.int32)
    member = (route_flat[:, None] == labels[None, :]).astype(jnp.int32)
    ranks = jnp.cumsum(member, 0) - 1
    return route_flat * CAP + jnp.sum(ranks * member, 1)


def owner_of(slot_ids, count_rows, per_row):
    picked = jnp.arange(slot_ids.shape[0], dtype=jnp.int32) // per_row
    return jnp.full((EXPERTS * CAP,), count_rows, jnp.int32).at[slot_ids].set(picked)


def silu_slope(value):
    sigma = jax.nn.sigmoid(value)
    return sigma * (1.0 + value * (1.0 - sigma))


def block_scores(query_block, key_block, seg_block, index_block, key_segments, key_index, table):
    seen = visible(seg_block, index_block, key_segments, key_index, table)
    raw = jnp.einsum("bhd,lhd->hbl", query_block, key_block, preferred_element_type=jnp.float32)
    return jnp.where(seen[None], raw * HEAD_DIM ** (-0.5), -1e30)


def fetch(norm_gains, project, mixing, router, expander, reducer, spreader, collector):
    return (
        lax.all_gather(norm_gains, GROUP, axis=1, tiled=True),
        lax.all_gather(project, GROUP, axis=1, tiled=True),
        lax.all_gather(mixing, GROUP, axis=1, tiled=True),
        lax.all_gather(router, GROUP, axis=0, tiled=True),
        lax.all_gather(expander, GROUP, axis=2, tiled=True),
        lax.all_gather(reducer, GROUP, axis=2, tiled=True),
        lax.all_gather(spreader, GROUP, axis=1, tiled=True),
        lax.all_gather(collector, GROUP, axis=1, tiled=True),
    )


def reduce_end(grads):
    (
        gain_part,
        project_part,
        mixing_part,
        router_part,
        expander_part,
        reducer_part,
        spreader_part,
        collector_part,
    ) = grads
    return (
        lax.psum_scatter(gain_part, GROUP, scatter_dimension=1, tiled=True),
        lax.psum_scatter(project_part, GROUP, scatter_dimension=1, tiled=True),
        lax.psum_scatter(mixing_part, GROUP, scatter_dimension=1, tiled=True),
        lax.psum_scatter(router_part, GROUP, scatter_dimension=0, tiled=True),
        lax.psum_scatter(expander_part, GROUP, scatter_dimension=2, tiled=True),
        lax.psum_scatter(reducer_part, GROUP, scatter_dimension=2, tiled=True),
        lax.psum_scatter(spreader_part, GROUP, scatter_dimension=1, tiled=True),
        lax.psum_scatter(collector_part, GROUP, scatter_dimension=1, tiled=True),
    )


def forward_pass(tree_tokens, tree_segments, tree_parents, tree_routes, weights, offset):
    norm_gains, project, mixing, router, expander, reducer, spreader, collector = weights
    row_count = tree_tokens.shape[0]
    model_width = tree_tokens.shape[1]
    tree_length = tree_segments.shape[0]
    local_heads = project.shape[2] // HEAD_DIM
    table = ancestry(tree_parents)
    place = lax.dynamic_slice_in_dim(positions(tree_segments, table), offset, row_count).astype(
        jnp.float32
    )
    row_segments = lax.dynamic_slice_in_dim(tree_segments, offset, row_count)
    row_index = offset + jnp.arange(row_count, dtype=jnp.int32)
    key_index = jnp.arange(tree_length, dtype=jnp.int32)
    inputs = tree_tokens.astype(jnp.float32)
    scale_one = lax.rsqrt(jnp.mean(inputs * inputs, -1, keepdims=True) + epsilon)
    normed_one = inputs * scale_one
    first_in = (normed_one * norm_gains[0].astype(jnp.float32)).astype(jnp.bfloat16)
    mapped = jnp.einsum("td,cdh->cth", first_in, project, preferred_element_type=jnp.float32)
    head_shape = (row_count, local_heads, HEAD_DIM)
    queries = turn(mapped[0].reshape(head_shape), place, False).astype(jnp.bfloat16)
    keys_own = (
        turn(mapped[1].reshape(head_shape), place, False)
        .astype(jnp.bfloat16)
        .reshape(row_count, -1)
    )
    values_own = mapped[2].astype(jnp.bfloat16)
    keys_flat, values_flat = (
        lax.all_gather(keys_own, SEQ, axis=0, tiled=True),
        lax.all_gather(values_own, SEQ, axis=0, tiled=True),
    )
    keys_all = keys_flat.reshape(tree_length, local_heads, HEAD_DIM)
    values_all = values_flat.reshape(tree_length, local_heads, HEAD_DIM)
    blocks = row_count // QB
    query_blocks = queries.reshape(blocks, QB, local_heads, HEAD_DIM)
    seg_blocks = row_segments.reshape(blocks, QB)
    index_blocks = row_index.reshape(blocks, QB)

    def attend(entries):
        query_block, seg_block, index_block = entries
        scores = block_scores(
            query_block, keys_all, seg_block, index_block, tree_segments, key_index, table
        )
        row_peak = jnp.max(scores, -1, keepdims=True)
        expo = jnp.exp(scores - row_peak)
        row_total = jnp.sum(expo, -1, keepdims=True)
        chances_soft = expo / row_total
        mixed_block = jnp.einsum(
            "hbl,lhd->bhd",
            chances_soft.astype(jnp.bfloat16),
            values_all,
            preferred_element_type=jnp.float32,
        )
        return (mixed_block, (row_peak + jnp.log(row_total))[..., 0])

    mixed, log_totals = lax.map(attend, (query_blocks, seg_blocks, index_blocks))
    heads_out = mixed.reshape(row_count, -1).astype(jnp.bfloat16)
    attended = lax.psum(
        jnp.dot(heads_out, mixing, preferred_element_type=jnp.float32).astype(jnp.bfloat16),
        TENSOR,
    ).astype(jnp.float32)
    second = inputs + attended
    scale_two = lax.rsqrt(jnp.mean(second * second, -1, keepdims=True) + epsilon)
    normed_two = second * scale_two
    hidden_in = (normed_two * norm_gains[1].astype(jnp.float32)).astype(jnp.bfloat16)
    logits = jnp.dot(hidden_in, router, preferred_element_type=jnp.float32)
    shifted = jnp.exp(logits - jnp.max(logits, -1, keepdims=True))
    chances = shifted / jnp.sum(shifted, -1, keepdims=True)
    picks = (tree_routes[:, :, None] == jnp.arange(EXPERTS, dtype=jnp.int32)[None, None, :]).astype(
        jnp.float32
    )
    gates = jnp.sum(picks * chances[:, None, :], -1)
    per_row = tree_routes.shape[1]
    slot_ids = slot_of(tree_routes.reshape(-1))
    owners = owner_of(slot_ids, row_count, per_row)
    padded = jnp.concatenate([hidden_in, jnp.zeros((1, model_width), jnp.bfloat16)], 0)
    routed = jnp.take(padded, owners, axis=0).reshape(EXPERTS, CAP, model_width)
    raised = jnp.einsum("ecd,egdf->gecf", routed, expander, preferred_element_type=jnp.float32)
    activated = (jax.nn.silu(raised[0]) * raised[1]).astype(jnp.bfloat16)
    lowered = jnp.einsum(
        "ecf,efd->ecd", activated, reducer, preferred_element_type=jnp.float32
    ).reshape(EXPERTS * CAP, model_width)
    returned = jnp.take(lowered, slot_ids, axis=0).reshape(row_count, per_row, model_width)
    blended = jnp.sum(gates[:, :, None] * returned, 1)
    spread = jnp.einsum("td,gdf->gtf", hidden_in, spreader, preferred_element_type=jnp.float32)
    common = (jax.nn.silu(spread[0]) * spread[1]).astype(jnp.bfloat16)
    shared_out = jnp.dot(common, collector, preferred_element_type=jnp.float32)
    branches = lax.psum((blended + shared_out).astype(jnp.bfloat16), TENSOR).astype(jnp.float32)
    output_tree = (second + branches).astype(jnp.bfloat16)
    kept = types.SimpleNamespace(
        table=table,
        place=place,
        offset=offset,
        row_segments=row_segments,
        seg_blocks=seg_blocks,
        index_blocks=index_blocks,
        scale_one=scale_one,
        normed_one=normed_one,
        first_in=first_in,
        queries=queries,
        query_blocks=query_blocks,
        keys_all=keys_all,
        values_all=values_all,
        log_totals=log_totals,
        heads_out=heads_out,
        scale_two=scale_two,
        normed_two=normed_two,
        hidden_in=hidden_in,
        chances=chances,
        picks=picks,
        gates=gates,
        slot_ids=slot_ids,
        routed=routed,
        raised=raised,
        activated=activated,
        returned=returned,
        spread=spread,
        common=common,
    )
    return (kept, output_tree)


def backward_pass(tree_cot, tree_segments, kept, weights):
    norm_gains, project, mixing, router, expander, reducer, spreader, collector = weights
    upstream = tree_cot.astype(jnp.float32)
    row_count = upstream.shape[0]
    model_width = upstream.shape[1]
    shared_grad = upstream.astype(jnp.bfloat16)
    common_grad = jnp.einsum(
        "td,fd->tf", shared_grad, collector, preferred_element_type=jnp.float32
    )
    collector_part = jnp.einsum(
        "tf,td->fd", kept.common, shared_grad, preferred_element_type=jnp.float32
    )
    spread = kept.spread
    spread_grad = jnp.stack(
        [common_grad * spread[1] * silu_slope(spread[0]), common_grad * jax.nn.silu(spread[0])]
    ).astype(jnp.bfloat16)
    spreader_part = jnp.einsum(
        "td,gtf->gdf", kept.hidden_in, spread_grad, preferred_element_type=jnp.float32
    )
    hidden_grad = jnp.einsum(
        "gtf,gdf->td", spread_grad, spreader, preferred_element_type=jnp.float32
    )
    gates = kept.gates
    slot_ids = kept.slot_ids
    per_row = gates.shape[1]
    pair_grad = (
        (gates[:, :, None] * upstream[:, None, :])
        .astype(jnp.bfloat16)
        .reshape(row_count * per_row, model_width)
    )
    lowered_grad = (
        jnp.zeros((EXPERTS * CAP, model_width), jnp.bfloat16)
        .at[slot_ids]
        .set(pair_grad)
        .reshape(EXPERTS, CAP, model_width)
    )
    activated_grad = jnp.einsum(
        "ecd,efd->ecf", lowered_grad, reducer, preferred_element_type=jnp.float32
    )
    reducer_part = jnp.einsum(
        "ecf,ecd->efd", kept.activated, lowered_grad, preferred_element_type=jnp.float32
    )
    raised = kept.raised
    raised_grad = jnp.stack(
        [
            activated_grad * raised[1] * silu_slope(raised[0]),
            activated_grad * jax.nn.silu(raised[0]),
        ]
    ).astype(jnp.bfloat16)
    expander_part = jnp.einsum(
        "ecd,gecf->egdf", kept.routed, raised_grad, preferred_element_type=jnp.float32
    )
    routed_grad = jnp.einsum(
        "gecf,egdf->ecd", raised_grad, expander, preferred_element_type=jnp.float32
    ).reshape(EXPERTS * CAP, model_width)
    hidden_grad = hidden_grad + jnp.sum(
        jnp.take(routed_grad, slot_ids, axis=0).reshape(row_count, per_row, model_width), 1
    )
    gate_grad = jnp.sum(upstream[:, None, :] * kept.returned, -1)
    hidden_grad, gate_grad = (
        lax.psum(hidden_grad.astype(jnp.bfloat16), TENSOR).astype(jnp.float32),
        lax.psum(gate_grad.astype(jnp.bfloat16), TENSOR).astype(jnp.float32),
    )
    chances = kept.chances
    chance_grad = jnp.sum(kept.picks * gate_grad[:, :, None], 1)
    logit_grad = chances * (chance_grad - jnp.sum(chances * chance_grad, -1, keepdims=True))
    hidden_grad = hidden_grad + jnp.dot(logit_grad, router.astype(jnp.float32).T, precision=highest)
    router_part = jnp.dot(kept.hidden_in.astype(jnp.float32).T, logit_grad, precision=highest)
    normed_two = kept.normed_two
    gain_two = jnp.sum(hidden_grad * normed_two, 0)
    scaled_two = hidden_grad * norm_gains[1].astype(jnp.float32)
    second_grad = upstream + kept.scale_two * (
        scaled_two - normed_two * jnp.mean(scaled_two * normed_two, -1, keepdims=True)
    )
    branch_grad = second_grad.astype(jnp.bfloat16)
    mixing_part = jnp.einsum(
        "th,td->hd", kept.heads_out, branch_grad, preferred_element_type=jnp.float32
    )
    heads_grad = jnp.einsum(
        "td,hd->th", branch_grad, mixing, preferred_element_type=jnp.float32
    ).astype(jnp.bfloat16)
    keys_all = kept.keys_all
    values_all = kept.values_all
    table = kept.table
    query_blocks = kept.query_blocks
    tree_length = keys_all.shape[0]
    local_heads = keys_all.shape[1]
    key_index = jnp.arange(tree_length, dtype=jnp.int32)
    grad_blocks = heads_grad.reshape(query_blocks.shape)
    factor = HEAD_DIM ** (-0.5)

    def attend_back(carry, entries):
        keys_grad, values_grad = carry
        query_block, grad_block, log_block, seg_block, index_block = entries
        scores = block_scores(
            query_block, keys_all, seg_block, index_block, tree_segments, key_index, table
        )
        chances_soft = jnp.exp(scores - log_block[..., None])
        prob_grad = jnp.einsum(
            "bhd,lhd->hbl", grad_block, values_all, preferred_element_type=jnp.float32
        )
        centre = jnp.sum(chances_soft * prob_grad, -1, keepdims=True)
        score_grad = (chances_soft * (prob_grad - centre) * factor).astype(jnp.bfloat16)
        query_grad_block = jnp.einsum(
            "hbl,lhd->bhd", score_grad, keys_all, preferred_element_type=jnp.float32
        )
        keys_grad = keys_grad + jnp.einsum(
            "hbl,bhd->lhd", score_grad, query_block, preferred_element_type=jnp.float32
        )
        values_grad = values_grad + jnp.einsum(
            "hbl,bhd->lhd",
            chances_soft.astype(jnp.bfloat16),
            grad_block,
            preferred_element_type=jnp.float32,
        )
        return ((keys_grad, values_grad), query_grad_block)

    zero_kv = jnp.zeros((tree_length, local_heads, HEAD_DIM), jnp.float32)
    (keys_grad, values_grad), query_grad = lax.scan(
        attend_back,
        (zero_kv, zero_kv),
        (query_blocks, grad_blocks, kept.log_totals, kept.seg_blocks, kept.index_blocks),
    )
    keys_own_grad, values_own_grad = (
        lax.psum_scatter(
            keys_grad.reshape(tree_length, -1).astype(jnp.bfloat16),
            SEQ,
            scatter_dimension=0,
            tiled=True,
        ).astype(jnp.float32),
        lax.psum_scatter(
            values_grad.reshape(tree_length, -1).astype(jnp.bfloat16),
            SEQ,
            scatter_dimension=0,
            tiled=True,
        ).astype(jnp.float32),
    )
    place = kept.place
    query_back = turn(query_grad.reshape(row_count, local_heads, HEAD_DIM), place, True).reshape(
        row_count, -1
    )
    key_back = turn(keys_own_grad.reshape(row_count, local_heads, HEAD_DIM), place, True).reshape(
        row_count, -1
    )
    mapped_grad = jnp.stack([query_back, key_back, values_own_grad]).astype(jnp.bfloat16)
    project_part = jnp.einsum(
        "td,cth->cdh", kept.first_in, mapped_grad, preferred_element_type=jnp.float32
    )
    first_grad = lax.psum(
        jnp.einsum("cth,cdh->td", mapped_grad, project, preferred_element_type=jnp.float32).astype(
            jnp.bfloat16
        ),
        TENSOR,
    ).astype(jnp.float32)
    normed_one = kept.normed_one
    gain_one = jnp.sum(first_grad * normed_one, 0)
    scaled_one = first_grad * norm_gains[0].astype(jnp.float32)
    input_tree = (
        second_grad
        + kept.scale_one
        * (scaled_one - normed_one * jnp.mean(scaled_one * normed_one, -1, keepdims=True))
    ).astype(jnp.bfloat16)
    gain_part = jnp.stack([gain_one, gain_two])
    return (
        input_tree,
        (
            gain_part,
            project_part,
            mixing_part,
            router_part,
            expander_part,
            reducer_part,
            spreader_part,
            collector_part,
        ),
    )


def local(
    tokens,
    cotangent,
    segments,
    parents,
    routes,
    norm_gains,
    project,
    mixing,
    router,
    expander,
    reducer,
    spreader,
    collector,
):
    tree_count = tokens.shape[0]
    offset = lax.axis_index(SEQ) * tokens.shape[1]
    outputs = []
    input_grads = []
    running = None
    for tree_index in range(tree_count):
        forward_weights = fetch(
            norm_gains, project, mixing, router, expander, reducer, spreader, collector
        )
        kept, output_tree = forward_pass(
            tokens[tree_index],
            segments[tree_index],
            parents[tree_index],
            routes[tree_index],
            forward_weights,
            offset,
        )
        backward_weights = fetch(
            norm_gains, project, mixing, router, expander, reducer, spreader, collector
        )
        input_tree, tree_grads = backward_pass(
            cotangent[tree_index], segments[tree_index], kept, backward_weights
        )
        outputs.append(output_tree)
        input_grads.append(input_tree)
        if running is None:
            running = tree_grads
        else:
            running = tuple((before + addend for before, addend in zip(running, tree_grads)))
    running = reduce_end(running)
    return (
        jnp.stack(outputs),
        jnp.stack(input_grads),
        running[0],
        running[1],
        running[2],
        running[3],
        running[4],
        running[5],
        running[6],
        running[7],
    )


VMEM_BYTES = 56 << 20
TILE = 256
ROWS = 256


def contract(left, right, left_dim, right_dim):
    return lax.dot_general(
        left, right, (((left_dim,), (right_dim,)), ((), ())), preferred_element_type=jnp.float32
    )


def spans(head, width):
    if isinstance(head, int):
        start = head * HEAD_DIM
    else:
        start = pl.multiple_of(head * HEAD_DIM, HEAD_DIM)
    return (pl.ds(start, HEAD_DIM), pl.ds(width + start, HEAD_DIM), pl.ds(head, 1))


def scores_of(keys, queries, seen):
    return jnp.where(seen, contract(keys, queries, 0, 0), -1e30)


def seen_block(number, place_ref, key_bits_ref, query_bits, length):
    start = pl.multiple_of((place_ref[0] - number) * length, length)
    seen = (key_bits_ref[pl.ds(start, length), :] & query_bits) != 0
    if number == 0:
        keys = lax.broadcasted_iota(jnp.int32, seen.shape, 0)
        rows = lax.broadcasted_iota(jnp.int32, seen.shape, 1)
        seen = seen & (keys <= rows)
    return seen


def attend_kernel(number, final, heads, place_ref, query_ref, key_bits_ref, query_bits_ref, *refs):
    pair_ref = refs[0]
    if number:
        old_peak_ref, old_total_ref, old_mixed_ref = refs[1:4]
    peak_ref, total_ref, mixed_ref = refs[-3:]
    length = query_ref.shape[1]
    width = heads * HEAD_DIM

    def block():
        seen = seen_block(number, place_ref, key_bits_ref, query_bits_ref[...], length)

        def one(head, _):
            span, value_span, row = spans(head, width)
            scores = scores_of(pair_ref[span, :], query_ref[span, :], seen)
            peak = jnp.max(scores, 0, keepdims=True)
            if number:
                before = old_peak_ref[row, :]
                peak = jnp.maximum(before, peak)
                shrink = jnp.exp(before - peak)
            expo = jnp.exp(scores - peak)
            total = jnp.sum(expo, 0, keepdims=True)
            mixed = jnp.dot(
                pair_ref[value_span, :],
                expo.astype(jnp.bfloat16),
                preferred_element_type=jnp.float32,
            )
            if number:
                total = total + shrink * old_total_ref[row, :]
                mixed = mixed + shrink * old_mixed_ref[span, :]
            peak_ref[row, :] = peak
            total_ref[row, :] = total
            mixed_ref[span, :] = mixed
            return 0

        lax.fori_loop(0, heads, one, 0)

    def keep():
        peak_ref[...] = old_peak_ref[...]
        total_ref[...] = old_total_ref[...]
        mixed_ref[...] = old_mixed_ref[...]

    if number:
        pl.when(place_ref[0] >= number)(block)
        pl.when(place_ref[0] < number)(keep)
    else:
        block()
    if final:
        out_ref, log_ref = refs[4:6]
        for head in range(heads):
            span, _, row = spans(head, width)
            out_ref[span, :] = (mixed_ref[span, :] / total_ref[row, :]).astype(out_ref.dtype)
            log_ref[row, :] = peak_ref[row, :] + jnp.log(total_ref[row, :])


def attend_back_kernel(
    number,
    heads,
    place_ref,
    query_ref,
    out_ref,
    grad_ref,
    log_ref,
    key_bits_ref,
    query_bits_ref,
    pair_ref,
    *refs
):
    query_grad_ref, pair_grad_ref = refs[-2:]
    length = query_ref.shape[1]
    width = heads * HEAD_DIM

    def block():
        seen = seen_block(number, place_ref, key_bits_ref, query_bits_ref[...], length)

        def one(head, _):
            span, value_span, row = spans(head, width)
            queries = query_ref[span, :]
            grads = grad_ref[span, :]
            keys = pair_ref[span, :]
            centre = jnp.sum(
                grads.astype(jnp.float32) * out_ref[span, :].astype(jnp.float32), 0, keepdims=True
            )
            chances = jnp.exp(scores_of(keys, queries, seen) - log_ref[row, :])
            prob_grad = contract(pair_ref[value_span, :], grads, 0, 0)
            score_grad = (chances * (prob_grad - centre)).astype(jnp.bfloat16)
            value_grad = contract(grads, chances.astype(jnp.bfloat16), 1, 1)
            key_grad = contract(queries, score_grad, 1, 1)
            query_grad = jnp.dot(keys, score_grad, preferred_element_type=jnp.float32)
            pair_grad_ref[span, :] = key_grad.astype(pair_grad_ref.dtype)
            pair_grad_ref[value_span, :] = value_grad.astype(pair_grad_ref.dtype)
            if len(refs) > 2:
                query_grad = query_grad + refs[0][span, :]
            query_grad_ref[span, :] = query_grad
            return 0

        lax.fori_loop(0, heads, one, 0)

    def empty():
        pair_grad_ref[...] = jnp.zeros_like(pair_grad_ref)
        if len(refs) > 2:
            query_grad_ref[...] = refs[0][...]
        else:
            query_grad_ref[...] = jnp.zeros_like(query_grad_ref)

    if number:
        pl.when(place_ref[0] >= number)(block)
        pl.when(place_ref[0] < number)(empty)
    else:
        block()


def per_tree(array):
    return pl.BlockSpec((None,) + array.shape[1:], lambda tree: (tree, 0, 0))


def attend_call(kernel, name, place, operands, results, flops):
    trees, width, length = operands[0].shape
    return pl.pallas_call(
        kernel,
        grid=(trees,),
        out_shape=results,
        in_specs=[pl.BlockSpec(memory_space=pltpu.SMEM)] + [per_tree(value) for value in operands],
        out_specs=tuple(per_tree(value) for value in results),
        compiler_params=pltpu.CompilerParams(vmem_limit_bytes=VMEM_BYTES),
        cost_estimate=pl.CostEstimate(
            flops=flops * trees * width * length * length,
            transcendentals=trees * width * length * length // HEAD_DIM,
            bytes_accessed=16 * trees * width * length,
        ),
        name=name,
    )(place, *operands)


def attend(number, final, place, queries, key_bits, query_bits, pair, state):
    trees, width, length = queries.shape
    heads = width // HEAD_DIM
    row = jax.ShapeDtypeStruct((trees, heads, length), jnp.float32)
    field = jax.ShapeDtypeStruct(queries.shape, jnp.float32)
    results = (row, row, field)
    if final:
        results = (jax.ShapeDtypeStruct(queries.shape, jnp.bfloat16), row) + results
    return attend_call(
        functools.partial(attend_kernel, number, final, heads),
        "attend",
        place,
        (queries, key_bits, query_bits, pair) + tuple(state),
        results,
        16,
    )


def attend_back(number, kind, place, operands):
    trees, width, length = operands[0].shape
    heads = width // HEAD_DIM
    return attend_call(
        functools.partial(attend_back_kernel, number, heads),
        "attend_back",
        place,
        operands,
        (
            jax.ShapeDtypeStruct((trees, width, length), jnp.float32),
            jax.ShapeDtypeStruct((trees, 2 * width, length), kind),
        ),
        40,
    )


def gated_kernel(
    rows_ref, grads_ref, weights_ref, lowered_ref, routed_ref, first_ref, second_ref, active_ref
):
    @pl.when(pl.program_id(0) == 0)
    def _():
        lowered_ref[...] = jnp.zeros_like(lowered_ref)
        routed_ref[...] = jnp.zeros_like(routed_ref)

    def some(index, _):
        part = (pl.ds(pl.multiple_of(index * ROWS, ROWS), ROWS), slice(None))
        rows = rows_ref[part]
        grads = grads_ref[part]
        gate_weights = weights_ref[0, 0]
        up_weights = weights_ref[0, 1]
        down_weights = weights_ref[0, 2]
        first = jnp.dot(rows, gate_weights, preferred_element_type=jnp.float32)
        second = jnp.dot(rows, up_weights, preferred_element_type=jnp.float32)
        sigma = 1.0 / (1.0 + jnp.exp(-first))
        swish = first * sigma
        activated = (swish * second).astype(jnp.bfloat16)
        activated_grad = jnp.dot(grads, down_weights, preferred_element_type=jnp.float32)
        first_grad = (activated_grad * second * (sigma + swish * (1.0 - sigma))).astype(
            jnp.bfloat16
        )
        second_grad = (activated_grad * swish).astype(jnp.bfloat16)
        lowered_ref[part] += contract(activated, down_weights, 1, 1)
        routed_ref[part] += contract(first_grad, gate_weights, 1, 1) + contract(
            second_grad, up_weights, 1, 1
        )
        first_ref[part] = first_grad
        second_ref[part] = second_grad
        active_ref[part] = activated
        return 0

    lax.fori_loop(0, rows_ref.shape[0] // ROWS, some, 0)


def gated(rows, grads, weights, tile):
    count, model_width = rows.shape
    chunks, _, _, hidden = weights.shape
    tiles = hidden // tile
    fixed = pl.BlockSpec((count, model_width), lambda step: (0, 0))
    moving = pl.BlockSpec(
        (1, 3, model_width, tile), lambda step: (step // tiles, 0, 0, step % tiles)
    )
    column = pl.BlockSpec((count, tile), lambda step: (0, step))
    field = jax.ShapeDtypeStruct((count, model_width), jnp.float32)
    wide = jax.ShapeDtypeStruct((count, chunks * hidden), jnp.bfloat16)
    results = pl.pallas_call(
        gated_kernel,
        grid=(chunks * tiles,),
        out_shape=(field, field, wide, wide, wide),
        in_specs=[fixed, fixed, moving],
        out_specs=(fixed, fixed, column, column, column),
        compiler_params=pltpu.CompilerParams(vmem_limit_bytes=VMEM_BYTES),
        cost_estimate=pl.CostEstimate(
            flops=12 * count * model_width * chunks * hidden,
            transcendentals=count * chunks * hidden,
            bytes_accessed=12 * count * model_width + 6 * (count + model_width) * chunks * hidden,
        ),
        name="gated",
    )(rows, grads, weights)
    return (results[0], results[1], results[2:])


def parts_kernel(
    rows_ref, grads_ref, first_ref, second_ref, active_ref, parts_ref, turned_rows, turned_grads
):
    owned = parts_ref.shape[3]

    @pl.when(pl.program_id(0) == 0)
    def _():
        turned_rows[...] = rows_ref[...].T
        turned_grads[...] = grads_ref[...].T

    def some(index, _):
        part = (pl.ds(pl.multiple_of(index * 2 * owned, 2 * owned), 2 * owned), slice(None))
        rows = turned_rows[part]
        results = (
            contract(rows, first_ref[...], 1, 0),
            contract(rows, second_ref[...], 1, 0),
            contract(turned_grads[part], active_ref[...], 1, 0),
        )
        for kind, result in enumerate(results):
            for half in range(2):
                piece = result[half * owned : (half + 1) * owned]
                parts_ref[0, 2 * index + half, kind] = piece.astype(jnp.bfloat16)
        return 0

    lax.fori_loop(0, parts_ref.shape[1] // 2, some, 0)


def weight_parts(rows, grads, wide, chunks, owners, tile):
    count, model_width = rows.shape
    hidden = wide[0].shape[1] // chunks
    tiles = hidden // tile
    owned = model_width // owners
    fixed = pl.BlockSpec((count, model_width), lambda step: (0, 0))
    column = pl.BlockSpec((count, tile), lambda step: (0, step))
    return pl.pallas_call(
        parts_kernel,
        grid=(chunks * tiles,),
        out_shape=jax.ShapeDtypeStruct((chunks, owners, 3, owned, hidden), jnp.bfloat16),
        in_specs=[fixed, fixed, column, column, column],
        out_specs=pl.BlockSpec(
            (1, owners, 3, owned, tile), lambda step: (step // tiles, 0, 0, 0, step % tiles)
        ),
        scratch_shapes=[pltpu.VMEM((model_width, count), jnp.bfloat16)] * 2,
        compiler_params=pltpu.CompilerParams(vmem_limit_bytes=VMEM_BYTES),
        cost_estimate=pl.CostEstimate(
            flops=6 * count * model_width * chunks * hidden,
            transcendentals=0,
            bytes_accessed=4 * count * model_width + 6 * (count + model_width) * chunks * hidden,
        ),
        name="weight_parts",
    )(rows, grads, *wide)


def swap(piece, axes, size, step):
    return lax.ppermute(piece, axes, [(i, i ^ step) for i in range(size)])


def pick(stacked, index):
    return lax.dynamic_index_in_dim(stacked, index, 0, keepdims=False)


def share(piece, axes, size, dim):
    step = size // 2
    while step:
        piece = jnp.concatenate([piece, swap(piece, axes, size, step)], dim)
        step //= 2
    return piece


def reversed_bits(index, size):
    bits = size.bit_length() - 1
    return sum(((index >> bit) & 1) << (bits - 1 - bit) for bit in range(bits))


def tied(*values):
    return lax.optimization_barrier(values)


def route(blocks):
    return lax.all_to_all(blocks, GROUP, split_axis=0, concat_axis=0)


def by_rows(field):
    order = tuple(range(field.ndim))
    return with_layout_constraint(field, Layout(major_to_minor=order))


def turned(field, cosine, sine, backward):
    half = HEAD_DIM // 2
    shape = field.shape
    split = field.reshape(shape[0], -1, 2, half, shape[-1])
    first_half = split[:, :, 0]
    second_half = split[:, :, 1]
    if backward:
        parts = [
            first_half * cosine + second_half * sine,
            second_half * cosine - first_half * sine,
        ]
    else:
        parts = [
            first_half * cosine - second_half * sine,
            second_half * cosine + first_half * sine,
        ]
    return jnp.stack(parts, 2).reshape(shape)


def tree_tables(segments, parents):
    count = parents.shape[1]
    labels = jnp.arange(count, dtype=jnp.int32)
    is_parent = parents[:, :, None] == labels[None, None, :]
    grand = jnp.sum(jnp.where(is_parent, parents[:, None, :], 0), 2)
    itself = labels[None, :, None] == labels[None, None, :]
    table = itself | is_parent | (grand[:, :, None] == labels[None, None, :])
    member = segments[:, None, :] == labels[None, :, None]
    lengths = jnp.sum(member.astype(jnp.int32), 2)
    ahead = jnp.sum(jnp.where(labels[:, None] > labels[None, :], lengths[:, None, :], 0), 2)
    moving = jnp.sum(jnp.where(table, lengths[:, None, :], 0), 2) - lengths - ahead
    place = jnp.arange(segments.shape[1], dtype=jnp.int32) + jnp.sum(
        jnp.where(member, moving[:, :, None], 0), 1
    )
    bits = jnp.sum(jnp.where(table, jnp.left_shift(1, labels)[None, None, :], 0), 2)
    paths = jnp.sum(jnp.where(member, bits[:, :, None], 0), 1)
    return (place, paths, jnp.left_shift(1, segments))


def local_fast(
    tokens,
    cotangent,
    segments,
    parents,
    routes,
    norm_gains,
    project,
    mixing,
    router,
    expander,
    reducer,
    spreader,
    collector,
):
    bf16, f32 = jnp.bfloat16, jnp.float32
    group_size = lax.axis_size(GROUP)
    seq_size = lax.axis_size(SEQ)
    shards = lax.axis_size(TENSOR)
    member_index = lax.axis_index(GROUP)
    seq_index = lax.axis_index(SEQ)
    shard = lax.axis_index(TENSOR)
    trees, rows, model_width = tokens.shape
    part_width = project.shape[2]
    owned = project.shape[1]
    hidden = spreader.shape[2]
    slots = CAP // shards
    quarter = rows // shards
    place_arg = seq_index.astype(jnp.int32).reshape(1)

    extra = EXPERTS + 2
    pad = -extra % 128
    small = jnp.concatenate(
        [
            project[0],
            project[1],
            project[2],
            mixing.T,
            router,
            norm_gains.T,
            jnp.zeros((owned, pad), bf16),
        ],
        1,
    )
    small = lax.all_gather(small, GROUP, axis=0, tiled=True)
    project_all = small[:, : 3 * part_width]
    mixing_own = small[:, 3 * part_width : 4 * part_width].T
    router_all = small[:, 4 * part_width : 4 * part_width + EXPERTS]
    gains = small[:, 4 * part_width + EXPERTS : 4 * part_width + extra].T.astype(f32)
    mixing_all = share(mixing_own, TENSOR, shards, 0)
    labels = jnp.arange(EXPERTS, dtype=jnp.int32)
    named = jnp.any(routes[:, None, :, :] == labels[None, :, None, None], 3)
    earlier = (
        jnp.arange(rows, dtype=jnp.int32)[:, None] < jnp.arange(rows, dtype=jnp.int32)[None, :]
    )
    ranks = jnp.einsum(
        "bes,st->bet", named.astype(bf16), earlier.astype(bf16), preferred_element_type=f32
    ).astype(jnp.int32)
    slot_index = shard * slots + jnp.arange(slots, dtype=jnp.int32)
    chosen = (
        (named[:, :, None, :] & (ranks[:, :, None, :] == slot_index[None, None, :, None]))
        .astype(bf16)
        .reshape(trees, EXPERTS * slots, rows)
    )

    def pick_rows(field):
        picked = jnp.einsum("bst,btd->bsd", chosen, field, preferred_element_type=f32).astype(bf16)
        return picked.reshape(trees, EXPERTS, slots, field.shape[-1]).swapaxes(0, 1)

    def send_rows(picked):
        return route(picked).reshape(EXPERTS * trees * slots, picked.shape[-1])

    def bring_rows(field):
        back = route(field.reshape(EXPERTS, trees, slots, field.shape[-1])).swapaxes(0, 1)
        return back.reshape(trees, EXPERTS * slots, field.shape[-1])

    def combine_rows(chosen, back):
        return by_rows(jnp.einsum("bst,bsd->btd", chosen, back, preferred_element_type=f32))

    place, paths, key_bits = tree_tables(segments, parents)
    offset = seq_index * rows
    own_place = lax.dynamic_slice_in_dim(place, offset, rows, 1).astype(f32)
    own_paths = lax.dynamic_slice_in_dim(paths, offset, rows, 1)
    half = HEAD_DIM // 2
    rates = jnp.exp(-math.log(theta) * 2.0 * jnp.arange(half, dtype=f32) / HEAD_DIM)
    angle = rates[None, :, None] * own_place[:, None, :]
    cosine = jnp.cos(angle)[:, None]
    sine = jnp.sin(angle)[:, None]
    inputs = tokens.astype(f32)
    scale_one = lax.rsqrt(jnp.mean(inputs * inputs, -1, keepdims=True) + epsilon)
    first_in = (inputs * scale_one * gains[0]).astype(bf16)
    mapped = jnp.einsum("dh,btd->bht", project_all, first_in, preferred_element_type=f32)
    queries = (
        turned(mapped[:, :part_width], cosine, sine, False) * HEAD_DIM ** (-0.5)
    ).astype(bf16)
    pairs_own = jnp.concatenate(
        [
            turned(mapped[:, part_width : 2 * part_width], cosine, sine, False).astype(bf16),
            mapped[:, 2 * part_width :].astype(bf16),
        ],
        1,
    )
    key_column = key_bits[:, :, None]
    path_row = own_paths[:, None, :]
    pairs = [pairs_own]
    links = [pairs_own[tree : tree + 1] for tree in range(trees)]
    shared_bundle = jnp.concatenate([spreader, collector.T[None]], 0)
    state = ()
    for number in range(seq_size):
        if number + 1 < seq_size:
            links = [
                lax.ppermute(link, SEQ, [(i, i + 1) for i in range(seq_size - 1)])
                for link in links
            ]
        else:
            picked_cotangent, pairs[-1] = tied(pick_rows(cotangent), pairs[-1])
        state = attend(
            number,
            number == seq_size - 1,
            place_arg,
            queries,
            key_column,
            path_row,
            pairs[number],
            state,
        )
        if number + 1 < seq_size:
            *links, first_state = tied(*links, state[0])
            state = (first_state,) + tuple(state[1:])
            pairs.append(jnp.concatenate(links, 0))
    outs, logs = state[:2]

    bundles = jnp.concatenate([expander, reducer.transpose(0, 2, 1)[:, None]], 1)
    own_expert = route(bundles).swapaxes(0, 1).reshape(3, model_width, hidden)
    expert_weights = lax.all_gather(own_expert, TENSOR, axis=0, tiled=False)
    outs, expert_weights = tied(outs, expert_weights)
    heads = share(outs, TENSOR, shards, 1)
    upstream_rows = send_rows(picked_cotangent)
    heads, upstream_rows = tied(heads, upstream_rows)
    second = inputs + by_rows(
        jnp.einsum("bht,hd->btd", heads, mixing_all, preferred_element_type=f32)
    )

    scale_two = lax.rsqrt(jnp.mean(second * second, -1, keepdims=True) + epsilon)
    hidden_in = (second * scale_two * gains[1]).astype(bf16)
    flat = (trees * rows, model_width)
    flat_hidden = hidden_in.reshape(flat)
    flat_cotangent = cotangent.reshape(flat)
    expert_rows = send_rows(pick_rows(hidden_in))
    expert_rows, shared_bundle = tied(expert_rows, shared_bundle)
    shared_weights = lax.all_gather(
        shared_bundle, GROUP, axis=1, tiled=True
    )
    row_chances = jax.nn.softmax(jnp.dot(expert_rows, router_all, preferred_element_type=f32), -1)
    own_label = jnp.arange(EXPERTS, dtype=jnp.int32) == member_index
    row_gates = jnp.sum(jnp.where(own_label[None], row_chances, 0.0), -1, keepdims=True)
    row_grads = (row_gates * upstream_rows.astype(f32)).astype(bf16)
    lowered, routed_back, expert_wide = gated(expert_rows, row_grads, expert_weights, TILE)
    gate_grads = jnp.sum(upstream_rows.astype(f32) * lowered, -1, keepdims=True)
    lanes = jnp.arange(128, dtype=jnp.int32)[None]
    back_rows = jnp.concatenate(
        [
            routed_back.astype(bf16),
            jnp.where(lanes == member_index, gate_grads, 0.0).astype(bf16),
        ],
        1,
    )
    flat_hidden, row_grads, back_rows = tied(flat_hidden, row_grads, back_rows)
    shared_out, shared_back, shared_wide = gated(
        flat_hidden, flat_cotangent, shared_weights[None], TILE
    )
    expert_parts = weight_parts(
        expert_rows, row_grads, expert_wide, shards, group_size, TILE
    )
    back_rows = bring_rows(back_rows)
    chosen, shared_back = tied(chosen, shared_back)
    returned_back = combine_rows(chosen, back_rows)
    out_rows = (row_gates * lowered).astype(bf16)
    shared_parts = weight_parts(
        flat_hidden, flat_cotangent, shared_wide, 1, group_size, TILE
    )

    def own_rows(field):
        return lax.dynamic_slice_in_dim(field, shard * quarter, quarter, 1)

    def add_shards(field):
        held = field.astype(bf16).reshape(trees, shards, quarter, field.shape[-1])
        step = 1
        while step < shards:
            paired = held.reshape(trees, -1, 2, quarter, field.shape[-1])
            bit = (shard // step) % 2
            kept = lax.dynamic_index_in_dim(paired, bit, 2, keepdims=False)
            sent = lax.dynamic_index_in_dim(paired, 1 - bit, 2, keepdims=False)
            added = kept.astype(f32) + swap(sent, TENSOR, shards, step).astype(f32)
            step *= 2
            held = added.astype(bf16) if step < shards else added
        return held[:, 0]

    def spread_shards(field):
        pieces = share(field[None], TENSOR, shards, 0)
        return jnp.concatenate(
            [pick(pieces, reversed_bits(shard ^ other, shards)) for other in range(shards)], 1
        )

    summed = add_shards(
        returned_back
        + jnp.pad(shared_back.reshape(trees, rows, model_width), ((0, 0), (0, 0), (0, 128)))
    )
    summed, shared_parts, out_rows = tied(summed, shared_parts, out_rows)
    chance_grad = summed[..., model_width : model_width + EXPERTS]
    quarter_second = own_rows(second)
    quarter_scale = own_rows(scale_two)
    quarter_normed = quarter_second * quarter_scale
    quarter_hidden = own_rows(hidden_in)
    logits = jnp.dot(quarter_hidden, router_all, preferred_element_type=f32)
    chances = jax.nn.softmax(logits, -1)
    logit_grad = chances * (chance_grad - jnp.sum(chances * chance_grad, -1, keepdims=True))
    hidden_grad = summed[..., :model_width] + jnp.einsum(
        "bte,de->btd", logit_grad, router_all.astype(f32), precision=highest
    )
    router_part = jnp.einsum(
        "btd,bte->de", quarter_hidden.astype(f32), logit_grad, precision=highest
    )
    gain_two = jnp.sum(hidden_grad * quarter_normed, (0, 1))
    scaled_two = hidden_grad * gains[1]
    second_grad = own_rows(cotangent).astype(f32) + quarter_scale * (
        scaled_two - quarter_normed * jnp.mean(scaled_two * quarter_normed, -1, keepdims=True)
    )
    branch_grad = spread_shards(second_grad.astype(bf16))
    returned_out = combine_rows(chosen, bring_rows(out_rows))
    partial_out = (returned_out + shared_out.reshape(trees, rows, model_width)).astype(bf16)

    heads_grad = jnp.einsum(
        "hd,btd->bht", mixing_own, branch_grad, preferred_element_type=f32
    ).astype(bf16)
    mixing_part = jnp.einsum("btd,bht->dh", branch_grad, outs, preferred_element_type=f32)
    def block_back(number, query_grad):
        return attend_back(
            number,
            bf16 if number == seq_size - 1 else f32,
            place_arg,
            (queries, outs, heads_grad, logs, key_column, path_row, pairs[number]) + query_grad,
        )

    query_grad, pair_grad = block_back(seq_size - 1, ())
    shared_grads = lax.psum_scatter(
        shared_parts[0], GROUP, scatter_dimension=0, tiled=True
    )[0].astype(f32)
    moving = [pair_grad[tree] for tree in range(trees)]
    for step in range(seq_size - 1):
        query_grad, pair_grad = block_back(seq_size - 2 - step, (query_grad,))
        moved = [
            lax.ppermute(grads.astype(bf16), SEQ, [(i + 1, i) for i in range(seq_size - 1)])
            for grads in moving
        ]
        if step == 0:
            *moved, expert_parts = tied(*moved, expert_parts)
            expert_own = lax.psum_scatter(expert_parts, TENSOR, scatter_dimension=0, tiled=False)
        moving = [pair_grad[tree] + moved[tree].astype(f32) for tree in range(trees)]
        if step < seq_size - 2:
            query_grad, *moving = tied(query_grad, *moving)
    own_grads = moving
    pair_grad, shared_grads, partial_out = tied(jnp.stack(own_grads), shared_grads, partial_out)
    output = spread_shards((quarter_second + add_shards(partial_out)).astype(bf16))
    spreader_grad = shared_grads[:2]
    collector_grad = shared_grads[2].T
    query_grad = query_grad * HEAD_DIM ** (-0.5)
    mapped_grad = jnp.concatenate(
        [
            turned(query_grad, cosine, sine, True),
            turned(pair_grad[:, :part_width], cosine, sine, True),
            pair_grad[:, part_width:],
        ],
        1,
    ).astype(bf16)
    first_part = by_rows(
        jnp.einsum("bht,dh->btd", mapped_grad, project_all, preferred_element_type=f32)
    ).astype(bf16)
    first_grad = add_shards(first_part)
    project_part = by_rows(
        jnp.einsum("btd,bht->dh", first_in, mapped_grad, preferred_element_type=f32)
    )
    quarter_scale_one = own_rows(scale_one)
    quarter_normed_one = own_rows(inputs) * quarter_scale_one
    scaled_one = first_grad * gains[0]
    input_grad = spread_shards(
        (
            second_grad
            + quarter_scale_one
            * (
                scaled_one
                - quarter_normed_one * jnp.mean(scaled_one * quarter_normed_one, -1, keepdims=True)
            )
        ).astype(bf16)
    )


    early_width = part_width + EXPERTS + 1
    early_width += -early_width % 128
    early_parts = jnp.concatenate(
        [
            mixing_part,
            router_part,
            gain_two[:, None],
            jnp.zeros((model_width, early_width - part_width - EXPERTS - 1), f32),
        ],
        1,
    ).astype(bf16)
    small_parts = jnp.concatenate([early_parts, project_part.astype(bf16)], 1)
    small_home = route(small_parts.reshape(group_size, owned, -1))
    small_home, expert_own = tied(small_home, expert_own)
    expert_grads = route(expert_own).astype(f32)
    expander_grad = expert_grads[:, :2]
    reducer_grad = expert_grads[:, 2].transpose(0, 2, 1)
    small_grads = jnp.sum(
        small_home.astype(f32),
        0,
    )
    project_grad = (
        small_grads[:, early_width:].reshape(owned, 3, part_width).transpose(1, 0, 2)
    )
    mixing_grad = small_grads[:, :part_width].T
    rest = small_grads[:, part_width : part_width + EXPERTS + 1]
    gain_one = jnp.sum(project_grad * project.astype(f32), (0, 2)) / norm_gains[0].astype(f32)
    tiny = lax.psum(
        jnp.concatenate([rest.T, gain_one[None]], 0),
        TENSOR,
    )
    tiny, input_grad = tied(tiny, input_grad)
    router_grad = tiny[:EXPERTS].T
    gain_grad = jnp.stack([tiny[EXPERTS + 1], tiny[EXPERTS]])
    return (
        output,
        input_grad,
        gain_grad,
        project_grad,
        mixing_grad,
        router_grad,
        expander_grad,
        reducer_grad,
        spreader_grad,
        collector_grad,
    )


def solution(mesh):
    in_specs = (
        P(DP, SEQ, None),
        P(DP, SEQ, None),
        P(DP, None),
        P(DP, None),
        P(DP, SEQ, None),
        P(None, GROUP),
        P(None, GROUP, TENSOR),
        P(TENSOR, GROUP),
        P(GROUP, None),
        P(None, None, GROUP, TENSOR),
        P(None, TENSOR, GROUP),
        P(None, GROUP, TENSOR),
        P(TENSOR, GROUP),
    )
    out_specs = (
        P(DP, SEQ, None),
        P(DP, SEQ, None),
        P(None, GROUP),
        P(None, GROUP, TENSOR),
        P(TENSOR, GROUP),
        P(GROUP, None),
        P(None, None, GROUP, TENSOR),
        P(None, TENSOR, GROUP),
        P(None, GROUP, TENSOR),
        P(TENSOR, GROUP),
    )
    sizes = mesh.shape
    group_size = sizes[DP] * sizes[SEQ]
    shards = sizes[TENSOR]
    fits = group_size == EXPERTS and shards & (shards - 1) == 0 and CAP % shards == 0
    body = local_fast if fits else local
    return jax.shard_map(body, mesh=mesh, in_specs=in_specs, out_specs=out_specs, check_vma=False)
```
